32 devices in a mesh: chan: 2 (over x), srow: 4 (over y, core), scol: 4 (over z).
Axes of the slice: x: 2, y: 2, z: 4, core: 2. Of those that a mesh axis runs over, the one named last changes fastest.
Arguments:
- vis: bfloat16 [2, 2, 512, 512], P('chan', None, 'srow', 'scol'), may hold values from -4 to 4
- model: bfloat16 [2, 64, 2, 512, 512], P('chan', None, None, 'srow', 'scol'), may hold values from -1 to 1, as said below
- flags: int32 [2, 32, 32], P('chan', 'srow', 'scol'), may hold values 0 or 1
- gains: float32 [2, 64, 2, 512], P('chan', None, None, ('srow', 'scol')), may hold values from -3 to 3
- consensus: float32 [64, 1, 2, 512], P(None, None, None, ('srow', 'scol')), may hold values from -3 to 3
- dual: float32 [2, 64, 2, 512], P('chan', None, None, ('srow', 'scol')), may hold values from -2 to 2
- rho: float32 [8], replicated, may hold values from 0.5 to 8
- cluster: int32 [64], replicated, may hold values from 0 to 7
Outputs:
- gains_out: float32 [2, 64, 2, 512], P('chan', None, None, ('srow', 'scol'))
- consensus_out: float32 [64, 1, 2, 512], P(None, None, None, ('srow', 'scol'))
- dual_out: float32 [2, 64, 2, 512], P('chan', None, None, ('srow', 'scol'))
The draws below stay inside these ranges and needn't reach their ends.
Inputs may be any that keep to these rules, and one draw needn't show every extreme that they name: `model`: entries of about 1 / sqrt(512) in size.
All inputs are finite; a program needn't handle non-finite values. No bound on the sum of `flags` on one device may be relied on, other than what follows from the above.
Results may differ from the reference program's by a relative error of at most 0.0003.
Values sent between devices are 32-bit elements; how exact they have to be, the bound alone decides.
No kernel may reach another device: no remote copies, remote signals or barrier semaphores. Data moves between devices by JAX's collectives and lax.ppermute only.
A program may use at most 64 MiB of HBM per device.

```python
import math
import jax
import jax.numpy as jnp
from jax import lax

STATIONS = 512
DIRS = 64
CLUSTERS = 8
TILE = 16
ITERS = 4
GROUPS = 2
BASIS = 1
N_SROW = 4
N_SCOL = 4


def column_map():
    span = STATIONS // (N_SROW * N_SCOL)
    col_block = STATIONS // N_SCOL
    row_block = STATIONS // N_SROW
    index = jnp.arange(STATIONS, dtype=jnp.int32)
    return index % col_block // span * row_block + index // col_block * span + index % span


def group_levels(peak):
    return peak ** (0.5 * jnp.arange(GROUPS, dtype=jnp.float32) / max(GROUPS - 1, 1))


def station_scales(key):
    owners = N_SROW * N_SCOL
    scale_key = jax.random.fold_in(key, 707)
    powers = jax.random.uniform(scale_key, (owners,), jnp.float32, -1.5, 0.5)
    return jnp.repeat(10.0 ** powers, STATIONS // owners)


def model_group(key, group):
    group_key = jax.random.fold_in(jax.random.fold_in(key, 101), group)
    shape = (DIRS, 2, STATIONS, STATIONS)
    base = jnp.clip(jax.random.normal(group_key, shape, jnp.float32), -4.0, 4.0)
    return (base * STATIONS ** (-0.5)).astype(jnp.bfloat16)


def gain_draw(key):
    gain_key = jax.random.fold_in(key, 202)
    shape = (GROUPS, DIRS, 2, STATIONS)
    values = jnp.clip(0.7 * jax.random.normal(gain_key, shape, jnp.float32), -3.0, 3.0)
    return values


def draw_model(key, part):
    return lax.map(lambda group: model_group(key, group), jnp.arange(GROUPS, dtype=jnp.int32))


def draw_gains(key, part):
    return gain_draw(key)


def draw_vis(key, part):
    current = gain_draw(key)
    peak = 3.0
    levels = group_levels(peak)
    shift_key = jax.random.fold_in(key, 303)
    per_station = station_scales(key)
    shift = 0.3 * jax.random.normal(shift_key, current.shape, jnp.float32) * levels[:, None, None, None]
    shift = shift * per_station[None, None, None, :]
    true_gains = current + shift
    columns = column_map()

    def predict(items):
        group, g_true = items
        model_block = model_group(key, group).astype(jnp.float32)
        m_real = model_block[:, 0]
        m_imag = model_block[:, 1]
        g_col = g_true[:, :, columns]
        c_real = g_col[:, 0][:, None, :]
        c_imag = g_col[:, 1][:, None, :]
        z_real = m_real * c_real + m_imag * c_imag
        z_imag = m_imag * c_real - m_real * c_imag
        r_real = g_true[:, 0][:, :, None]
        r_imag = g_true[:, 1][:, :, None]
        pred_real = jnp.sum(r_real * z_real - r_imag * z_imag, axis=0)
        pred_imag = jnp.sum(r_real * z_imag + r_imag * z_real, axis=0)
        return jnp.stack([pred_real, pred_imag])
    predicted = lax.map(predict, (jnp.arange(GROUPS, dtype=jnp.int32), true_gains))
    noise_key = jax.random.fold_in(key, 404)
    noise_part = jax.random.normal(noise_key, (GROUPS, 2, STATIONS, STATIONS), jnp.float32)
    noise_part = 0.1 * (DIRS / STATIONS) ** 0.5 * noise_part * levels[:, None, None, None]
    return jnp.clip(predicted + noise_part, -4.0, 4.0).astype(jnp.bfloat16)


def place_ends(array, rng, least, high):
    place = [jax.random.randint(jax.random.fold_in(rng, axis), (), 0, length) for axis, length in enumerate(array.shape)]
    main_axis = array.shape.index(max(array.shape))
    neighbour = place[:main_axis] + [(place[main_axis] + 1) % array.shape[main_axis]] + place[main_axis + 1:]
    return array.at[tuple(place)].set(least).at[tuple(neighbour)].set(high)


def shard_levels(rng, extent, shards, smallest, largest):
    factor_of, own = 1.0, jax.random.fold_in(rng, 6)
    for position, shards_of in shards:
        steps = jnp.exp(jax.random.uniform(jax.random.fold_in(own, position), (shards_of,), jnp.float32, smallest / len(shards), largest / len(shards)))
        factor_of = factor_of * jnp.repeat(steps, extent[position] // shards_of).reshape([-1 if axis == position else 1 for axis in range(len(extent))])
    return factor_of


def centred(rng, dims, spread, limit, pieces=(), kind=jnp.bfloat16):
    result = spread * jax.random.normal(rng, dims, jnp.float32)
    if pieces:
        result = result * shard_levels(rng, dims, pieces, -0.22, 0.18)
    return jnp.clip(result, -limit, limit).astype(kind)


def setup_inputs(seed: int = 0) -> dict:
    streams_of = jax.random.split(jax.random.key(seed), 9)
    return {
        "vis": draw_vis(jax.random.fold_in(streams_of[8], 71), 0),
        "model": draw_model(jax.random.fold_in(streams_of[8], 71), 0),
        "flags": place_ends((jax.random.randint(streams_of[2], (GROUPS, STATIONS // TILE, STATIONS // TILE), 0, 8) < 7).astype(jnp.int32), jax.random.fold_in(streams_of[2], 1), 0, 1),
        "gains": draw_gains(jax.random.fold_in(streams_of[8], 71), 0),
        "consensus": centred(streams_of[4], (DIRS, BASIS, 2, STATIONS), 0.5, 3.0, ((3, 16),), jnp.float32),
        "dual": centred(streams_of[5], (GROUPS, DIRS, 2, STATIONS), 0.3, 2.0, ((0, 2), (3, 16)), jnp.float32),
        "rho": jnp.clip(jnp.exp(jax.random.uniform(streams_of[6], (CLUSTERS,), jnp.float32, math.log(0.5), math.log(8.0))), 0.5, 8.0),
        "cluster": place_ends(jax.random.randint(streams_of[7], (DIRS,), 0, CLUSTERS), jax.random.fold_in(streams_of[7], 1), 0, CLUSTERS - 1).astype(jnp.int32),
    }


EPS = 1e-05
STEP = 0.5

def basis_table(groups, order):
    xval = (jnp.arange(groups, dtype=jnp.float32) + 0.5) / groups
    columns = [math.comb(order - 1, b) * xval ** b * (1.0 - xval) ** (order - 1 - b) for b in range(order)]
    return jnp.stack(columns, axis=1)

def column_stations(stations, rows_grid, cols_grid):
    span = stations // (rows_grid * cols_grid)
    col_block = stations // cols_grid
    row_block = stations // rows_grid
    index = jnp.arange(stations, dtype=jnp.int32)
    return index % col_block // span * row_block + index // col_block * span + index % span

def local_terms(vis_block, model_block, weight, g_row, g_col):
    m_real = model_block[:, 0].astype(jnp.float32)
    m_imag = model_block[:, 1].astype(jnp.float32)
    c_real = g_col[:, 0][:, None, :]
    c_imag = g_col[:, 1][:, None, :]
    z_real = m_real * c_real + m_imag * c_imag
    z_imag = m_imag * c_real - m_real * c_imag
    r_real = g_row[:, 0][:, :, None]
    r_imag = g_row[:, 1][:, :, None]
    pred_real = jnp.sum(r_real * z_real - r_imag * z_imag, axis=0)
    pred_imag = jnp.sum(r_real * z_imag + r_imag * z_real, axis=0)
    res_real = vis_block[0].astype(jnp.float32) - pred_real
    res_imag = vis_block[1].astype(jnp.float32) - pred_imag
    w_real = weight * res_real
    w_imag = weight * res_imag
    power = jnp.sum(w_real * res_real + w_imag * res_imag)
    a_term = jnp.sum(weight[None] * (z_real * z_real + z_imag * z_imag), axis=-1)
    cross_real = jnp.sum(z_real * w_real[None] + z_imag * w_imag[None], axis=-1)
    cross_imag = jnp.sum(z_real * w_imag[None] - z_imag * w_real[None], axis=-1)
    return (power, a_term, jnp.stack([cross_real, cross_imag], axis=-2))

def solve(cross, a_term, g_now, target, rho_eff):
    denom = a_term + rho_eff[:, None]
    fresh = (cross + a_term[..., None, :] * g_now + rho_eff[:, None, None] * target) / denom[..., None, :]
    return g_now + STEP * (fresh - g_now)

def gram_solve(table, rhs):
    gram = jnp.dot(table.T, table, precision=lax.Precision.HIGHEST)
    factor = jnp.linalg.cholesky(gram)
    order = rhs.shape[1]
    flat = jnp.moveaxis(rhs, 1, 0).reshape(order, -1)
    sol = jax.scipy.linalg.cho_solve((factor, True), flat)
    return jnp.moveaxis(sol.reshape((order, rhs.shape[0]) + rhs.shape[2:]), 0, 1)

def reference(vis, model, flags, gains, consensus, dual, rho, cluster):
    table = basis_table(GROUPS, BASIS)
    columns = column_stations(STATIONS, N_SROW, N_SCOL)
    rho_dir = rho[cluster]
    fl = flags.astype(jnp.float32)
    weights = jnp.repeat(jnp.repeat(fl, TILE, axis=1), TILE, axis=2)
    target = jnp.einsum('fb,kbcp->fkcp', table, consensus, precision=lax.Precision.HIGHEST) - dual
    g = gains

    def one_group(items):
        vis_block, model_block, weight, g_group = items
        return local_terms(vis_block, model_block, weight, g_group, g_group[:, :, columns])
    for step in range(ITERS):
        power, a_term, cross = lax.map(one_group, (vis, model, weights, g))
        rho_eff = rho_dir * (jnp.sum(power) / (GROUPS * STATIONS * STATIONS) + EPS)
        g = solve(cross, a_term, g, target, rho_eff)
    sums = jnp.einsum('fb,fkcp->kbcp', table, g + dual, precision=lax.Precision.HIGHEST)
    coeffs = gram_solve(table, sums)
    dual_out = dual + g - jnp.einsum('fb,kbcp->fkcp', table, coeffs, precision=lax.Precision.HIGHEST)
    return (g, coeffs, dual_out)
```

```python
import functools
import math

import jax
import jax.numpy as jnp
from jax import lax
from jax.experimental import pallas as pl
from jax.experimental.pallas import tpu as pltpu
from jax.sharding import PartitionSpec as P

STATIONS = 512
TILE = 16
ITERS = 4

EPS = 1e-05
STEP = 0.5

VMEM_LIMIT = 40 << 20


def basis_table(groups, order):
    xval = (jnp.arange(groups, dtype=jnp.float32) + 0.5) / groups
    columns = [
        math.comb(order - 1, b) * xval**b * (1.0 - xval) ** (order - 1 - b) for b in range(order)
    ]
    return jnp.stack(columns, axis=1)


def gram_solve(table, rhs):
    gram = jnp.dot(table.T, table, precision=lax.Precision.HIGHEST)
    factor = jnp.linalg.cholesky(gram)
    order = rhs.shape[1]
    flat = jnp.moveaxis(rhs, 1, 0).reshape(order, -1)
    sol = jax.scipy.linalg.cho_solve((factor, True), flat)
    return jnp.moveaxis(sol.reshape((order, rhs.shape[0]) + rhs.shape[2:]), 0, 1)


def lane_block(shape, span):
    return lax.broadcasted_iota(jnp.int32, shape, 1) // span


def pack_plane(plane, block, span):
    dirs, lanes = plane.shape
    parts = lanes // span
    rows = dirs // parts
    where = lane_block((rows, lanes), span)
    packed = None
    for q in range(parts):
        piece = plane[q * rows : (q + 1) * rows]
        shift = lax.rem((q - block) * span + lanes, lanes)
        piece = pltpu.roll(piece, shift, 1)
        packed = piece if packed is None else jnp.where(where == q, piece, packed)
    return packed


def unpack_planes(pieces, blocks, span):
    rows, lanes = pieces[0].shape
    parts = lanes // span
    where = lane_block((rows, lanes), span)
    out = []
    for q in range(parts):
        plane = None
        for piece, block in zip(pieces, blocks):
            shift = lax.rem((block - q) * span + lanes, lanes)
            moved = pltpu.roll(piece, shift, 1)
            plane = moved if plane is None else jnp.where(where == block, moved, plane)
        out.append(plane)
    return jnp.concatenate(out, axis=0)


def solve(a, cr, ci, gr, gi, tr, ti, rho_eff):
    denom = a + rho_eff
    fresh_r = (cr + a * gr + rho_eff * tr) / denom
    fresh_i = (ci + a * gi + rho_eff * ti) / denom
    return gr + STEP * (fresh_r - gr), gi + STEP * (fresh_i - gi)


def prepare_kernel(model_ref, vis_ref, weight_ref, mt_ref, vt_ref):
    weight = weight_ref[...]
    for k in range(model_ref.shape[0]):
        for p in range(2):
            block = model_ref[k, p].astype(jnp.float32)
            mt_ref[k, p] = (block.T * weight).astype(jnp.bfloat16)

    @pl.when(pl.program_id(0) == 0)
    def _():
        for p in range(2):
            vt_ref[p] = vis_ref[p].astype(jnp.float32).T * weight


def prepare(model, vis, weight_t):
    dirs, _, rows, cols = model.shape
    step = 8
    return pl.pallas_call(
        prepare_kernel,
        grid=(dirs // step,),
        in_specs=[
            pl.BlockSpec((step, 2, rows, cols), lambda n: (n, 0, 0, 0)),
            pl.BlockSpec((2, rows, cols), lambda n: (0, 0, 0)),
            pl.BlockSpec((cols, rows), lambda n: (0, 0)),
        ],
        out_specs=[
            pl.BlockSpec((step, 2, cols, rows), lambda n: (n, 0, 0, 0)),
            pl.BlockSpec((2, cols, rows), lambda n: (0, 0, 0)),
        ],
        out_shape=[
            jax.ShapeDtypeStruct((dirs, 2, cols, rows), jnp.bfloat16),
            jax.ShapeDtypeStruct((2, cols, rows), jnp.float32),
        ],
        name="prepare",
    )(model, vis, weight_t)


def local_terms(mt_ref, vt_ref, grow_ref, gcol_ref, out_ref, z_ref, r_ref, ct_ref):
    dirs, _, cols, rows = mt_ref.shape
    ct_ref[...] = gcol_ref[...].T
    chunk = 16

    def predict(n, carry):
        c0 = pl.multiple_of(n * chunk, chunk)
        here = pl.ds(c0, chunk)
        ctile = ct_ref[here, :]
        acc_r = vt_ref[0, here, :]
        acc_i = vt_ref[1, here, :]
        for k in range(dirs):
            mr = mt_ref[k, 0, here, :].astype(jnp.float32)
            mi = mt_ref[k, 1, here, :].astype(jnp.float32)
            cr = jnp.broadcast_to(ctile[:, k : k + 1], (chunk, rows))
            ci = jnp.broadcast_to(ctile[:, dirs + k : dirs + k + 1], (chunk, rows))
            zr = mr * cr + mi * ci
            zi = mi * cr - mr * ci
            z_ref[k, 0, here, :] = zr
            z_ref[k, 1, here, :] = zi
            gr = grow_ref[k : k + 1, :]
            gi = grow_ref[dirs + k : dirs + k + 1, :]
            acc_r = acc_r - (gr * zr - gi * zi)
            acc_i = acc_i - (gr * zi + gi * zr)
        r_ref[0, here, :] = acc_r
        r_ref[1, here, :] = acc_i
        sq = acc_r * acc_r + acc_i * acc_i
        return carry + sq[:8] + sq[8:]

    power = lax.fori_loop(0, cols // chunk, predict, jnp.zeros((8, rows), jnp.float32))
    out_ref[3 * dirs : 3 * dirs + 8, :] = power

    group = 8

    def terms(n, carry):
        k0 = pl.multiple_of(n * group, group)
        for half in range(2):
            sums = [[None] * 3 for _ in range(group // 2)]
            for c in range(0, cols, 8):
                rr = r_ref[0, c : c + 8, :]
                ri = r_ref[1, c : c + 8, :]
                for kk in range(group // 2):
                    k = k0 + half * (group // 2) + kk
                    zr = z_ref[k, 0, c : c + 8, :]
                    zi = z_ref[k, 1, c : c + 8, :]
                    new = (zr * zr + zi * zi, zr * rr + zi * ri, zr * ri - zi * rr)
                    for s in range(3):
                        old = sums[kk][s]
                        sums[kk][s] = new[s] if old is None else old + new[s]
            for s in range(3):
                block = jnp.concatenate(
                    [jnp.sum(sums[kk][s], axis=0, keepdims=True) for kk in range(group // 2)], axis=0
                )
                out_ref[pl.ds(s * dirs + k0 + half * (group // 2), group // 2), :] = block
        return carry

    lax.fori_loop(0, dirs // group, terms, 0)


def first_kernel(ids_ref, *refs, ns, nz, span):
    rows_in = refs[:nz]
    cols_in = refs[nz : nz + ns]
    mt_ref, vt_ref = refs[nz + ns : nz + ns + 2]
    out_ref, grow_ref, gcol_ref, trow_ref, tcol_ref = refs[nz + ns + 2 : nz + ns + 7]
    scratch = refs[nz + ns + 7 :]
    dirs = mt_ref.shape[0]
    i, j = ids_ref[0], ids_ref[1]
    depth = dirs * span // mt_ref.shape[3]
    for pieces, g_ref, t_ref, me in ((rows_in, grow_ref, trow_ref, j), (cols_in, gcol_ref, tcol_ref, i)):
        blocks = [jnp.bitwise_xor(me, n) for n in range(len(pieces))]
        for q in range(4):
            plane = unpack_planes([p[q * depth : (q + 1) * depth, :] for p in pieces], blocks, span)
            dst = g_ref if q < 2 else t_ref
            at = (q % 2) * dirs
            dst[at : at + dirs, :] = plane
    local_terms(mt_ref, vt_ref, grow_ref, gcol_ref, out_ref, *scratch)


def sweep_kernel(ids_ref, *refs, ns, span, scale):
    pieces = refs[:ns]
    sum_ref, growin_ref, gcolin_ref, trow_ref, tcol_ref, rho_ref, mt_ref, vt_ref = refs[ns : ns + 8]
    out_ref, grow_ref, gcol_ref = refs[ns + 8 : ns + 11]
    scratch = refs[ns + 11 :]
    dirs = mt_ref.shape[0]
    i = ids_ref[0]
    depth = dirs * span // mt_ref.shape[3]
    power = pieces[0][3 * depth :, :]
    for p in pieces[1:]:
        power = power + p[3 * depth :, :]
    rho_eff = rho_ref[...] * (jnp.sum(power) * scale + EPS)
    re, im = slice(0, dirs), slice(dirs, 2 * dirs)
    grow_ref[re, :], grow_ref[im, :] = solve(
        sum_ref[0:dirs, :],
        sum_ref[dirs : 2 * dirs, :],
        sum_ref[2 * dirs : 3 * dirs, :],
        growin_ref[re, :],
        growin_ref[im, :],
        trow_ref[re, :],
        trow_ref[im, :],
        rho_eff,
    )
    blocks = [jnp.bitwise_xor(i, n) for n in range(ns)]
    a, cr, ci = [
        unpack_planes([p[q * depth : (q + 1) * depth, :] for p in pieces], blocks, span)
        for q in range(3)
    ]
    gcol_ref[re, :], gcol_ref[im, :] = solve(
        a, cr, ci, gcolin_ref[re, :], gcolin_ref[im, :], tcol_ref[re, :], tcol_ref[im, :], rho_eff
    )
    local_terms(mt_ref, vt_ref, grow_ref, gcol_ref, out_ref, *scratch)


def combine_kernel(ids_ref, *refs, nz, extra, span):
    parts = refs[:nz]
    powers = refs[nz : nz + extra]
    sum_ref, own_ref = refs[nz + extra :]
    dirs = sum_ref.shape[0] // 3
    j = ids_ref[1]
    depth = dirs * span // sum_ref.shape[1]
    for q in range(3):
        at = slice(q * dirs, (q + 1) * dirs)
        total = parts[0][at, :]
        for p in parts[1:]:
            total = total + p[at, :]
        sum_ref[at, :] = total
        own_ref[q * depth : (q + 1) * depth, :] = pack_plane(total, j, span)
    power = parts[0][3 * dirs :, :]
    for p in parts[1:]:
        power = power + p[3 * dirs :, :]
    for p in powers:
        power = power + p[...]
    own_ref[3 * depth :, :] = power


def final_kernel(*refs, ns, scale):
    pieces = refs[:ns]
    g_ref, t_ref, rho_ref, out_ref = refs[ns:]
    depth = rho_ref.shape[0]
    power = pieces[0][3 * depth :, :]
    for p in pieces[1:]:
        power = power + p[3 * depth :, :]
    rho_eff = rho_ref[...] * (jnp.sum(power) * scale + EPS)
    own = pieces[0]
    out_ref[0:depth, :], out_ref[depth : 2 * depth, :] = solve(
        own[0:depth, :],
        own[depth : 2 * depth, :],
        own[2 * depth : 3 * depth, :],
        g_ref[0:depth, :],
        g_ref[depth : 2 * depth, :],
        t_ref[0:depth, :],
        t_ref[depth : 2 * depth, :],
        rho_eff,
    )


SMEM = pl.BlockSpec(memory_space=pltpu.SMEM)
VMEM = pl.BlockSpec(memory_space=pltpu.VMEM)


def f32(*shape):
    return jax.ShapeDtypeStruct(shape, jnp.float32)


def call(kernel, name, ids, args, outs, scratch=()):
    lead = [] if ids is None else [ids]
    return pl.pallas_call(
        kernel,
        in_specs=[SMEM] * len(lead) + [VMEM] * len(args),
        out_specs=[VMEM] * len(outs),
        out_shape=outs,
        scratch_shapes=scratch,
        compiler_params=pltpu.CompilerParams(vmem_limit_bytes=VMEM_LIMIT),
        name=name,
    )(*lead, *args)


def swap(x, axis, n):
    size = lax.axis_size(axis)
    return lax.ppermute(x, axis, [(m, m ^ n) for m in range(size)])


def to_packed(x, lanes):
    dirs, _, span = x.shape
    parts = lanes // span
    x = x.reshape(parts, dirs // parts, 2, span)
    return x.transpose(2, 1, 0, 3).reshape(2 * dirs // parts, lanes)


def from_packed(x, span):
    rows, lanes = x.shape
    parts = lanes // span
    x = x.reshape(2, rows // 2, parts, span)
    return x.transpose(2, 1, 0, 3).reshape(parts * rows // 2, 2, span)


def shards(vis, model, flags, gains, consensus, dual, rho, cluster):
    groups = lax.axis_size("chan")
    ns = lax.axis_size("srow")
    nz = lax.axis_size("scol")
    order = consensus.shape[1]
    dirs = gains.shape[1]
    span = gains.shape[3]
    rows, cols = vis.shape[2:]
    i, j, f = lax.axis_index("srow"), lax.axis_index("scol"), lax.axis_index("chan")
    ids = jnp.stack([i, j]).astype(jnp.int32)

    table = basis_table(groups, order)
    brow = lax.dynamic_index_in_dim(table, f, 0, keepdims=False)
    dual_own = dual[0]
    target = jnp.einsum("b,kbcp->kcp", brow, consensus, precision=lax.Precision.HIGHEST) - dual_own
    start = jnp.concatenate([to_packed(gains[0], rows), to_packed(target, rows)], axis=0)

    row_parts = [start] + [swap(start, "scol", n) for n in range(1, nz)]
    col_parts = [start] + [swap(start, "srow", n) for n in range(1, ns)]

    matches = cluster[:, None] == jnp.arange(rho.shape[0], dtype=jnp.int32)[None, :]
    rho_dir = jnp.sum(jnp.where(matches, rho[None, :], 0.0), axis=1)
    rho_rows = jnp.broadcast_to(rho_dir[:, None], (dirs, rows))
    parts = rows // span
    rho_packed = jnp.repeat(rho_dir.reshape(parts, dirs // parts).T, span, axis=1)
    fl = flags[0].astype(jnp.float32).T
    weight_t = jnp.repeat(jnp.repeat(fl, TILE, axis=0), TILE, axis=1)
    mt, vt = prepare(model[0], vis[0], weight_t)

    scratch = [
        pltpu.VMEM((dirs, 2, cols, rows), jnp.float32),
        pltpu.VMEM((2, cols, rows), jnp.float32),
        pltpu.VMEM((cols, 2 * dirs), jnp.float32),
    ]
    scale = 1.0 / (groups * STATIONS * STATIONS)
    depth = dirs * span // rows
    plane = f32(2 * dirs, rows)
    partial, grow, gcol, trow, tcol = call(
        functools.partial(first_kernel, ns=ns, nz=nz, span=span),
        "first",
        ids,
        row_parts + col_parts + [mt, vt],
        [f32(3 * dirs + 8, rows), plane, plane, plane, plane],
        scratch,
    )
    g_packed, t_packed = start[: 2 * depth], start[2 * depth :]
    for step in range(ITERS):
        swaps = [partial] + [swap(partial, "scol", n) for n in range(1, nz)]
        power = partial[3 * dirs :]
        if groups == 2:
            both = ("chan", "scol")
            powers = [swap(power, both, nz + n) for n in range(nz)]
        else:
            powers = [lax.psum(power, ("chan", "scol")) - sum(s[3 * dirs :] for s in swaps)]
        sums, own = call(
            functools.partial(combine_kernel, nz=nz, extra=len(powers), span=span),
            "combine",
            ids,
            swaps + powers,
            [f32(3 * dirs, rows), f32(3 * depth + 8, rows)],
        )
        pieces = [own] + [swap(own, "srow", n) for n in range(1, ns)]
        if step < ITERS - 1:
            partial, grow_new, gcol_new = call(
                functools.partial(sweep_kernel, ns=ns, span=span, scale=scale),
                "sweep",
                ids,
                pieces + [sums, grow, gcol, trow, tcol, rho_rows, mt, vt],
                [f32(3 * dirs + 8, rows), plane, plane],
                scratch,
            )
            grow, gcol = grow_new, gcol_new
        own_g = call(
            functools.partial(final_kernel, ns=ns, scale=scale),
            "own",
            None,
            pieces + [g_packed, t_packed, rho_packed],
            [f32(2 * depth, rows)],
        )[0]
        g_packed = own_g
    g = from_packed(g_packed, span)
    local = brow[None, :, None, None] * (g + dual_own)[:, None, :, :]
    if groups == 2:
        sums = local + swap(local, "chan", 1)
    else:
        sums = lax.psum(local, "chan")
    coeffs = gram_solve(table, sums)
    dual_new = (
        dual_own + g - jnp.einsum("b,kbcp->kcp", brow, coeffs, precision=lax.Precision.HIGHEST)
    )
    return (g[None], coeffs, dual_new[None])


def solution(mesh):
    placed = (
        P("chan", None, "srow", "scol"),
        P("chan", None, None, "srow", "scol"),
        P("chan", "srow", "scol"),
        P("chan", None, None, ("srow", "scol")),
        P(None, None, None, ("srow", "scol")),
        P("chan", None, None, ("srow", "scol")),
        P(),
        P(),
    )
    return jax.shard_map(
        shards,
        mesh=mesh,
        in_specs=placed,
        out_specs=(
            P("chan", None, None, ("srow", "scol")),
            P(None, None, None, ("srow", "scol")),
            P("chan", None, None, ("srow", "scol")),
        ),
        check_vma=False,
    )
```

```python
import functools
import math

import jax
import jax.numpy as jnp
from jax import lax
from jax.experimental import pallas as pl
from jax.experimental.pallas import tpu as pltpu
from jax.sharding import PartitionSpec as P

STATIONS = 512
TILE = 16
ITERS = 4

EPS = 1e-05
STEP = 0.5

VMEM_LIMIT = 24 << 20


def basis_table(groups, order):
    xval = (jnp.arange(groups, dtype=jnp.float32) + 0.5) / groups
    columns = [
        math.comb(order - 1, b) * xval**b * (1.0 - xval) ** (order - 1 - b) for b in range(order)
    ]
    return jnp.stack(columns, axis=1)


def gram_solve(table, rhs):
    gram = jnp.dot(table.T, table, precision=lax.Precision.HIGHEST)
    factor = jnp.linalg.cholesky(gram)
    order = rhs.shape[1]
    flat = jnp.moveaxis(rhs, 1, 0).reshape(order, -1)
    sol = jax.scipy.linalg.cho_solve((factor, True), flat)
    return jnp.moveaxis(sol.reshape((order, rhs.shape[0]) + rhs.shape[2:]), 0, 1)


def lane_block(shape, span):
    return lax.broadcasted_iota(jnp.int32, shape, 1) // span


def pack_plane(plane, block, span):
    dirs, lanes = plane.shape
    parts = lanes // span
    rows = dirs // parts
    where = lane_block((rows, lanes), span)
    packed = None
    for q in range(parts):
        piece = plane[q * rows : (q + 1) * rows]
        shift = lax.rem((q - block) * span + lanes, lanes)
        piece = pltpu.roll(piece, shift, 1)
        packed = piece if packed is None else jnp.where(where == q, piece, packed)
    return packed


def unpack_planes(pieces, blocks, span):
    rows, lanes = pieces[0].shape
    parts = lanes // span
    where = lane_block((rows, lanes), span)
    out = []
    for q in range(parts):
        plane = None
        for piece, block in zip(pieces, blocks):
            shift = lax.rem((block - q) * span + lanes, lanes)
            moved = pltpu.roll(piece, shift, 1)
            plane = moved if plane is None else jnp.where(where == block, moved, plane)
        out.append(plane)
    return jnp.concatenate(out, axis=0)


def solve(a, cr, ci, gr, gi, tr, ti, rho_eff):
    denom = a + rho_eff
    fresh_r = (cr + a * gr + rho_eff * tr) / denom
    fresh_i = (ci + a * gi + rho_eff * ti) / denom
    return gr + STEP * (fresh_r - gr), gi + STEP * (fresh_i - gi)


def prepare_kernel(model_ref, vis_ref, weight_ref, mt_ref, vt_ref):
    weight = weight_ref[...]
    for k in range(model_ref.shape[0]):
        for p in range(2):
            block = model_ref[k, p].astype(jnp.float32)
            mt_ref[k, p] = (block.T * weight).astype(jnp.bfloat16)

    @pl.when(pl.program_id(0) == 0)
    def _():
        for p in range(2):
            vt_ref[p] = vis_ref[p].astype(jnp.float32).T * weight


def prepare(model, vis, weight_t):
    dirs, _, rows, cols = model.shape
    step = 8
    return pl.pallas_call(
        prepare_kernel,
        grid=(dirs // step,),
        in_specs=[
            pl.BlockSpec((step, 2, rows, cols), lambda n: (n, 0, 0, 0)),
            pl.BlockSpec((2, rows, cols), lambda n: (0, 0, 0)),
            pl.BlockSpec((cols, rows), lambda n: (0, 0)),
        ],
        out_specs=[
            pl.BlockSpec((step, 2, cols, rows), lambda n: (n, 0, 0, 0)),
            pl.BlockSpec((2, cols, rows), lambda n: (0, 0, 0)),
        ],
        out_shape=[
            jax.ShapeDtypeStruct((dirs, 2, cols, rows), jnp.bfloat16),
            jax.ShapeDtypeStruct((2, cols, rows), jnp.float32),
        ],
        name="prepare",
    )(model, vis, weight_t)


def residual(mt_ref, vt_ref, grow_ref, gcol_ref, z_ref, r_ref, p_ref, ct_ref):
    dirs, _, cols, rows = mt_ref.shape
    ct_ref[...] = gcol_ref[...].T
    chunk = 64

    def predict(n, carry):
        here = pl.ds(pl.multiple_of(n * chunk, chunk), chunk)
        ctile = ct_ref[here, :]
        acc_r = vt_ref[0, here, :]
        acc_i = vt_ref[1, here, :]
        for k in range(dirs):
            mr = mt_ref[k, 0, here, :].astype(jnp.float32)
            mi = mt_ref[k, 1, here, :].astype(jnp.float32)
            cr = jnp.broadcast_to(ctile[:, k : k + 1], (chunk, rows))
            ci = jnp.broadcast_to(ctile[:, dirs + k : dirs + k + 1], (chunk, rows))
            zr = mr * cr + mi * ci
            zi = mi * cr - mr * ci
            z_ref[k, 0, here, :] = zr
            z_ref[k, 1, here, :] = zi
            gr = grow_ref[k : k + 1, :]
            gi = grow_ref[dirs + k : dirs + k + 1, :]
            acc_r = acc_r - (gr * zr - gi * zi)
            acc_i = acc_i - (gr * zi + gi * zr)
        r_ref[0, here, :] = acc_r
        r_ref[1, here, :] = acc_i
        sq = acc_r * acc_r + acc_i * acc_i
        for c in range(0, chunk, 8):
            carry = carry + sq[c : c + 8]
        return carry

    p_ref[...] = lax.fori_loop(0, cols // chunk, predict, jnp.zeros(p_ref.shape, jnp.float32))


def terms_kernel(z_ref, r_ref, out_ref):
    dirs, _, cols, rows = z_ref.shape
    group = 8
    part = 4

    def terms(n, carry):
        k0 = pl.multiple_of(n * group, group)
        blocks = [[], [], []]
        for half in range(0, group, part):
            sums = [[None] * 3 for _ in range(part)]
            for c in range(0, cols, 8):
                rr = r_ref[0, c : c + 8, :]
                ri = r_ref[1, c : c + 8, :]
                for kk in range(part):
                    zr = z_ref[k0 + half + kk, 0, c : c + 8, :]
                    zi = z_ref[k0 + half + kk, 1, c : c + 8, :]
                    new = (zr * zr + zi * zi, zr * rr + zi * ri, zr * ri - zi * rr)
                    for s in range(3):
                        old = sums[kk][s]
                        sums[kk][s] = new[s] if old is None else old + new[s]
            for s in range(3):
                blocks[s] += [jnp.sum(sums[kk][s], axis=0, keepdims=True) for kk in range(part)]
        for s in range(3):
            out_ref[pl.ds(s * dirs + k0, group), :] = jnp.concatenate(blocks[s], axis=0)
        return carry

    lax.fori_loop(0, dirs // group, terms, 0)
    out_ref[3 * dirs :, :] = jnp.zeros((8, rows), jnp.float32)


def first_kernel(ids_ref, *refs, ns, nz, span):
    rows_in = refs[:nz]
    cols_in = refs[nz : nz + ns]
    mt_ref, vt_ref = refs[nz + ns : nz + ns + 2]
    outs = refs[nz + ns + 2 : nz + ns + 5]
    grow_ref, gcol_ref, trow_ref, tcol_ref, ct_ref = refs[nz + ns + 5 :]
    dirs = mt_ref.shape[0]
    i, j = ids_ref[0], ids_ref[1]
    depth = dirs * span // mt_ref.shape[3]
    for pieces, g_ref, t_ref, me in ((rows_in, grow_ref, trow_ref, j), (cols_in, gcol_ref, tcol_ref, i)):
        blocks = [jnp.bitwise_xor(me, n) for n in range(len(pieces))]
        for q in range(4):
            plane = unpack_planes([p[q * depth : (q + 1) * depth, :] for p in pieces], blocks, span)
            dst = g_ref if q < 2 else t_ref
            at = (q % 2) * dirs
            dst[at : at + dirs, :] = plane
    residual(mt_ref, vt_ref, grow_ref, gcol_ref, *outs, ct_ref)


def sweep_kernel(ids_ref, *refs, ns, span, scale):
    pieces = refs[:ns]
    sum_ref, growin_ref, gcolin_ref, trow_ref, tcol_ref, rho_ref, mt_ref, vt_ref = refs[ns : ns + 8]
    outs = refs[ns + 8 : ns + 11]
    grow_ref, gcol_ref, ct_ref = refs[ns + 11 :]
    dirs = mt_ref.shape[0]
    i = ids_ref[0]
    depth = dirs * span // mt_ref.shape[3]
    power = pieces[0][3 * depth :, :]
    for p in pieces[1:]:
        power = power + p[3 * depth :, :]
    rho_eff = rho_ref[...] * (jnp.sum(power) * scale + EPS)
    re, im = slice(0, dirs), slice(dirs, 2 * dirs)
    grow_ref[re, :], grow_ref[im, :] = solve(
        sum_ref[0:dirs, :],
        sum_ref[dirs : 2 * dirs, :],
        sum_ref[2 * dirs : 3 * dirs, :],
        growin_ref[re, :],
        growin_ref[im, :],
        trow_ref[re, :],
        trow_ref[im, :],
        rho_eff,
    )
    blocks = [jnp.bitwise_xor(i, n) for n in range(ns)]
    a, cr, ci = [
        unpack_planes([p[q * depth : (q + 1) * depth, :] for p in pieces], blocks, span)
        for q in range(3)
    ]
    gcol_ref[re, :], gcol_ref[im, :] = solve(
        a, cr, ci, gcolin_ref[re, :], gcolin_ref[im, :], tcol_ref[re, :], tcol_ref[im, :], rho_eff
    )
    residual(mt_ref, vt_ref, grow_ref, gcol_ref, *outs, ct_ref)


def combine_kernel(ids_ref, *refs, nz, span):
    parts = refs[:nz]
    sum_ref, own_ref = refs[nz:]
    dirs = sum_ref.shape[0] // 3
    j = ids_ref[1]
    depth = dirs * span // sum_ref.shape[1]
    for q in range(3):
        at = slice(q * dirs, (q + 1) * dirs)
        total = parts[0][at, :]
        for p in parts[1:]:
            total = total + p[at, :]
        sum_ref[at, :] = total
        own_ref[q * depth : (q + 1) * depth, :] = pack_plane(total, j, span)
    power = parts[0][3 * dirs :, :]
    for p in parts[1:]:
        power = power + p[3 * dirs :, :]
    own_ref[3 * depth :, :] = power


def final_kernel(*refs, ns, scale):
    pieces = refs[:ns]
    g_ref, t_ref, rho_ref, out_ref = refs[ns:]
    depth = rho_ref.shape[0]
    power = pieces[0][3 * depth :, :]
    for p in pieces[1:]:
        power = power + p[3 * depth :, :]
    rho_eff = rho_ref[...] * (jnp.sum(power) * scale + EPS)
    own = pieces[0]
    out_ref[0:depth, :], out_ref[depth : 2 * depth, :] = solve(
        own[0:depth, :],
        own[depth : 2 * depth, :],
        own[2 * depth : 3 * depth, :],
        g_ref[0:depth, :],
        g_ref[depth : 2 * depth, :],
        t_ref[0:depth, :],
        t_ref[depth : 2 * depth, :],
        rho_eff,
    )


SMEM = pl.BlockSpec(memory_space=pltpu.SMEM)
VMEM = pl.BlockSpec(memory_space=pltpu.VMEM)


def f32(*shape):
    return jax.ShapeDtypeStruct(shape, jnp.float32)


def call(kernel, name, ids, args, outs, scratch=()):
    lead = [] if ids is None else [ids]
    return pl.pallas_call(
        kernel,
        in_specs=[SMEM] * len(lead) + [VMEM] * len(args),
        out_specs=[VMEM] * len(outs),
        out_shape=outs,
        scratch_shapes=scratch,
        compiler_params=pltpu.CompilerParams(vmem_limit_bytes=VMEM_LIMIT),
        name=name,
    )(*lead, *args)


def swap(x, axis, n):
    size = lax.axis_size(axis)
    return lax.ppermute(x, axis, [(m, m ^ n) for m in range(size)])


def to_packed(x, lanes):
    dirs, _, span = x.shape
    parts = lanes // span
    x = x.reshape(parts, dirs // parts, 2, span)
    return x.transpose(2, 1, 0, 3).reshape(2 * dirs // parts, lanes)


def from_packed(x, span):
    rows, lanes = x.shape
    parts = lanes // span
    x = x.reshape(2, rows // 2, parts, span)
    return x.transpose(2, 1, 0, 3).reshape(parts * rows // 2, 2, span)


def shards(vis, model, flags, gains, consensus, dual, rho, cluster):
    groups = lax.axis_size("chan")
    ns = lax.axis_size("srow")
    nz = lax.axis_size("scol")
    order = consensus.shape[1]
    dirs = gains.shape[1]
    span = gains.shape[3]
    rows, cols = vis.shape[2:]
    i, j, f = lax.axis_index("srow"), lax.axis_index("scol"), lax.axis_index("chan")
    ids = jnp.stack([i, j]).astype(jnp.int32)

    table = basis_table(groups, order)
    brow = lax.dynamic_index_in_dim(table, f, 0, keepdims=False)
    dual_own = dual[0]
    target = jnp.einsum("b,kbcp->kcp", brow, consensus, precision=lax.Precision.HIGHEST) - dual_own
    start = jnp.concatenate([to_packed(gains[0], rows), to_packed(target, rows)], axis=0)

    row_parts = [start] + [swap(start, "scol", n) for n in range(1, nz)]
    col_parts = [start] + [swap(start, "srow", n) for n in range(1, ns)]

    matches = cluster[:, None] == jnp.arange(rho.shape[0], dtype=jnp.int32)[None, :]
    rho_dir = jnp.sum(jnp.where(matches, rho[None, :], 0.0), axis=1)
    rho_rows = jnp.broadcast_to(rho_dir[:, None], (dirs, rows))
    parts = rows // span
    rho_packed = jnp.repeat(rho_dir.reshape(parts, dirs // parts).T, span, axis=1)
    fl = flags[0].astype(jnp.float32).T
    weight_t = jnp.repeat(jnp.repeat(fl, TILE, axis=0), TILE, axis=1)
    mt, vt = prepare(model[0], vis[0], weight_t)

    scratch = [pltpu.VMEM((cols, 2 * dirs), jnp.float32)]
    scale = 1.0 / (groups * STATIONS * STATIONS)
    depth = dirs * span // rows
    plane = f32(2 * dirs, rows)
    fields = [f32(dirs, 2, cols, rows), f32(2, cols, rows), f32(8, rows)]
    z, r, power, grow, gcol, trow, tcol = call(
        functools.partial(first_kernel, ns=ns, nz=nz, span=span),
        "first",
        ids,
        row_parts + col_parts + [mt, vt],
        fields + [plane, plane, plane, plane],
        scratch,
    )
    g_packed, t_packed = start[: 2 * depth], start[2 * depth :]
    for step in range(ITERS):
        if groups == 2:
            power = power + swap(power, ("chan", "srow"), ns + 1)
        else:
            power = lax.psum(power, "chan")
        partial = call(terms_kernel, "terms", None, [z, r], [f32(3 * dirs + 8, rows)])[0]
        partial = lax.dynamic_update_slice(partial, power, (3 * dirs, 0))
        sums, own = call(
            functools.partial(combine_kernel, nz=nz, span=span),
            "combine",
            ids,
            [partial] + [swap(partial, "scol", n) for n in range(nz - 1, 0, -1)],
            [f32(3 * dirs, rows), f32(3 * depth + 8, rows)],
        )
        pieces = [own] + [swap(own, "srow", n) for n in range(1, ns)]
        if step < ITERS - 1:
            z, r, power, grow_new, gcol_new = call(
                functools.partial(sweep_kernel, ns=ns, span=span, scale=scale),
                "sweep",
                ids,
                pieces + [sums, grow, gcol, trow, tcol, rho_rows, mt, vt],
                fields + [plane, plane],
                scratch,
            )
            grow, gcol = grow_new, gcol_new
        g_packed = call(
            functools.partial(final_kernel, ns=ns, scale=scale),
            "own",
            None,
            pieces + [g_packed, t_packed, rho_packed],
            [f32(2 * depth, rows)],
        )[0]
    g = from_packed(g_packed, span)
    local = brow[None, :, None, None] * (g + dual_own)[:, None, :, :]
    if groups == 2:
        sums = local + swap(local, "chan", 1)
    else:
        sums = lax.psum(local, "chan")
    coeffs = gram_solve(table, sums)
    dual_new = (
        dual_own + g - jnp.einsum("b,kbcp->kcp", brow, coeffs, precision=lax.Precision.HIGHEST)
    )
    return (g[None], coeffs, dual_new[None])


def solution(mesh):
    placed = (
        P("chan", None, "srow", "scol"),
        P("chan", None, None, "srow", "scol"),
        P("chan", "srow", "scol"),
        P("chan", None, None, ("srow", "scol")),
        P(None, None, None, ("srow", "scol")),
        P("chan", None, None, ("srow", "scol")),
        P(),
        P(),
    )
    return jax.shard_map(
        shards,
        mesh=mesh,
        in_specs=placed,
        out_specs=(
            P("chan", None, None, ("srow", "scol")),
            P(None, None, None, ("srow", "scol")),
            P("chan", None, None, ("srow", "scol")),
        ),
        check_vma=False,
    )
```

```python
import functools
import math

import jax
import jax.numpy as jnp
from jax import lax
from jax.experimental import pallas as pl
from jax.experimental.pallas import tpu as pltpu
from jax.sharding import PartitionSpec as P

STATIONS = 512
TILE = 16
ITERS = 4

EPS = 1e-05
STEP = 0.5

VMEM_LIMIT = 24 << 20


def basis_table(groups, order):
    xval = (jnp.arange(groups, dtype=jnp.float32) + 0.5) / groups
    columns = [
        math.comb(order - 1, b) * xval**b * (1.0 - xval) ** (order - 1 - b) for b in range(order)
    ]
    return jnp.stack(columns, axis=1)


def gram_solve(table, rhs):
    gram = jnp.dot(table.T, table, precision=lax.Precision.HIGHEST)
    factor = jnp.linalg.cholesky(gram)
    order = rhs.shape[1]
    flat = jnp.moveaxis(rhs, 1, 0).reshape(order, -1)
    sol = jax.scipy.linalg.cho_solve((factor, True), flat)
    return jnp.moveaxis(sol.reshape((order, rhs.shape[0]) + rhs.shape[2:]), 0, 1)


def lane_block(shape, span):
    return lax.broadcasted_iota(jnp.int32, shape, 1) // span


def pack_plane(plane, block, span):
    dirs, lanes = plane.shape
    parts = lanes // span
    rows = dirs // parts
    where = lane_block((rows, lanes), span)
    packed = None
    for q in range(parts):
        piece = plane[q * rows : (q + 1) * rows]
        shift = lax.rem((q - block) * span + lanes, lanes)
        piece = pltpu.roll(piece, shift, 1)
        packed = piece if packed is None else jnp.where(where == q, piece, packed)
    return packed


def unpack_planes(pieces, blocks, span):
    rows, lanes = pieces[0].shape
    parts = lanes // span
    where = lane_block((rows, lanes), span)
    out = []
    for q in range(parts):
        plane = None
        for piece, block in zip(pieces, blocks):
            shift = lax.rem((block - q) * span + lanes, lanes)
            moved = pltpu.roll(piece, shift, 1)
            plane = moved if plane is None else jnp.where(where == block, moved, plane)
        out.append(plane)
    return jnp.concatenate(out, axis=0)


def solve(a, cr, ci, gr, gi, tr, ti, rho_eff):
    denom = a + rho_eff
    fresh_r = (cr + a * gr + rho_eff * tr) / denom
    fresh_i = (ci + a * gi + rho_eff * ti) / denom
    return gr + STEP * (fresh_r - gr), gi + STEP * (fresh_i - gi)


def pack_kernel(brow_ref, gains_ref, consensus_ref, dual_ref, start_ref, dual_out_ref):
    span, dirs = gains_ref.shape[1:]
    lanes = start_ref.shape[1]
    depth = dirs * span // lanes
    rows = []
    for p in range(2):
        target = brow_ref[0] * consensus_ref[0, p]
        for b in range(1, consensus_ref.shape[0]):
            target = target + brow_ref[b] * consensus_ref[b, p]
        rows.append(target - dual_ref[p])
    for fields, out_ref in (
        ([gains_ref[0], gains_ref[1]] + rows, start_ref),
        ([dual_ref[0], dual_ref[1]], dual_out_ref),
    ):
        plane = to_plane(fields, lanes)[:dirs]
        for n in range(len(fields)):
            out_ref[n * depth : (n + 1) * depth, :] = pack_plane(plane, n, span)


def to_plane(fields, lanes):
    x = jnp.concatenate(fields, axis=0)
    if x.shape[0] < lanes:
        x = jnp.concatenate([x, jnp.zeros((lanes - x.shape[0], x.shape[1]), x.dtype)], axis=0)
    if x.shape[1] < lanes:
        x = jnp.concatenate([x, jnp.zeros((lanes, lanes - x.shape[1]), x.dtype)], axis=1)
    return x.T


def prepare_kernel(rho_ref, cluster_ref, flags_ref, model_ref, vis_ref, *outs):
    mt_ref, vt_ref, rho_rows_ref, rho_packed_ref = outs
    dirs, _, rows, cols = model_ref.shape
    where = lax.broadcasted_iota(jnp.int32, (1, rows), 1) // TILE
    bands = []
    for b in range(cols // TILE):
        band = jnp.zeros((1, rows), jnp.float32)
        for r in range(rows // TILE):
            band = jnp.where(where == r, flags_ref[r, b].astype(jnp.float32), band)
        bands.append(jnp.broadcast_to(band, (TILE, rows)))
    weight = jnp.concatenate(bands, axis=0)
    weight_bf16 = weight.astype(jnp.bfloat16)
    for p in range(2):
        vt_ref[p] = vis_ref[p].astype(jnp.float32).T * weight
    for k in range(dirs):
        rho_rows_ref[k : k + 1, :] = jnp.full((1, rows), rho_ref[cluster_ref[k]], jnp.float32)
    rho_packed_ref[...] = pack_plane(rho_rows_ref[...], 0, rows * rho_packed_ref.shape[0] // dirs)

    def turn(n, carry):
        for k in range(4):
            for p in range(2):
                mt_ref[4 * n + k, p] = model_ref[4 * n + k, p].T * weight_bf16
        return carry

    lax.fori_loop(0, dirs // 4, turn, 0)


def residual(mt_ref, vt_ref, grow_ref, gcol_ref, z_ref, r_ref, p_ref, ct_ref):
    dirs, _, cols, rows = mt_ref.shape
    ct_ref[...] = gcol_ref[...].T
    chunk = 64

    def predict(n, carry):
        here = pl.ds(pl.multiple_of(n * chunk, chunk), chunk)
        ctile = ct_ref[here, :]
        acc_r = vt_ref[0, here, :]
        acc_i = vt_ref[1, here, :]
        for k in range(dirs):
            mr = mt_ref[k, 0, here, :].astype(jnp.float32)
            mi = mt_ref[k, 1, here, :].astype(jnp.float32)
            cr = jnp.broadcast_to(ctile[:, k : k + 1], (chunk, rows))
            ci = jnp.broadcast_to(ctile[:, dirs + k : dirs + k + 1], (chunk, rows))
            zr = mr * cr + mi * ci
            zi = mi * cr - mr * ci
            z_ref[k, 0, here, :] = zr
            z_ref[k, 1, here, :] = zi
            gr = grow_ref[k : k + 1, :]
            gi = grow_ref[dirs + k : dirs + k + 1, :]
            acc_r = acc_r - (gr * zr - gi * zi)
            acc_i = acc_i - (gr * zi + gi * zr)
        r_ref[0, here, :] = acc_r
        r_ref[1, here, :] = acc_i
        sq = acc_r * acc_r + acc_i * acc_i
        for c in range(0, chunk, 8):
            carry = carry + sq[c : c + 8]
        return carry

    p_ref[...] = lax.fori_loop(0, cols // chunk, predict, jnp.zeros(p_ref.shape, jnp.float32))


def terms_kernel(z_ref, r_ref, out_ref):
    dirs, _, cols, rows = z_ref.shape
    group = 8
    part = 4

    def terms(n, carry):
        k0 = pl.multiple_of(n * group, group)
        blocks = [[], [], []]
        for half in range(0, group, part):
            sums = [[None] * 3 for _ in range(part)]
            for c in range(0, cols, 8):
                rr = r_ref[0, c : c + 8, :]
                ri = r_ref[1, c : c + 8, :]
                for kk in range(part):
                    zr = z_ref[k0 + half + kk, 0, c : c + 8, :]
                    zi = z_ref[k0 + half + kk, 1, c : c + 8, :]
                    new = (zr * zr + zi * zi, zr * rr + zi * ri, zr * ri - zi * rr)
                    for s in range(3):
                        old = sums[kk][s]
                        sums[kk][s] = new[s] if old is None else old + new[s]
            for s in range(3):
                blocks[s] += [jnp.sum(sums[kk][s], axis=0, keepdims=True) for kk in range(part)]
        for s in range(3):
            out_ref[pl.ds(s * dirs + k0, group), :] = jnp.concatenate(blocks[s], axis=0)
        return carry

    lax.fori_loop(0, dirs // group, terms, 0)
    out_ref[3 * dirs :, :] = jnp.zeros((8, rows), jnp.float32)


def last_terms_kernel(ids_ref, z_ref, r_ref, *refs, span):
    outs, all_ref = refs[:-1], refs[-1]
    dirs, _, cols, rows = z_ref.shape
    depth = dirs * span // rows
    terms_kernel(z_ref, r_ref, all_ref)
    for n, out_ref in enumerate(outs):
        block = jnp.bitwise_xor(ids_ref[1], n)
        for q in range(3):
            plane = all_ref[q * dirs : (q + 1) * dirs, :]
            out_ref[q * depth : (q + 1) * depth, :] = pack_plane(plane, block, span)
        out_ref[3 * depth :, :] = jnp.zeros((8, rows), jnp.float32)


def first_kernel(ids_ref, *refs, ns, nz, span):
    rows_in = refs[:nz]
    cols_in = refs[nz : nz + ns]
    mt_ref, vt_ref = refs[nz + ns : nz + ns + 2]
    outs = refs[nz + ns + 2 : nz + ns + 5]
    grow_ref, gcol_ref, trow_ref, tcol_ref, ct_ref = refs[nz + ns + 5 :]
    dirs = mt_ref.shape[0]
    i, j = ids_ref[0], ids_ref[1]
    depth = dirs * span // mt_ref.shape[3]
    for pieces, g_ref, t_ref, me in ((rows_in, grow_ref, trow_ref, j), (cols_in, gcol_ref, tcol_ref, i)):
        blocks = [jnp.bitwise_xor(me, n) for n in range(len(pieces))]
        for q in range(4):
            plane = unpack_planes([p[q * depth : (q + 1) * depth, :] for p in pieces], blocks, span)
            dst = g_ref if q < 2 else t_ref
            at = (q % 2) * dirs
            dst[at : at + dirs, :] = plane
    residual(mt_ref, vt_ref, grow_ref, gcol_ref, *outs, ct_ref)


def sweep_kernel(ids_ref, *refs, ns, span, scale):
    pieces = refs[:ns]
    sum_ref, growin_ref, gcolin_ref, trow_ref, tcol_ref, rho_ref, mt_ref, vt_ref = refs[ns : ns + 8]
    outs = refs[ns + 8 : ns + 11]
    grow_ref, gcol_ref, ct_ref = refs[ns + 11 :]
    dirs = mt_ref.shape[0]
    i = ids_ref[0]
    depth = dirs * span // mt_ref.shape[3]
    power = pieces[0][3 * depth :, :]
    for p in pieces[1:]:
        power = power + p[3 * depth :, :]
    rho_eff = rho_ref[...] * (jnp.sum(power) * scale + EPS)
    re, im = slice(0, dirs), slice(dirs, 2 * dirs)
    grow_ref[re, :], grow_ref[im, :] = solve(
        sum_ref[0:dirs, :],
        sum_ref[dirs : 2 * dirs, :],
        sum_ref[2 * dirs : 3 * dirs, :],
        growin_ref[re, :],
        growin_ref[im, :],
        trow_ref[re, :],
        trow_ref[im, :],
        rho_eff,
    )
    blocks = [jnp.bitwise_xor(i, n) for n in range(ns)]
    a, cr, ci = [
        unpack_planes([p[q * depth : (q + 1) * depth, :] for p in pieces], blocks, span)
        for q in range(3)
    ]
    gcol_ref[re, :], gcol_ref[im, :] = solve(
        a, cr, ci, gcolin_ref[re, :], gcolin_ref[im, :], tcol_ref[re, :], tcol_ref[im, :], rho_eff
    )
    residual(mt_ref, vt_ref, grow_ref, gcol_ref, *outs, ct_ref)


def combine_kernel(ids_ref, *refs, nz, span):
    parts = refs[:nz]
    sum_ref, own_ref = refs[nz:]
    dirs = sum_ref.shape[0] // 3
    j = ids_ref[1]
    depth = dirs * span // sum_ref.shape[1]
    for q in range(3):
        at = slice(q * dirs, (q + 1) * dirs)
        total = parts[0][at, :]
        for p in parts[1:]:
            total = total + p[at, :]
        sum_ref[at, :] = total
        own_ref[q * depth : (q + 1) * depth, :] = pack_plane(total, j, span)
    power = parts[0][3 * dirs :, :]
    for p in parts[1:]:
        power = power + p[3 * dirs :, :]
    own_ref[3 * depth :, :] = power


def last_combine_kernel(ids_ref, *refs, nz, span):
    parts = refs[:nz]
    g_ref, t_ref, d_ref, power_ref, mail_ref = refs[nz:]
    dirs = g_ref.shape[0] // 2
    depth = dirs * span // g_ref.shape[1]
    j = ids_ref[1]
    total = parts[0][...]
    for p in parts[1:]:
        total = total + p[...]
    mail_ref[: 3 * depth, :] = total[: 3 * depth]
    power_ref[...] = total[3 * depth :]
    for n, ref in enumerate((g_ref, t_ref)):
        for p in range(2):
            at = (3 + 2 * n + p) * depth
            plane = ref[p * dirs : (p + 1) * dirs, :]
            mail_ref[at : at + depth, :] = pack_plane(plane, j, span)
    mail_ref[7 * depth :, :] = d_ref[...]


def final_kernel(ids_ref, scal_ref, *refs, ns, scale, pair, span):
    powers = refs[:ns]
    mails = refs[ns : ns + 1 + pair]
    rho_ref = refs[ns + 1 + pair]
    outs = refs[ns + 2 + pair :]
    depth, lanes = rho_ref.shape
    dirs = depth * lanes // span
    power = powers[0][...]
    for p in powers[1:]:
        power = power + p[...]
    rho_eff = rho_ref[...] * (jnp.sum(power) * scale + EPS)
    news = []
    for mail in mails:
        a, cr, ci, gr, gi, tr, ti = [mail[q * depth : (q + 1) * depth, :] for q in range(7)]
        news.append(solve(a, cr, ci, gr, gi, tr, ti, rho_eff))
    fields = list(news[0])
    if pair:
        duals = [[m[q * depth : (q + 1) * depth, :] for q in (7, 8)] for m in mails]
        first = ids_ref[2] == 0
        coeffs, new_duals = [], []
        for p in range(2):
            own, other = [news[n][p] + duals[n][p] for n in range(2)]
            low, high = jnp.where(first, own, other), jnp.where(first, other, own)
            total = scal_ref[0] * low + scal_ref[1] * high
            coeffs.append(total / scal_ref[2] / scal_ref[2])
            brow = jnp.where(first, scal_ref[0], scal_ref[1])
            new_duals.append(duals[0][p] + news[0][p] - brow * coeffs[p])
        fields += coeffs + new_duals
    parts = lanes // span
    for at in range(0, len(fields), parts):
        group = fields[at : at + parts]
        plane = unpack_planes(group, list(range(len(group))), span)
        plane = jnp.concatenate([plane, jnp.zeros((lanes - dirs, lanes), jnp.float32)], axis=0)
        turned = plane.T
        for n in range(len(group)):
            out_ref = outs[(at + n) // 2]
            out_ref[(at + n) % 2] = turned[n * span : (n + 1) * span, :dirs]


SMEM = pl.BlockSpec(memory_space=pltpu.SMEM)
VMEM = pl.BlockSpec(memory_space=pltpu.VMEM)


def f32(*shape):
    return jax.ShapeDtypeStruct(shape, jnp.float32)


def call(kernel, name, lead, args, outs, scratch=()):
    return pl.pallas_call(
        kernel,
        in_specs=[SMEM] * len(lead) + [VMEM] * len(args),
        out_specs=[VMEM] * len(outs),
        out_shape=outs,
        scratch_shapes=scratch,
        compiler_params=pltpu.CompilerParams(vmem_limit_bytes=VMEM_LIMIT),
        name=name,
    )(*lead, *args)


def swap(x, axis, n):
    size = lax.axis_size(axis)
    return lax.ppermute(x, axis, [(m, m ^ n) for m in range(size)])


def shards(vis, model, flags, gains, consensus, dual, rho, cluster):
    groups = lax.axis_size("chan")
    ns = lax.axis_size("srow")
    nz = lax.axis_size("scol")
    order = consensus.shape[1]
    dirs = gains.shape[1]
    span = gains.shape[3]
    rows, cols = vis.shape[2:]
    depth = dirs * span // rows
    i, j, f = lax.axis_index("srow"), lax.axis_index("scol"), lax.axis_index("chan")
    ids = jnp.stack([i, j, f]).astype(jnp.int32)
    pair = groups == 2 and order == 1

    table = basis_table(groups, order)
    brow = lax.dynamic_index_in_dim(table, f, 0, keepdims=False)
    start, dual_packed = call(
        pack_kernel,
        "pack",
        [brow],
        [
            gains[0].transpose(1, 2, 0),
            consensus.transpose(1, 2, 3, 0),
            dual[0].transpose(1, 2, 0),
        ],
        [f32(4 * depth, rows), f32(2 * depth, rows)],
    )
    row_parts = [start] + [swap(start, "scol", n) for n in range(1, nz)]
    col_parts = [start] + [swap(start, "srow", n) for n in range(1, ns)]
    mt, vt, rho_rows, rho_packed = call(
        prepare_kernel,
        "prepare",
        [rho, cluster, flags[0]],
        [model[0], vis[0]],
        [
            jax.ShapeDtypeStruct((dirs, 2, cols, rows), jnp.bfloat16),
            f32(2, cols, rows),
            f32(dirs, rows),
            f32(depth, rows),
        ],
    )

    scratch = [pltpu.VMEM((cols, 2 * dirs), jnp.float32)]
    scale = 1.0 / (groups * STATIONS * STATIONS)
    plane = f32(2 * dirs, rows)
    fields = [f32(dirs, 2, cols, rows), f32(2, cols, rows), f32(8, rows)]
    z, r, power, grow, gcol, trow, tcol = call(
        functools.partial(first_kernel, ns=ns, nz=nz, span=span),
        "first",
        [ids],
        row_parts + col_parts + [mt, vt],
        fields + [plane, plane, plane, plane],
        scratch,
    )
    for step in range(ITERS):
        last = step == ITERS - 1
        if groups == 2:
            power = power + swap(power, ("chan", "srow"), ns + 1)
        else:
            power = lax.psum(power, "chan")
        if last:
            break
        partial = call(terms_kernel, "terms", [], [z, r], [f32(3 * dirs + 8, rows)])[0]
        partial = lax.dynamic_update_slice(partial, power, (3 * dirs, 0))
        order_z = sorted(range(1, nz), key=lambda n: (n > 2, -n))
        sums, own = call(
            functools.partial(combine_kernel, nz=nz, span=span),
            "combine",
            [ids],
            [partial] + [swap(partial, "scol", n) for n in order_z],
            [f32(3 * dirs, rows), f32(3 * depth + 8, rows)],
        )
        pieces = [own] + [swap(own, "srow", n) for n in range(1, ns)]
        z, r, power, grow, gcol = call(
            functools.partial(sweep_kernel, ns=ns, span=span, scale=scale),
            "sweep",
            [ids],
            pieces + [sums, grow, gcol, trow, tcol, rho_rows, mt, vt],
            fields + [plane, plane],
            scratch,
        )

    parts = call(
        functools.partial(last_terms_kernel, span=span),
        "terms",
        [ids],
        [z, r],
        [f32(3 * depth + 8, rows)] * nz,
        [pltpu.VMEM((3 * dirs + 8, rows), jnp.float32)],
    )
    parts = [lax.dynamic_update_slice(part, power, (3 * depth, 0)) for part in parts]
    power, mail = call(
        functools.partial(last_combine_kernel, nz=nz, span=span),
        "combine",
        [ids],
        [parts[0]] + [swap(parts[n], "scol", n) for n in range(1, nz)] + [grow, trow, dual_packed],
        [f32(8, rows), f32(9 * depth, rows)],
    )
    powers = [power] + [swap(power, "srow", n) for n in range(1, ns)]
    mails = [mail] + ([swap(mail, "chan", 1)] if pair else [])
    gram = jnp.dot(table.T, table, precision=lax.Precision.HIGHEST)
    factor = jnp.linalg.cholesky(gram)
    scal = jnp.concatenate([table[:, 0], factor[:1, 0]])
    outs = call(
        functools.partial(final_kernel, ns=ns, scale=scale, pair=int(pair), span=span),
        "final",
        [ids, scal],
        powers + mails + [rho_packed],
        [f32(2, span, dirs)] * (3 if pair else 1),
    )
    outs = [x.transpose(2, 0, 1) for x in outs]
    if pair:
        g, coeffs, dual_new = outs
        return (g[None], coeffs[:, None], dual_new[None])
    g = outs[0]
    dual_own = dual[0]
    local = brow[None, :, None, None] * (g + dual_own)[:, None, :, :]
    coeffs = gram_solve(table, lax.psum(local, "chan"))
    dual_new = (
        dual_own + g - jnp.einsum("b,kbcp->kcp", brow, coeffs, precision=lax.Precision.HIGHEST)
    )
    return (g[None], coeffs, dual_new[None])


def solution(mesh):
    placed = (
        P("chan", None, "srow", "scol"),
        P("chan", None, None, "srow", "scol"),
        P("chan", "srow", "scol"),
        P("chan", None, None, ("srow", "scol")),
        P(None, None, None, ("srow", "scol")),
        P("chan", None, None, ("srow", "scol")),
        P(),
        P(),
    )
    return jax.shard_map(
        shards,
        mesh=mesh,
        in_specs=placed,
        out_specs=(
            P("chan", None, None, ("srow", "scol")),
            P(None, None, None, ("srow", "scol")),
            P("chan", None, None, ("srow", "scol")),
        ),
        check_vma=False,
    )
```

```python
import functools
import math

import jax
import jax.numpy as jnp
import numpy as np
from jax import lax
from jax.experimental import pallas as pl
from jax.experimental.pallas import tpu as pltpu
from jax.sharding import PartitionSpec as P

STATIONS = 512
TILE = 16
ITERS = 4

EPS = 1e-05
STEP = 0.5

VMEM_LIMIT = 24 << 20


def basis_table(groups, order):
    xval = (jnp.arange(groups, dtype=jnp.float32) + 0.5) / groups
    columns = [
        math.comb(order - 1, b) * xval**b * (1.0 - xval) ** (order - 1 - b) for b in range(order)
    ]
    return jnp.stack(columns, axis=1)


def pair_scalars(pair):
    if not pair:
        return None
    xval = (np.arange(2, dtype=np.float32) + np.float32(0.5)) / np.float32(2)
    column = xval**0 * (np.float32(1.0) - xval) ** 0
    return float(column[0]), float(column[1]), float(np.sqrt(np.sum(column * column)))


def gram_solve(table, rhs):
    gram = jnp.dot(table.T, table, precision=lax.Precision.HIGHEST)
    factor = jnp.linalg.cholesky(gram)
    order = rhs.shape[1]
    flat = jnp.moveaxis(rhs, 1, 0).reshape(order, -1)
    sol = jax.scipy.linalg.cho_solve((factor, True), flat)
    return jnp.moveaxis(sol.reshape((order, rhs.shape[0]) + rhs.shape[2:]), 0, 1)


def lane_block(shape, span):
    return lax.broadcasted_iota(jnp.int32, shape, 1) // span


def pack_plane(plane, block, span):
    dirs, lanes = plane.shape
    parts = lanes // span
    rows = dirs // parts
    where = lane_block((rows, lanes), span)
    packed = None
    for q in range(parts):
        piece = plane[q * rows : (q + 1) * rows]
        shift = lax.rem((q - block) * span + lanes, lanes)
        piece = pltpu.roll(piece, shift, 1)
        packed = piece if packed is None else jnp.where(where == q, piece, packed)
    return packed


def unpack_planes(pieces, blocks, span):
    rows, lanes = pieces[0].shape
    parts = lanes // span
    where = lane_block((rows, lanes), span)
    out = []
    for q in range(parts):
        plane = None
        for piece, block in zip(pieces, blocks):
            shift = lax.rem((block - q) * span + lanes, lanes)
            moved = pltpu.roll(piece, shift, 1)
            plane = moved if plane is None else jnp.where(where == block, moved, plane)
        out.append(plane)
    return jnp.concatenate(out, axis=0)


def solve(a, cr, ci, gr, gi, tr, ti, rho_eff):
    denom = a + rho_eff
    fresh_r = (cr + a * gr + rho_eff * tr) / denom
    fresh_i = (ci + a * gi + rho_eff * ti) / denom
    return gr + STEP * (fresh_r - gr), gi + STEP * (fresh_i - gi)


def fetch(sources, targets, sems):
    copies = [
        pltpu.make_async_copy(src, dst, sems.at[n])
        for n, (src, dst) in enumerate(zip(sources, targets))
    ]
    for copy in copies:
        copy.start()
    return copies


def pack_kernel(brow_ref, *refs):
    start_ref, dual_out_ref = refs[3:5]
    gains_ref, consensus_ref, dual_ref = refs[5:8]
    for copy in fetch(refs[:3], refs[5:8], refs[8]):
        copy.wait()
    span, dirs = gains_ref.shape[1:]
    lanes = start_ref.shape[1]
    depth = dirs * span // lanes
    rows = []
    for p in range(2):
        target = brow_ref[0] * consensus_ref[0, p]
        for b in range(1, consensus_ref.shape[0]):
            target = target + brow_ref[b] * consensus_ref[b, p]
        rows.append(target - dual_ref[p])
    for fields, out_ref in (
        ([gains_ref[0], gains_ref[1]] + rows, start_ref),
        ([dual_ref[0], dual_ref[1]], dual_out_ref),
    ):
        plane = to_plane(fields, lanes)[:dirs]
        for n in range(len(fields)):
            out_ref[n * depth : (n + 1) * depth, :] = pack_plane(plane, n, span)


def to_plane(fields, lanes):
    x = jnp.concatenate(fields, axis=0)
    if x.shape[0] < lanes:
        x = jnp.concatenate([x, jnp.zeros((lanes - x.shape[0], x.shape[1]), x.dtype)], axis=0)
    if x.shape[1] < lanes:
        x = jnp.concatenate([x, jnp.zeros((lanes, lanes - x.shape[1]), x.dtype)], axis=1)
    return x.T


def prepare_kernel(*refs):
    ins = refs[:5]
    mt_ref, vt_ref, rho_rows_ref, rho_packed_ref = refs[5:9]
    rho_ref, cluster_ref, flags_ref, model_ref, vis_ref, sems = refs[9:]
    dirs, _, rows, cols = model_ref.shape
    pieces = 8
    size = dirs // pieces
    small = fetch(ins[:3] + ins[4:], [rho_ref, cluster_ref, flags_ref, vis_ref], sems)
    large = fetch(
        [ins[3].at[pl.ds(n * size, size)] for n in range(pieces)],
        [model_ref.at[pl.ds(n * size, size)] for n in range(pieces)],
        sems.at[pl.ds(4, pieces)],
    )
    for copy in small:
        copy.wait()
    where = lax.broadcasted_iota(jnp.int32, (1, rows), 1) // TILE
    bands = []
    for b in range(cols // TILE):
        band = jnp.zeros((1, rows), jnp.float32)
        for r in range(rows // TILE):
            band = jnp.where(where == r, flags_ref[r, b].astype(jnp.float32), band)
        bands.append(jnp.broadcast_to(band, (TILE, rows)))
    weight = jnp.concatenate(bands, axis=0)
    weight_bf16 = weight.astype(jnp.bfloat16)
    for p in range(2):
        vt_ref[p] = vis_ref[p].astype(jnp.float32).T * weight
    for k in range(dirs):
        rho_rows_ref[k : k + 1, :] = jnp.full((1, rows), rho_ref[cluster_ref[k]], jnp.float32)
    rho_packed_ref[...] = pack_plane(rho_rows_ref[...], 0, rows * rho_packed_ref.shape[0] // dirs)
    for n in range(pieces):
        large[n].wait()

        def turn(m, carry):
            for k in range(4):
                for p in range(2):
                    at = n * size + 4 * m + k
                    mt_ref[at, p] = model_ref[at, p].T * weight_bf16
            return carry

        lax.fori_loop(0, size // 4, turn, 0)


def residual(mt_ref, vt_ref, grow_ref, gcol_ref, z_ref, r_ref, p_ref, ct_ref):
    dirs, _, cols, rows = mt_ref.shape
    ct_ref[...] = gcol_ref[...].T
    chunk = 64

    def predict(n, carry):
        here = pl.ds(pl.multiple_of(n * chunk, chunk), chunk)
        ctile = ct_ref[here, :]
        acc_r = vt_ref[0, here, :]
        acc_i = vt_ref[1, here, :]
        for k in range(dirs):
            mr = mt_ref[k, 0, here, :].astype(jnp.float32)
            mi = mt_ref[k, 1, here, :].astype(jnp.float32)
            cr = jnp.broadcast_to(ctile[:, k : k + 1], (chunk, rows))
            ci = jnp.broadcast_to(ctile[:, dirs + k : dirs + k + 1], (chunk, rows))
            zr = mr * cr + mi * ci
            zi = mi * cr - mr * ci
            z_ref[k, 0, here, :] = zr
            z_ref[k, 1, here, :] = zi
            gr = grow_ref[k : k + 1, :]
            gi = grow_ref[dirs + k : dirs + k + 1, :]
            acc_r = acc_r - (gr * zr - gi * zi)
            acc_i = acc_i - (gr * zi + gi * zr)
        r_ref[0, here, :] = acc_r
        r_ref[1, here, :] = acc_i
        sq = acc_r * acc_r + acc_i * acc_i
        for c in range(0, chunk, 8):
            carry = carry + sq[c : c + 8]
        return carry

    p_ref[...] = lax.fori_loop(0, cols // chunk, predict, jnp.zeros(p_ref.shape, jnp.float32))


def terms_kernel(z_ref, r_ref, out_ref):
    dirs, _, cols, rows = z_ref.shape
    group = 8
    part = 4

    def terms(n, carry):
        k0 = pl.multiple_of(n * group, group)
        blocks = [[], [], []]
        for half in range(0, group, part):
            sums = [[None] * 3 for _ in range(part)]
            for c in range(0, cols, 8):
                rr = r_ref[0, c : c + 8, :]
                ri = r_ref[1, c : c + 8, :]
                for kk in range(part):
                    zr = z_ref[k0 + half + kk, 0, c : c + 8, :]
                    zi = z_ref[k0 + half + kk, 1, c : c + 8, :]
                    new = (zr * zr + zi * zi, zr * rr + zi * ri, zr * ri - zi * rr)
                    for s in range(3):
                        old = sums[kk][s]
                        sums[kk][s] = new[s] if old is None else old + new[s]
            for s in range(3):
                blocks[s] += [jnp.sum(sums[kk][s], axis=0, keepdims=True) for kk in range(part)]
        for s in range(3):
            out_ref[pl.ds(s * dirs + k0, group), :] = jnp.concatenate(blocks[s], axis=0)
        return carry

    lax.fori_loop(0, dirs // group, terms, 0)
    out_ref[3 * dirs :, :] = jnp.zeros((8, rows), jnp.float32)


def last_terms_kernel(ids_ref, z_ref, r_ref, *refs, span):
    outs, all_ref = refs[:-1], refs[-1]
    dirs, _, cols, rows = z_ref.shape
    depth = dirs * span // rows
    terms_kernel(z_ref, r_ref, all_ref)
    for n, out_ref in enumerate(outs):
        block = jnp.bitwise_xor(ids_ref[1], n)
        for q in range(3):
            plane = all_ref[q * dirs : (q + 1) * dirs, :]
            out_ref[q * depth : (q + 1) * depth, :] = pack_plane(plane, block, span)
        out_ref[3 * depth :, :] = jnp.zeros((8, rows), jnp.float32)


def first_kernel(ids_ref, *refs, ns, nz, span):
    rows_in = refs[:nz]
    cols_in = refs[nz : nz + ns]
    mt_ref, vt_ref = refs[nz + ns : nz + ns + 2]
    outs = refs[nz + ns + 2 : nz + ns + 5]
    grow_ref, gcol_ref, trow_ref, tcol_ref, ct_ref = refs[nz + ns + 5 :]
    dirs = mt_ref.shape[0]
    i, j = ids_ref[0], ids_ref[1]
    depth = dirs * span // mt_ref.shape[3]
    for pieces, g_ref, t_ref, me in ((rows_in, grow_ref, trow_ref, j), (cols_in, gcol_ref, tcol_ref, i)):
        blocks = [jnp.bitwise_xor(me, n) for n in range(len(pieces))]
        for q in range(4):
            plane = unpack_planes([p[q * depth : (q + 1) * depth, :] for p in pieces], blocks, span)
            dst = g_ref if q < 2 else t_ref
            at = (q % 2) * dirs
            dst[at : at + dirs, :] = plane
    residual(mt_ref, vt_ref, grow_ref, gcol_ref, *outs, ct_ref)


def sweep_kernel(ids_ref, *refs, ns, span, scale):
    pieces = refs[:ns]
    sum_ref, growin_ref, gcolin_ref, trow_ref, tcol_ref, rho_ref, mt_ref, vt_ref = refs[ns : ns + 8]
    outs = refs[ns + 8 : ns + 11]
    grow_ref, gcol_ref, ct_ref = refs[ns + 11 :]
    dirs = mt_ref.shape[0]
    i = ids_ref[0]
    depth = dirs * span // mt_ref.shape[3]
    power = pieces[0][3 * depth :, :]
    for p in pieces[1:]:
        power = power + p[3 * depth :, :]
    rho_eff = rho_ref[...] * (jnp.sum(power) * scale + EPS)
    re, im = slice(0, dirs), slice(dirs, 2 * dirs)
    grow_ref[re, :], grow_ref[im, :] = solve(
        sum_ref[0:dirs, :],
        sum_ref[dirs : 2 * dirs, :],
        sum_ref[2 * dirs : 3 * dirs, :],
        growin_ref[re, :],
        growin_ref[im, :],
        trow_ref[re, :],
        trow_ref[im, :],
        rho_eff,
    )
    blocks = [jnp.bitwise_xor(i, n) for n in range(ns)]
    a, cr, ci = [
        unpack_planes([p[q * depth : (q + 1) * depth, :] for p in pieces], blocks, span)
        for q in range(3)
    ]
    gcol_ref[re, :], gcol_ref[im, :] = solve(
        a, cr, ci, gcolin_ref[re, :], gcolin_ref[im, :], tcol_ref[re, :], tcol_ref[im, :], rho_eff
    )
    residual(mt_ref, vt_ref, grow_ref, gcol_ref, *outs, ct_ref)


def combine_kernel(ids_ref, *refs, nz, span):
    parts = refs[:nz]
    sum_ref, own_ref = refs[nz:]
    dirs = sum_ref.shape[0] // 3
    j = ids_ref[1]
    depth = dirs * span // sum_ref.shape[1]
    for q in range(3):
        at = slice(q * dirs, (q + 1) * dirs)
        total = parts[0][at, :]
        for p in parts[1:]:
            total = total + p[at, :]
        sum_ref[at, :] = total
        own_ref[q * depth : (q + 1) * depth, :] = pack_plane(total, j, span)
    power = parts[0][3 * dirs :, :]
    for p in parts[1:]:
        power = power + p[3 * dirs :, :]
    own_ref[3 * depth :, :] = power


def last_combine_kernel(ids_ref, *refs, nz, span):
    parts = refs[:nz]
    g_ref, t_ref, d_ref, power_ref, mail_ref = refs[nz:]
    dirs = g_ref.shape[0] // 2
    depth = dirs * span // g_ref.shape[1]
    j = ids_ref[1]
    total = parts[0][...]
    for p in parts[1:]:
        total = total + p[...]
    mail_ref[: 3 * depth, :] = total[: 3 * depth]
    power_ref[...] = total[3 * depth :]
    for n, ref in enumerate((g_ref, t_ref)):
        for p in range(2):
            at = (3 + 2 * n + p) * depth
            plane = ref[p * dirs : (p + 1) * dirs, :]
            mail_ref[at : at + depth, :] = pack_plane(plane, j, span)
    mail_ref[7 * depth :, :] = d_ref[...]


def final_kernel(ids_ref, *refs, ns, scale, pair, span, scal):
    powers = refs[:ns]
    mails = refs[ns : ns + 1 + pair]
    rho_ref = refs[ns + 1 + pair]
    outs = refs[ns + 2 + pair :]
    depth, lanes = rho_ref.shape
    dirs = depth * lanes // span
    power = powers[0][...]
    for p in powers[1:]:
        power = power + p[...]
    rho_eff = rho_ref[...] * (jnp.sum(power) * scale + EPS)
    news = []
    for mail in mails:
        a, cr, ci, gr, gi, tr, ti = [mail[q * depth : (q + 1) * depth, :] for q in range(7)]
        news.append(solve(a, cr, ci, gr, gi, tr, ti, rho_eff))
    fields = list(news[0])
    if pair:
        duals = [[m[q * depth : (q + 1) * depth, :] for q in (7, 8)] for m in mails]
        first = ids_ref[2] == 0
        coeffs, new_duals = [], []
        for p in range(2):
            own, other = [news[n][p] + duals[n][p] for n in range(2)]
            low, high = jnp.where(first, own, other), jnp.where(first, other, own)
            total = scal[0] * low + scal[1] * high
            coeffs.append(total / scal[2] / scal[2])
            brow = jnp.where(first, scal[0], scal[1])
            new_duals.append(duals[0][p] + news[0][p] - brow * coeffs[p])
        fields += coeffs + new_duals
    parts = lanes // span
    for at in range(0, len(fields), parts):
        group = fields[at : at + parts]
        plane = unpack_planes(group, list(range(len(group))), span)
        plane = jnp.concatenate([plane, jnp.zeros((lanes - dirs, lanes), jnp.float32)], axis=0)
        turned = plane.T
        for n in range(len(group)):
            out_ref = outs[(at + n) // 2]
            out_ref[(at + n) % 2] = turned[n * span : (n + 1) * span, :dirs]


SMEM = pl.BlockSpec(memory_space=pltpu.SMEM)
VMEM = pl.BlockSpec(memory_space=pltpu.VMEM)
HBM = pl.BlockSpec(memory_space=pltpu.HBM)


def f32(*shape):
    return jax.ShapeDtypeStruct(shape, jnp.float32)


def call(kernel, name, lead, args, outs, scratch=(), place=VMEM):
    if place is HBM:
        args = [pltpu.with_memory_space_constraint(x, pltpu.HBM) for x in args]
    return pl.pallas_call(
        kernel,
        in_specs=[SMEM] * len(lead) + [place] * len(args),
        out_specs=[VMEM] * len(outs),
        out_shape=outs,
        scratch_shapes=scratch,
        compiler_params=pltpu.CompilerParams(vmem_limit_bytes=VMEM_LIMIT),
        name=name,
    )(*lead, *args)


def swap(x, axis, n):
    size = lax.axis_size(axis)
    return lax.ppermute(x, axis, [(m, m ^ n) for m in range(size)])


def shards(vis, model, flags, gains, consensus, dual, rho, cluster):
    groups = lax.axis_size("chan")
    ns = lax.axis_size("srow")
    nz = lax.axis_size("scol")
    order = consensus.shape[1]
    dirs = gains.shape[1]
    span = gains.shape[3]
    rows, cols = vis.shape[2:]
    depth = dirs * span // rows
    i, j, f = lax.axis_index("srow"), lax.axis_index("scol"), lax.axis_index("chan")
    ids = jnp.stack([i, j, f]).astype(jnp.int32)
    pair = groups == 2 and order == 1

    table = basis_table(groups, order)
    brow = lax.dynamic_index_in_dim(table, f, 0, keepdims=False)
    own_in = [
        gains[0].transpose(1, 2, 0),
        consensus.transpose(1, 2, 3, 0),
        dual[0].transpose(1, 2, 0),
    ]
    start, dual_packed = call(
        pack_kernel,
        "pack",
        [brow],
        own_in,
        [f32(4 * depth, rows), f32(2 * depth, rows)],
        [pltpu.VMEM(x.shape, jnp.float32) for x in own_in] + [pltpu.SemaphoreType.DMA((3,))],
        HBM,
    )
    row_parts = [start] + [swap(start, "scol", n) for n in range(1, nz)]
    col_parts = [start] + [swap(start, "srow", n) for n in range(1, ns)]
    field_in = [rho, cluster, flags[0], model[0], vis[0]]
    mt, vt, rho_rows, rho_packed = call(
        prepare_kernel,
        "prepare",
        [],
        field_in,
        [
            jax.ShapeDtypeStruct((dirs, 2, cols, rows), jnp.bfloat16),
            f32(2, cols, rows),
            f32(dirs, rows),
            f32(depth, rows),
        ],
        [(pltpu.SMEM if n < 3 else pltpu.VMEM)(x.shape, x.dtype) for n, x in enumerate(field_in)]
        + [pltpu.SemaphoreType.DMA((12,))],
        HBM,
    )

    scratch = [pltpu.VMEM((cols, 2 * dirs), jnp.float32)]
    scale = 1.0 / (groups * STATIONS * STATIONS)
    plane = f32(2 * dirs, rows)
    fields = [f32(dirs, 2, cols, rows), f32(2, cols, rows), f32(8, rows)]
    z, r, power, grow, gcol, trow, tcol = call(
        functools.partial(first_kernel, ns=ns, nz=nz, span=span),
        "first",
        [ids],
        row_parts + col_parts + [mt, vt],
        fields + [plane, plane, plane, plane],
        scratch,
    )
    for step in range(ITERS):
        last = step == ITERS - 1
        if groups == 2:
            power = power + swap(power, ("chan", "srow"), ns + 1)
        else:
            power = lax.psum(power, "chan")
        if last:
            break
        partial = call(terms_kernel, "terms", [], [z, r], [f32(3 * dirs + 8, rows)])[0]
        partial = lax.dynamic_update_slice(partial, power, (3 * dirs, 0))
        order_z = sorted(range(1, nz), key=lambda n: (n > 2, -n))
        sums, own = call(
            functools.partial(combine_kernel, nz=nz, span=span),
            "combine",
            [ids],
            [partial] + [swap(partial, "scol", n) for n in order_z],
            [f32(3 * dirs, rows), f32(3 * depth + 8, rows)],
        )
        pieces = [own] + [swap(own, "srow", n) for n in range(1, ns)]
        z, r, power, grow, gcol = call(
            functools.partial(sweep_kernel, ns=ns, span=span, scale=scale),
            "sweep",
            [ids],
            pieces + [sums, grow, gcol, trow, tcol, rho_rows, mt, vt],
            fields + [plane, plane],
            scratch,
        )

    parts = call(
        functools.partial(last_terms_kernel, span=span),
        "terms",
        [ids],
        [z, r],
        [f32(3 * depth + 8, rows)] * nz,
        [pltpu.VMEM((3 * dirs + 8, rows), jnp.float32)],
    )
    parts = [lax.dynamic_update_slice(part, power, (3 * depth, 0)) for part in parts]
    power, mail = call(
        functools.partial(last_combine_kernel, nz=nz, span=span),
        "combine",
        [ids],
        [parts[0]] + [swap(parts[n], "scol", n) for n in range(1, nz)] + [grow, trow, dual_packed],
        [f32(8, rows), f32(9 * depth, rows)],
    )
    powers = [power] + [swap(power, "srow", n) for n in range(1, ns)]
    mails = [mail] + ([swap(mail, "chan", 1)] if pair else [])
    outs = call(
        functools.partial(
            final_kernel, ns=ns, scale=scale, pair=int(pair), span=span, scal=pair_scalars(pair)
        ),
        "final",
        [ids],
        powers + mails + [rho_packed],
        [f32(2, span, dirs)] * (3 if pair else 1),
    )
    outs = [x.transpose(2, 0, 1) for x in outs]
    if pair:
        g, coeffs, dual_new = outs
        return (g[None], coeffs[:, None], dual_new[None])
    g = outs[0]
    dual_own = dual[0]
    local = brow[None, :, None, None] * (g + dual_own)[:, None, :, :]
    coeffs = gram_solve(table, lax.psum(local, "chan"))
    dual_new = (
        dual_own + g - jnp.einsum("b,kbcp->kcp", brow, coeffs, precision=lax.Precision.HIGHEST)
    )
    return (g[None], coeffs, dual_new[None])


def solution(mesh):
    placed = (
        P("chan", None, "srow", "scol"),
        P("chan", None, None, "srow", "scol"),
        P("chan", "srow", "scol"),
        P("chan", None, None, ("srow", "scol")),
        P(None, None, None, ("srow", "scol")),
        P("chan", None, None, ("srow", "scol")),
        P(),
        P(),
    )
    return jax.shard_map(
        shards,
        mesh=mesh,
        in_specs=placed,
        out_specs=(
            P("chan", None, None, ("srow", "scol")),
            P(None, None, None, ("srow", "scol")),
            P("chan", None, None, ("srow", "scol")),
        ),
        check_vma=False,
    )
```

```python
import functools
import math

import jax
import jax.numpy as jnp
import numpy as np
from jax import lax
from jax.experimental import pallas as pl
from jax.experimental.pallas import tpu as pltpu
from jax.sharding import PartitionSpec as P

STATIONS = 512
TILE = 16
ITERS = 4

EPS = 1e-05
STEP = 0.5

VMEM_LIMIT = 24 << 20


def basis_table(groups, order):
    xval = (jnp.arange(groups, dtype=jnp.float32) + 0.5) / groups
    columns = [
        math.comb(order - 1, b) * xval**b * (1.0 - xval) ** (order - 1 - b) for b in range(order)
    ]
    return jnp.stack(columns, axis=1)


def pair_scalars(pair):
    if not pair:
        return None
    xval = (np.arange(2, dtype=np.float32) + np.float32(0.5)) / np.float32(2)
    column = xval**0 * (np.float32(1.0) - xval) ** 0
    return float(column[0]), float(column[1]), float(np.sqrt(np.sum(column * column)))


def gram_solve(table, rhs):
    gram = jnp.dot(table.T, table, precision=lax.Precision.HIGHEST)
    factor = jnp.linalg.cholesky(gram)
    order = rhs.shape[1]
    flat = jnp.moveaxis(rhs, 1, 0).reshape(order, -1)
    sol = jax.scipy.linalg.cho_solve((factor, True), flat)
    return jnp.moveaxis(sol.reshape((order, rhs.shape[0]) + rhs.shape[2:]), 0, 1)


def lane_block(shape, span):
    return lax.broadcasted_iota(jnp.int32, shape, 1) // span


def pack_plane(plane, block, span):
    dirs, lanes = plane.shape
    parts = lanes // span
    rows = dirs // parts
    where = lane_block((rows, lanes), span)
    packed = None
    for q in range(parts):
        piece = plane[q * rows : (q + 1) * rows]
        shift = lax.rem((q - block) * span + lanes, lanes)
        piece = pltpu.roll(piece, shift, 1)
        packed = piece if packed is None else jnp.where(where == q, piece, packed)
    return packed


def unpack_planes(pieces, blocks, span):
    rows, lanes = pieces[0].shape
    parts = lanes // span
    where = lane_block((rows, lanes), span)
    out = []
    for q in range(parts):
        plane = None
        for piece, block in zip(pieces, blocks):
            shift = lax.rem((block - q) * span + lanes, lanes)
            moved = pltpu.roll(piece, shift, 1)
            plane = moved if plane is None else jnp.where(where == block, moved, plane)
        out.append(plane)
    return jnp.concatenate(out, axis=0)


def solve(a, cr, ci, gr, gi, tr, ti, rho_eff):
    denom = a + rho_eff
    fresh_r = (cr + a * gr + rho_eff * tr) / denom
    fresh_i = (ci + a * gi + rho_eff * ti) / denom
    return gr + STEP * (fresh_r - gr), gi + STEP * (fresh_i - gi)


def fetch(sources, targets, sems):
    copies = [
        pltpu.make_async_copy(src, dst, sems.at[n])
        for n, (src, dst) in enumerate(zip(sources, targets))
    ]
    for copy in copies:
        copy.start()
    return copies


def pack_kernel(brow_ref, *refs):
    start_ref, dual_out_ref = refs[3:5]
    gains_ref, consensus_ref, dual_ref = refs[5:8]
    for copy in fetch(refs[:3], refs[5:8], refs[8]):
        copy.wait()
    span, dirs = gains_ref.shape[1:]
    lanes = start_ref.shape[1]
    depth = dirs * span // lanes
    rows = []
    for p in range(2):
        target = brow_ref[0] * consensus_ref[0, p]
        for b in range(1, consensus_ref.shape[0]):
            target = target + brow_ref[b] * consensus_ref[b, p]
        rows.append(target - dual_ref[p])
    for fields, out_ref in (
        ([gains_ref[0], gains_ref[1]] + rows, start_ref),
        ([dual_ref[0], dual_ref[1]], dual_out_ref),
    ):
        plane = to_plane(fields, lanes)[:dirs]
        for n in range(len(fields)):
            out_ref[n * depth : (n + 1) * depth, :] = pack_plane(plane, n, span)


def to_plane(fields, lanes):
    x = jnp.concatenate(fields, axis=0)
    if x.shape[0] < lanes:
        x = jnp.concatenate([x, jnp.zeros((lanes - x.shape[0], x.shape[1]), x.dtype)], axis=0)
    if x.shape[1] < lanes:
        x = jnp.concatenate([x, jnp.zeros((lanes, lanes - x.shape[1]), x.dtype)], axis=1)
    return x.T


def prepare_kernel(*refs):
    ins = refs[:5]
    mt_ref, vt_ref, rho_rows_ref, rho_packed_ref = refs[5:9]
    rho_ref, cluster_ref, flags_ref, model_ref, vis_ref, sems = refs[9:]
    dirs, _, rows, cols = model_ref.shape
    pieces = 8
    size = dirs // pieces
    small = fetch(ins[:3] + ins[4:], [rho_ref, cluster_ref, flags_ref, vis_ref], sems)
    large = fetch(
        [ins[3].at[pl.ds(n * size, size)] for n in range(pieces)],
        [model_ref.at[pl.ds(n * size, size)] for n in range(pieces)],
        sems.at[pl.ds(4, pieces)],
    )
    for copy in small:
        copy.wait()
    where = lax.broadcasted_iota(jnp.int32, (1, rows), 1) // TILE
    bands = []
    for b in range(cols // TILE):
        band = jnp.zeros((1, rows), jnp.float32)
        for r in range(rows // TILE):
            band = jnp.where(where == r, flags_ref[r, b].astype(jnp.float32), band)
        bands.append(jnp.broadcast_to(band, (TILE, rows)))
    weight = jnp.concatenate(bands, axis=0)
    weight_bf16 = weight.astype(jnp.bfloat16)
    for p in range(2):
        vt_ref[p] = vis_ref[p].astype(jnp.float32).T * weight
    for k in range(dirs):
        rho_rows_ref[k : k + 1, :] = jnp.full((1, rows), rho_ref[cluster_ref[k]], jnp.float32)
    rho_packed_ref[...] = pack_plane(rho_rows_ref[...], 0, rows * rho_packed_ref.shape[0] // dirs)
    for n in range(pieces):
        large[n].wait()

        def turn(m, carry):
            for k in range(4):
                for p in range(2):
                    at = n * size + 4 * m + k
                    mt_ref[at, p] = model_ref[at, p].T * weight_bf16
            return carry

        lax.fori_loop(0, size // 4, turn, 0)


def residual(mt_ref, vt_ref, grow_ref, gcol_ref, z_ref, r_ref, p_ref, ct_ref):
    dirs, _, cols, rows = mt_ref.shape
    ct_ref[...] = gcol_ref[...].T
    chunk = 64

    def predict(n, carry):
        here = pl.ds(pl.multiple_of(n * chunk, chunk), chunk)
        ctile = ct_ref[here, :]
        acc_r = vt_ref[0, here, :]
        acc_i = vt_ref[1, here, :]
        for k in range(dirs):
            mr = mt_ref[k, 0, here, :].astype(jnp.float32)
            mi = mt_ref[k, 1, here, :].astype(jnp.float32)
            cr = jnp.broadcast_to(ctile[:, k : k + 1], (chunk, rows))
            ci = jnp.broadcast_to(ctile[:, dirs + k : dirs + k + 1], (chunk, rows))
            zr = mr * cr + mi * ci
            zi = mi * cr - mr * ci
            z_ref[k, 0, here, :] = zr
            z_ref[k, 1, here, :] = zi
            gr = grow_ref[k : k + 1, :]
            gi = grow_ref[dirs + k : dirs + k + 1, :]
            acc_r = acc_r - (gr * zr - gi * zi)
            acc_i = acc_i - (gr * zi + gi * zr)
        r_ref[0, here, :] = acc_r
        r_ref[1, here, :] = acc_i
        sq = acc_r * acc_r + acc_i * acc_i
        for c in range(0, chunk, 8):
            carry = carry + sq[c : c + 8]
        return carry

    p_ref[...] = lax.fori_loop(0, cols // chunk, predict, jnp.zeros(p_ref.shape, jnp.float32))


def normal_terms(z_ref, r_ref, out_ref):
    dirs, _, cols, rows = z_ref.shape
    group = 8
    part = 4

    def terms(n, carry):
        k0 = pl.multiple_of(n * group, group)
        blocks = [[], [], []]
        for half in range(0, group, part):
            sums = [[None] * 3 for _ in range(part)]
            for c in range(0, cols, 8):
                rr = r_ref[0, c : c + 8, :]
                ri = r_ref[1, c : c + 8, :]
                for kk in range(part):
                    zr = z_ref[k0 + half + kk, 0, c : c + 8, :]
                    zi = z_ref[k0 + half + kk, 1, c : c + 8, :]
                    new = (zr * zr + zi * zi, zr * rr + zi * ri, zr * ri - zi * rr)
                    for s in range(3):
                        old = sums[kk][s]
                        sums[kk][s] = new[s] if old is None else old + new[s]
            for s in range(3):
                blocks[s] += [jnp.sum(sums[kk][s], axis=0, keepdims=True) for kk in range(part)]
        for s in range(3):
            out_ref[pl.ds(s * dirs + k0, group), :] = jnp.concatenate(blocks[s], axis=0)
        return carry

    lax.fori_loop(0, dirs // group, terms, 0)


def own_parity(shape, span, j):
    return lax.rem(lane_block(shape, span), 2) == lax.rem(j, 2)


def terms_kernel(ids_ref, z_ref, r_ref, same_ref, other_ref, all_ref, *, span):
    dirs, _, cols, rows = z_ref.shape
    half = dirs // 2
    normal_terms(z_ref, r_ref, all_ref)
    mine = own_parity((half, rows), span, ids_ref[1])
    for q in range(3):
        low = all_ref[q * dirs : q * dirs + half, :]
        high = pltpu.roll(all_ref[q * dirs + half : (q + 1) * dirs, :], span, 1)
        same_ref[q * half : (q + 1) * half, :] = jnp.where(mine, low, high)
        other_ref[q * half : (q + 1) * half, :] = jnp.where(mine, high, low)
    for ref in (same_ref, other_ref):
        ref[3 * half :, :] = jnp.zeros((8, rows), jnp.float32)


def unfold(same, other, span, j):
    mine = own_parity(same.shape, span, j)
    low = jnp.where(mine, same, other)
    high = pltpu.roll(jnp.where(mine, other, same), same.shape[1] - span, 1)
    return jnp.concatenate([low, high], axis=0)


def pack_folded(piece, j, span):
    half, lanes = piece.shape
    parts = lanes // span
    depth = 2 * half // parts
    where = lane_block((depth, lanes), span)
    packed = None
    for q in range(parts):
        block = j + q * depth // half
        at = q * depth % half
        shift = lax.rem((q - block) * span + 2 * lanes, lanes)
        moved = pltpu.roll(piece[at : at + depth], shift, 1)
        packed = moved if packed is None else jnp.where(where == q, moved, packed)
    return packed


def last_terms_kernel(ids_ref, z_ref, r_ref, *refs, span):
    outs, all_ref = refs[:-1], refs[-1]
    dirs, _, cols, rows = z_ref.shape
    depth = dirs * span // rows
    normal_terms(z_ref, r_ref, all_ref)
    for n, out_ref in enumerate(outs):
        block = jnp.bitwise_xor(ids_ref[1], n)
        for q in range(3):
            plane = all_ref[q * dirs : (q + 1) * dirs, :]
            out_ref[q * depth : (q + 1) * depth, :] = pack_plane(plane, block, span)
        out_ref[3 * depth :, :] = jnp.zeros((8, rows), jnp.float32)


def first_kernel(ids_ref, *refs, ns, nz, span):
    rows_in = refs[:nz]
    cols_in = refs[nz : nz + ns]
    mt_ref, vt_ref = refs[nz + ns : nz + ns + 2]
    outs = refs[nz + ns + 2 : nz + ns + 5]
    grow_ref, gcol_ref, trow_ref, tcol_ref, ct_ref = refs[nz + ns + 5 :]
    dirs = mt_ref.shape[0]
    i, j = ids_ref[0], ids_ref[1]
    depth = dirs * span // mt_ref.shape[3]
    for pieces, g_ref, t_ref, me in ((rows_in, grow_ref, trow_ref, j), (cols_in, gcol_ref, tcol_ref, i)):
        blocks = [jnp.bitwise_xor(me, n) for n in range(len(pieces))]
        for q in range(4):
            plane = unpack_planes([p[q * depth : (q + 1) * depth, :] for p in pieces], blocks, span)
            dst = g_ref if q < 2 else t_ref
            at = (q % 2) * dirs
            dst[at : at + dirs, :] = plane
    residual(mt_ref, vt_ref, grow_ref, gcol_ref, *outs, ct_ref)


def sweep_kernel(ids_ref, *refs, ns, span, scale):
    pieces = refs[:ns]
    same_ref, other_ref, growin_ref, gcolin_ref, trow_ref, tcol_ref = refs[ns : ns + 6]
    rho_ref, mt_ref, vt_ref = refs[ns + 6 : ns + 9]
    outs = refs[ns + 9 : ns + 12]
    grow_ref, gcol_ref, ct_ref = refs[ns + 12 :]
    dirs = mt_ref.shape[0]
    i = ids_ref[0]
    depth = dirs * span // mt_ref.shape[3]
    power = pieces[0][3 * depth :, :]
    for p in pieces[1:]:
        power = power + p[3 * depth :, :]
    rho_eff = rho_ref[...] * (jnp.sum(power) * scale + EPS)
    re, im = slice(0, dirs), slice(dirs, 2 * dirs)
    half = dirs // 2
    a, cr, ci = [
        unfold(
            same_ref[q * half : (q + 1) * half, :],
            other_ref[q * half : (q + 1) * half, :],
            span,
            ids_ref[1],
        )
        for q in range(3)
    ]
    grow_ref[re, :], grow_ref[im, :] = solve(
        a, cr, ci, growin_ref[re, :], growin_ref[im, :], trow_ref[re, :], trow_ref[im, :], rho_eff
    )
    blocks = [jnp.bitwise_xor(i, n) for n in range(ns)]
    a, cr, ci = [
        unpack_planes([p[q * depth : (q + 1) * depth, :] for p in pieces], blocks, span)
        for q in range(3)
    ]
    gcol_ref[re, :], gcol_ref[im, :] = solve(
        a, cr, ci, gcolin_ref[re, :], gcolin_ref[im, :], tcol_ref[re, :], tcol_ref[im, :], rho_eff
    )
    residual(mt_ref, vt_ref, grow_ref, gcol_ref, *outs, ct_ref)


def combine_kernel(ids_ref, *refs, nz, span):
    parts = refs[:nz]
    pair_ref, own_ref = refs[nz:]
    half = pair_ref.shape[0] // 3
    depth = 2 * half * span // pair_ref.shape[1]
    total = parts[0][...]
    for p in parts[1:]:
        total = total + p[...]
    pair_ref[...] = total[: 3 * half]
    for q in range(3):
        piece = total[q * half : (q + 1) * half]
        own_ref[q * depth : (q + 1) * depth, :] = pack_folded(piece, ids_ref[1], span)
    own_ref[3 * depth :, :] = total[3 * half :]


def last_combine_kernel(ids_ref, *refs, nz, span):
    parts = refs[:nz]
    g_ref, t_ref, d_ref, power_ref, mail_ref = refs[nz:]
    dirs = g_ref.shape[0] // 2
    depth = dirs * span // g_ref.shape[1]
    j = ids_ref[1]
    total = parts[0][...]
    for p in parts[1:]:
        total = total + p[...]
    mail_ref[: 3 * depth, :] = total[: 3 * depth]
    power_ref[...] = total[3 * depth :]
    for n, ref in enumerate((g_ref, t_ref)):
        for p in range(2):
            at = (3 + 2 * n + p) * depth
            plane = ref[p * dirs : (p + 1) * dirs, :]
            mail_ref[at : at + depth, :] = pack_plane(plane, j, span)
    mail_ref[7 * depth :, :] = d_ref[...]


def final_kernel(ids_ref, *refs, ns, scale, pair, span, scal):
    powers = refs[:ns]
    mails = refs[ns : ns + 1 + pair]
    rho_ref = refs[ns + 1 + pair]
    outs = refs[ns + 2 + pair :]
    depth, lanes = rho_ref.shape
    dirs = depth * lanes // span
    power = powers[0][...]
    for p in powers[1:]:
        power = power + p[...]
    rho_eff = rho_ref[...] * (jnp.sum(power) * scale + EPS)
    news = []
    for mail in mails:
        a, cr, ci, gr, gi, tr, ti = [mail[q * depth : (q + 1) * depth, :] for q in range(7)]
        news.append(solve(a, cr, ci, gr, gi, tr, ti, rho_eff))
    fields = list(news[0])
    if pair:
        duals = [[m[q * depth : (q + 1) * depth, :] for q in (7, 8)] for m in mails]
        first = ids_ref[2] == 0
        coeffs, new_duals = [], []
        for p in range(2):
            own, other = [news[n][p] + duals[n][p] for n in range(2)]
            low, high = jnp.where(first, own, other), jnp.where(first, other, own)
            total = scal[0] * low + scal[1] * high
            coeffs.append(total / scal[2] / scal[2])
            brow = jnp.where(first, scal[0], scal[1])
            new_duals.append(duals[0][p] + news[0][p] - brow * coeffs[p])
        fields += coeffs + new_duals
    parts = lanes // span
    for at in range(0, len(fields), parts):
        group = fields[at : at + parts]
        plane = unpack_planes(group, list(range(len(group))), span)
        plane = jnp.concatenate([plane, jnp.zeros((lanes - dirs, lanes), jnp.float32)], axis=0)
        turned = plane.T
        for n in range(len(group)):
            out_ref = outs[(at + n) // 2]
            out_ref[(at + n) % 2] = turned[n * span : (n + 1) * span, :dirs]


SMEM = pl.BlockSpec(memory_space=pltpu.SMEM)
VMEM = pl.BlockSpec(memory_space=pltpu.VMEM)
HBM = pl.BlockSpec(memory_space=pltpu.HBM)


def f32(*shape):
    return jax.ShapeDtypeStruct(shape, jnp.float32)


def call(kernel, name, lead, args, outs, scratch=(), place=VMEM):
    if place is HBM:
        args = [pltpu.with_memory_space_constraint(x, pltpu.HBM) for x in args]
    return pl.pallas_call(
        kernel,
        in_specs=[SMEM] * len(lead) + [place] * len(args),
        out_specs=[VMEM] * len(outs),
        out_shape=outs,
        scratch_shapes=scratch,
        compiler_params=pltpu.CompilerParams(vmem_limit_bytes=VMEM_LIMIT),
        name=name,
    )(*lead, *args)


def swap(x, axis, n):
    size = lax.axis_size(axis)
    return lax.ppermute(x, axis, [(m, m ^ n) for m in range(size)])


def shards(vis, model, flags, gains, consensus, dual, rho, cluster):
    groups = lax.axis_size("chan")
    ns = lax.axis_size("srow")
    nz = lax.axis_size("scol")
    order = consensus.shape[1]
    dirs = gains.shape[1]
    span = gains.shape[3]
    rows, cols = vis.shape[2:]
    depth = dirs * span // rows
    i, j, f = lax.axis_index("srow"), lax.axis_index("scol"), lax.axis_index("chan")
    ids = jnp.stack([i, j, f]).astype(jnp.int32)
    pair = groups == 2 and order == 1

    table = basis_table(groups, order)
    brow = lax.dynamic_index_in_dim(table, f, 0, keepdims=False)
    own_in = [
        gains[0].transpose(1, 2, 0),
        consensus.transpose(1, 2, 3, 0),
        dual[0].transpose(1, 2, 0),
    ]
    start, dual_packed = call(
        pack_kernel,
        "pack",
        [brow],
        own_in,
        [f32(4 * depth, rows), f32(2 * depth, rows)],
        [pltpu.VMEM(x.shape, jnp.float32) for x in own_in] + [pltpu.SemaphoreType.DMA((3,))],
        HBM,
    )
    row_parts = [start] + [swap(start, "scol", n) for n in range(1, nz)]
    col_parts = [start] + [swap(start, "srow", n) for n in range(1, ns)]
    field_in = [rho, cluster, flags[0], model[0], vis[0]]
    mt, vt, rho_rows, rho_packed = call(
        prepare_kernel,
        "prepare",
        [],
        field_in,
        [
            jax.ShapeDtypeStruct((dirs, 2, cols, rows), jnp.bfloat16),
            f32(2, cols, rows),
            f32(dirs, rows),
            f32(depth, rows),
        ],
        [(pltpu.SMEM if n < 3 else pltpu.VMEM)(x.shape, x.dtype) for n, x in enumerate(field_in)]
        + [pltpu.SemaphoreType.DMA((12,))],
        HBM,
    )

    scratch = [pltpu.VMEM((cols, 2 * dirs), jnp.float32)]
    scale = 1.0 / (groups * STATIONS * STATIONS)
    plane = f32(2 * dirs, rows)
    fields = [f32(dirs, 2, cols, rows), f32(2, cols, rows), f32(8, rows)]
    z, r, power, grow, gcol, trow, tcol = call(
        functools.partial(first_kernel, ns=ns, nz=nz, span=span),
        "first",
        [ids],
        row_parts + col_parts + [mt, vt],
        fields + [plane, plane, plane, plane],
        scratch,
    )
    for step in range(ITERS):
        last = step == ITERS - 1
        if groups == 2:
            power = power + swap(power, ("chan", "srow"), ns + 1)
        else:
            power = lax.psum(power, "chan")
        if last:
            break
        half = 3 * dirs // 2
        same, other = call(
            functools.partial(terms_kernel, span=span),
            "terms",
            [ids],
            [z, r],
            [f32(half + 8, rows)] * 2,
            [pltpu.VMEM((3 * dirs, rows), jnp.float32)],
        )
        same = lax.dynamic_update_slice(same, power, (half, 0))
        other = lax.dynamic_update_slice(other, power, (half, 0))
        pair_sums, own = call(
            functools.partial(combine_kernel, nz=nz, span=span),
            "combine",
            [ids],
            [same] + [swap(same if n % 2 == 0 else other, "scol", n) for n in range(1, nz)],
            [f32(half, rows), f32(3 * depth + 8, rows)],
        )
        other_sums = swap(pair_sums, "scol", 1)
        pieces = [own] + [swap(own, "srow", n) for n in range(1, ns)]
        z, r, power, grow, gcol = call(
            functools.partial(sweep_kernel, ns=ns, span=span, scale=scale),
            "sweep",
            [ids],
            pieces + [pair_sums, other_sums, grow, gcol, trow, tcol, rho_rows, mt, vt],
            fields + [plane, plane],
            scratch,
        )

    parts = call(
        functools.partial(last_terms_kernel, span=span),
        "terms",
        [ids],
        [z, r],
        [f32(3 * depth + 8, rows)] * nz,
        [pltpu.VMEM((3 * dirs, rows), jnp.float32)],
    )
    parts = [lax.dynamic_update_slice(part, power, (3 * depth, 0)) for part in parts]
    power, mail = call(
        functools.partial(last_combine_kernel, nz=nz, span=span),
        "combine",
        [ids],
        [parts[0]] + [swap(parts[n], "scol", n) for n in range(1, nz)] + [grow, trow, dual_packed],
        [f32(8, rows), f32(9 * depth, rows)],
    )
    powers = [power] + [swap(power, "srow", n) for n in range(1, ns)]
    mails = [mail] + ([swap(mail, "chan", 1)] if pair else [])
    outs = call(
        functools.partial(
            final_kernel, ns=ns, scale=scale, pair=int(pair), span=span, scal=pair_scalars(pair)
        ),
        "final",
        [ids],
        powers + mails + [rho_packed],
        [f32(2, span, dirs)] * (3 if pair else 1),
    )
    outs = [x.transpose(2, 0, 1) for x in outs]
    if pair:
        g, coeffs, dual_new = outs
        return (g[None], coeffs[:, None], dual_new[None])
    g = outs[0]
    dual_own = dual[0]
    local = brow[None, :, None, None] * (g + dual_own)[:, None, :, :]
    coeffs = gram_solve(table, lax.psum(local, "chan"))
    dual_new = (
        dual_own + g - jnp.einsum("b,kbcp->kcp", brow, coeffs, precision=lax.Precision.HIGHEST)
    )
    return (g[None], coeffs, dual_new[None])


def solution(mesh):
    placed = (
        P("chan", None, "srow", "scol"),
        P("chan", None, None, "srow", "scol"),
        P("chan", "srow", "scol"),
        P("chan", None, None, ("srow", "scol")),
        P(None, None, None, ("srow", "scol")),
        P("chan", None, None, ("srow", "scol")),
        P(),
        P(),
    )
    return jax.shard_map(
        shards,
        mesh=mesh,
        in_specs=placed,
        out_specs=(
            P("chan", None, None, ("srow", "scol")),
            P(None, None, None, ("srow", "scol")),
            P("chan", None, None, ("srow", "scol")),
        ),
        check_vma=False,
    )
```

```python
import functools
import math

import jax
import jax.numpy as jnp
import numpy as np
from jax import lax
from jax.experimental import pallas as pl
from jax.experimental.pallas import tpu as pltpu
from jax.sharding import PartitionSpec as P

STATIONS = 512
TILE = 16
ITERS = 4

EPS = 1e-05
STEP = 0.5

VMEM_LIMIT = 24 << 20


def basis_table(groups, order):
    xval = (jnp.arange(groups, dtype=jnp.float32) + 0.5) / groups
    columns = [
        math.comb(order - 1, b) * xval**b * (1.0 - xval) ** (order - 1 - b) for b in range(order)
    ]
    return jnp.stack(columns, axis=1)


def pair_scalars(pair):
    if not pair:
        return None
    xval = (np.arange(2, dtype=np.float32) + np.float32(0.5)) / np.float32(2)
    column = xval**0 * (np.float32(1.0) - xval) ** 0
    return float(column[0]), float(column[1]), float(np.sqrt(np.sum(column * column)))


def gram_solve(table, rhs):
    gram = jnp.dot(table.T, table, precision=lax.Precision.HIGHEST)
    factor = jnp.linalg.cholesky(gram)
    order = rhs.shape[1]
    flat = jnp.moveaxis(rhs, 1, 0).reshape(order, -1)
    sol = jax.scipy.linalg.cho_solve((factor, True), flat)
    return jnp.moveaxis(sol.reshape((order, rhs.shape[0]) + rhs.shape[2:]), 0, 1)


def lane_block(shape, span):
    return lax.broadcasted_iota(jnp.int32, shape, 1) // span


def pack_plane(plane, block, span):
    dirs, lanes = plane.shape
    parts = lanes // span
    rows = dirs // parts
    where = lane_block((rows, lanes), span)
    packed = None
    for q in range(parts):
        piece = plane[q * rows : (q + 1) * rows]
        shift = lax.rem((q - block) * span + lanes, lanes)
        piece = pltpu.roll(piece, shift, 1)
        packed = piece if packed is None else jnp.where(where == q, piece, packed)
    return packed


def unpack_planes(pieces, blocks, span):
    rows, lanes = pieces[0].shape
    parts = lanes // span
    where = lane_block((rows, lanes), span)
    out = []
    for q in range(parts):
        plane = None
        for piece, block in zip(pieces, blocks):
            shift = lax.rem((block - q) * span + lanes, lanes)
            moved = pltpu.roll(piece, shift, 1)
            plane = moved if plane is None else jnp.where(where == block, moved, plane)
        out.append(plane)
    return jnp.concatenate(out, axis=0)


def solve(a, cr, ci, gr, gi, tr, ti, rho_eff):
    denom = a + rho_eff
    fresh_r = (cr + a * gr + rho_eff * tr) / denom
    fresh_i = (ci + a * gi + rho_eff * ti) / denom
    return gr + STEP * (fresh_r - gr), gi + STEP * (fresh_i - gi)


def fetch(sources, targets, sems):
    copies = [
        pltpu.make_async_copy(src, dst, sems.at[n])
        for n, (src, dst) in enumerate(zip(sources, targets))
    ]
    for copy in copies:
        copy.start()
    return copies


def pack_kernel(*refs, alone):
    brow_ref, refs = ([1.0], refs) if alone else (refs[0], refs[1:])
    start_ref, dual_out_ref = refs[3:5]
    gains_ref, consensus_ref, dual_ref = refs[5:8]
    for copy in fetch(refs[:3], refs[5:8], refs[8]):
        copy.wait()
    span, dirs = gains_ref.shape[1:]
    lanes = start_ref.shape[1]
    depth = dirs * span // lanes
    rows = []
    for p in range(2):
        target = brow_ref[0] * consensus_ref[0, p]
        for b in range(1, consensus_ref.shape[0]):
            target = target + brow_ref[b] * consensus_ref[b, p]
        rows.append(target - dual_ref[p])
    for fields, out_ref in (
        ([gains_ref[0], gains_ref[1]] + rows, start_ref),
        ([dual_ref[0], dual_ref[1]], dual_out_ref),
    ):
        plane = to_plane(fields, lanes)[:dirs]
        for n in range(len(fields)):
            out_ref[n * depth : (n + 1) * depth, :] = pack_plane(plane, n, span)


def to_plane(fields, lanes):
    x = jnp.concatenate(fields, axis=0)
    if x.shape[0] < lanes:
        x = jnp.concatenate([x, jnp.zeros((lanes - x.shape[0], x.shape[1]), x.dtype)], axis=0)
    if x.shape[1] < lanes:
        x = jnp.concatenate([x, jnp.zeros((lanes, lanes - x.shape[1]), x.dtype)], axis=1)
    return x.T


def prepare_kernel(*refs):
    ins = refs[:5]
    mt_ref, vt_ref, rho_rows_ref, rho_packed_ref = refs[5:9]
    rho_ref, cluster_ref, flags_ref, model_ref, vis_ref, sems = refs[9:]
    dirs, _, rows, cols = model_ref.shape
    pieces = 8
    size = dirs // pieces
    small = fetch(ins[:3] + ins[4:], [rho_ref, cluster_ref, flags_ref, vis_ref], sems)
    large = fetch(
        [ins[3].at[pl.ds(n * size, size)] for n in range(pieces)],
        [model_ref.at[pl.ds(n * size, size)] for n in range(pieces)],
        sems.at[pl.ds(4, pieces)],
    )
    for copy in small:
        copy.wait()
    where = lax.broadcasted_iota(jnp.int32, (1, rows), 1) // TILE
    bands = []
    for b in range(cols // TILE):
        band = jnp.zeros((1, rows), jnp.float32)
        for r in range(rows // TILE):
            band = jnp.where(where == r, flags_ref[r, b].astype(jnp.float32), band)
        bands.append(jnp.broadcast_to(band, (TILE, rows)))
    weight = jnp.concatenate(bands, axis=0)
    weight_bf16 = weight.astype(jnp.bfloat16)
    for p in range(2):
        vt_ref[p] = vis_ref[p].astype(jnp.float32).T * weight
    for k in range(dirs):
        rho_rows_ref[k : k + 1, :] = jnp.full((1, rows), rho_ref[cluster_ref[k]], jnp.float32)
    rho_packed_ref[...] = pack_plane(rho_rows_ref[...], 0, rows * rho_packed_ref.shape[0] // dirs)
    for n in range(pieces):
        large[n].wait()

        def turn(m, carry):
            for k in range(4):
                for p in range(2):
                    at = n * size + 4 * m + k
                    mt_ref[at, p] = model_ref[at, p].T * weight_bf16
            return carry

        lax.fori_loop(0, size // 4, turn, 0)


def residual(mt_ref, vt_ref, grow_ref, gcol_ref, z_ref, r_ref, p_ref, ct_ref):
    dirs, _, cols, rows = mt_ref.shape
    ct_ref[...] = gcol_ref[...].T
    chunk = 64

    def predict(n, carry):
        here = pl.ds(pl.multiple_of(n * chunk, chunk), chunk)
        ctile = ct_ref[here, :]
        acc_r = vt_ref[0, here, :]
        acc_i = vt_ref[1, here, :]
        for k in range(dirs):
            mr = mt_ref[k, 0, here, :].astype(jnp.float32)
            mi = mt_ref[k, 1, here, :].astype(jnp.float32)
            cr = jnp.broadcast_to(ctile[:, k : k + 1], (chunk, rows))
            ci = jnp.broadcast_to(ctile[:, dirs + k : dirs + k + 1], (chunk, rows))
            zr = mr * cr + mi * ci
            zi = mi * cr - mr * ci
            z_ref[k, 0, here, :] = zr
            z_ref[k, 1, here, :] = zi
            gr = grow_ref[k : k + 1, :]
            gi = grow_ref[dirs + k : dirs + k + 1, :]
            acc_r = acc_r - (gr * zr - gi * zi)
            acc_i = acc_i - (gr * zi + gi * zr)
        r_ref[0, here, :] = acc_r
        r_ref[1, here, :] = acc_i
        sq = acc_r * acc_r + acc_i * acc_i
        for c in range(0, chunk, 8):
            carry = carry + sq[c : c + 8]
        return carry

    p_ref[...] = lax.fori_loop(0, cols // chunk, predict, jnp.zeros(p_ref.shape, jnp.float32))


def normal_terms(z_ref, r_ref, out_ref):
    dirs, _, cols, rows = z_ref.shape
    group = 8
    part = 4

    def terms(n, carry):
        k0 = pl.multiple_of(n * group, group)
        blocks = [[], [], []]
        for half in range(0, group, part):
            sums = [[None] * 3 for _ in range(part)]
            for c in range(0, cols, 8):
                rr = r_ref[0, c : c + 8, :]
                ri = r_ref[1, c : c + 8, :]
                for kk in range(part):
                    zr = z_ref[k0 + half + kk, 0, c : c + 8, :]
                    zi = z_ref[k0 + half + kk, 1, c : c + 8, :]
                    new = (zr * zr + zi * zi, zr * rr + zi * ri, zr * ri - zi * rr)
                    for s in range(3):
                        old = sums[kk][s]
                        sums[kk][s] = new[s] if old is None else old + new[s]
            for s in range(3):
                blocks[s] += [jnp.sum(sums[kk][s], axis=0, keepdims=True) for kk in range(part)]
        for s in range(3):
            out_ref[pl.ds(s * dirs + k0, group), :] = jnp.concatenate(blocks[s], axis=0)
        return carry

    lax.fori_loop(0, dirs // group, terms, 0)


def own_parity(shape, span, j):
    return lax.rem(lane_block(shape, span), 2) == lax.rem(j, 2)


def terms_kernel(z_ref, r_ref, same_ref, other_ref, all_ref, *, span):
    dirs, _, cols, rows = z_ref.shape
    half = dirs // 2
    normal_terms(z_ref, r_ref, all_ref)
    mine = own_parity((half, rows), span, lax.axis_index("scol"))
    for q in range(3):
        low = all_ref[q * dirs : q * dirs + half, :]
        high = pltpu.roll(all_ref[q * dirs + half : (q + 1) * dirs, :], span, 1)
        same_ref[q * half : (q + 1) * half, :] = jnp.where(mine, low, high)
        other_ref[q * half : (q + 1) * half, :] = jnp.where(mine, high, low)
    for ref in (same_ref, other_ref):
        ref[3 * half :, :] = jnp.zeros((8, rows), jnp.float32)


def unfold(same, other, span, j):
    mine = own_parity(same.shape, span, j)
    low = jnp.where(mine, same, other)
    high = pltpu.roll(jnp.where(mine, other, same), same.shape[1] - span, 1)
    return jnp.concatenate([low, high], axis=0)


def pack_folded(piece, j, span):
    half, lanes = piece.shape
    parts = lanes // span
    depth = 2 * half // parts
    where = lane_block((depth, lanes), span)
    packed = None
    for q in range(parts):
        block = j + q * depth // half
        at = q * depth % half
        shift = lax.rem((q - block) * span + 2 * lanes, lanes)
        moved = pltpu.roll(piece[at : at + depth], shift, 1)
        packed = moved if packed is None else jnp.where(where == q, moved, packed)
    return packed


def last_terms_kernel(z_ref, r_ref, *refs, span):
    outs, all_ref = refs[:-1], refs[-1]
    dirs, _, cols, rows = z_ref.shape
    depth = dirs * span // rows
    normal_terms(z_ref, r_ref, all_ref)
    for n, out_ref in enumerate(outs):
        block = jnp.bitwise_xor(lax.axis_index("scol"), n)
        for q in range(3):
            plane = all_ref[q * dirs : (q + 1) * dirs, :]
            out_ref[q * depth : (q + 1) * depth, :] = pack_plane(plane, block, span)
        out_ref[3 * depth :, :] = jnp.zeros((8, rows), jnp.float32)


def first_kernel(*refs, ns, nz, span):
    rows_in = refs[: 2 * nz : 2]
    cols_in = refs[1 : 2 * nz : 2]
    mt_ref, vt_ref = refs[nz + ns : nz + ns + 2]
    outs = refs[nz + ns + 2 : nz + ns + 5]
    grow_ref, gcol_ref, trow_ref, tcol_ref, ct_ref = refs[nz + ns + 5 :]
    dirs = mt_ref.shape[0]
    i, j = lax.axis_index("srow"), lax.axis_index("scol")
    depth = dirs * span // mt_ref.shape[3]
    for pieces, g_ref, t_ref, me in ((rows_in, grow_ref, trow_ref, j), (cols_in, gcol_ref, tcol_ref, i)):
        blocks = [jnp.bitwise_xor(me, n) for n in range(len(pieces))]
        for q in range(4):
            plane = unpack_planes([p[q * depth : (q + 1) * depth, :] for p in pieces], blocks, span)
            dst = g_ref if q < 2 else t_ref
            at = (q % 2) * dirs
            dst[at : at + dirs, :] = plane
    residual(mt_ref, vt_ref, grow_ref, gcol_ref, *outs, ct_ref)


def sweep_kernel(*refs, ns, span, scale):
    pieces = refs[:ns]
    same_ref, other_ref, growin_ref, gcolin_ref, trow_ref, tcol_ref = refs[ns : ns + 6]
    rho_ref, mt_ref, vt_ref = refs[ns + 6 : ns + 9]
    outs = refs[ns + 9 : ns + 12]
    grow_ref, gcol_ref, ct_ref = refs[ns + 12 :]
    dirs = mt_ref.shape[0]
    i = lax.axis_index("srow")
    depth = dirs * span // mt_ref.shape[3]
    power = pieces[0][3 * depth :, :]
    for p in pieces[1:]:
        power = power + p[3 * depth :, :]
    rho_eff = rho_ref[...] * (jnp.sum(power) * scale + EPS)
    re, im = slice(0, dirs), slice(dirs, 2 * dirs)
    half = dirs // 2
    a, cr, ci = [
        unfold(
            same_ref[q * half : (q + 1) * half, :],
            other_ref[q * half : (q + 1) * half, :],
            span,
            lax.axis_index("scol"),
        )
        for q in range(3)
    ]
    grow_ref[re, :], grow_ref[im, :] = solve(
        a, cr, ci, growin_ref[re, :], growin_ref[im, :], trow_ref[re, :], trow_ref[im, :], rho_eff
    )
    blocks = [jnp.bitwise_xor(i, n) for n in range(ns)]
    a, cr, ci = [
        unpack_planes([p[q * depth : (q + 1) * depth, :] for p in pieces], blocks, span)
        for q in range(3)
    ]
    gcol_ref[re, :], gcol_ref[im, :] = solve(
        a, cr, ci, gcolin_ref[re, :], gcolin_ref[im, :], tcol_ref[re, :], tcol_ref[im, :], rho_eff
    )
    residual(mt_ref, vt_ref, grow_ref, gcol_ref, *outs, ct_ref)


def combine_kernel(*refs, nz, span):
    parts = refs[:nz]
    pair_ref, own_ref = refs[nz:]
    half = pair_ref.shape[0] // 3
    depth = 2 * half * span // pair_ref.shape[1]
    total = parts[0][...]
    for p in parts[1:]:
        total = total + p[...]
    pair_ref[...] = total[: 3 * half]
    for q in range(3):
        piece = total[q * half : (q + 1) * half]
        own_ref[q * depth : (q + 1) * depth, :] = pack_folded(piece, lax.axis_index("scol"), span)
    own_ref[3 * depth :, :] = total[3 * half :]


def last_combine_kernel(*refs, nz, span):
    parts = refs[:nz]
    g_ref, t_ref, d_ref, power_ref, mail_ref = refs[nz:]
    dirs = g_ref.shape[0] // 2
    depth = dirs * span // g_ref.shape[1]
    j = lax.axis_index("scol")
    total = parts[0][...]
    for p in parts[1:]:
        total = total + p[...]
    mail_ref[: 3 * depth, :] = total[: 3 * depth]
    power_ref[...] = total[3 * depth :]
    for n, ref in enumerate((g_ref, t_ref)):
        for p in range(2):
            at = (3 + 2 * n + p) * depth
            plane = ref[p * dirs : (p + 1) * dirs, :]
            mail_ref[at : at + depth, :] = pack_plane(plane, j, span)
    mail_ref[7 * depth :, :] = d_ref[...]


def final_kernel(*refs, ns, scale, pair, span, scal):
    powers = refs[:ns]
    mails = refs[ns : ns + 1 + pair]
    rho_ref = refs[ns + 1 + pair]
    outs = refs[ns + 2 + pair :]
    depth, lanes = rho_ref.shape
    dirs = depth * lanes // span
    power = powers[0][...]
    for p in powers[1:]:
        power = power + p[...]
    rho_eff = rho_ref[...] * (jnp.sum(power) * scale + EPS)
    news = []
    for mail in mails:
        a, cr, ci, gr, gi, tr, ti = [mail[q * depth : (q + 1) * depth, :] for q in range(7)]
        news.append(solve(a, cr, ci, gr, gi, tr, ti, rho_eff))
    fields = list(news[0])
    if pair:
        duals = [[m[q * depth : (q + 1) * depth, :] for q in (7, 8)] for m in mails]
        first = lax.axis_index("chan") == 0
        coeffs, new_duals = [], []
        for p in range(2):
            own, other = [news[n][p] + duals[n][p] for n in range(2)]
            low, high = jnp.where(first, own, other), jnp.where(first, other, own)
            total = scal[0] * low + scal[1] * high
            coeffs.append(total / scal[2] / scal[2])
            brow = jnp.where(first, scal[0], scal[1])
            new_duals.append(duals[0][p] + news[0][p] - brow * coeffs[p])
        fields += coeffs + new_duals
    parts = lanes // span
    for at in range(0, len(fields), parts):
        group = fields[at : at + parts]
        plane = unpack_planes(group, list(range(len(group))), span)
        plane = jnp.concatenate([plane, jnp.zeros((lanes - dirs, lanes), jnp.float32)], axis=0)
        turned = plane.T
        for n in range(len(group)):
            out_ref = outs[(at + n) // 2]
            out_ref[(at + n) % 2] = turned[n * span : (n + 1) * span, :dirs]


SMEM = pl.BlockSpec(memory_space=pltpu.SMEM)
VMEM = pl.BlockSpec(memory_space=pltpu.VMEM)
HBM = pl.BlockSpec(memory_space=pltpu.HBM)


def f32(*shape):
    return jax.ShapeDtypeStruct(shape, jnp.float32)


def call(kernel, name, lead, args, outs, scratch=(), place=VMEM):
    if place is HBM:
        args = [pltpu.with_memory_space_constraint(x, pltpu.HBM) for x in args]
    return pl.pallas_call(
        kernel,
        in_specs=[SMEM] * len(lead) + [place] * len(args),
        out_specs=[VMEM] * len(outs),
        out_shape=outs,
        scratch_shapes=scratch,
        compiler_params=pltpu.CompilerParams(vmem_limit_bytes=VMEM_LIMIT),
        name=name,
    )(*lead, *args)


def swap(x, axis, n):
    size = lax.axis_size(axis)
    return lax.ppermute(x, axis, [(m, m ^ n) for m in range(size)])


def shards(vis, model, flags, gains, consensus, dual, rho, cluster):
    groups = lax.axis_size("chan")
    ns = lax.axis_size("srow")
    nz = lax.axis_size("scol")
    order = consensus.shape[1]
    dirs = gains.shape[1]
    span = gains.shape[3]
    rows, cols = vis.shape[2:]
    depth = dirs * span // rows
    f = lax.axis_index("chan")
    pair = groups == 2 and order == 1

    table = basis_table(groups, order)
    brow = lax.dynamic_index_in_dim(table, f, 0, keepdims=False)
    own_in = [
        gains[0].transpose(1, 2, 0),
        consensus.transpose(1, 2, 3, 0),
        dual[0].transpose(1, 2, 0),
    ]
    start, dual_packed = call(
        functools.partial(pack_kernel, alone=order == 1),
        "pack",
        [] if order == 1 else [brow],
        own_in,
        [f32(4 * depth, rows), f32(2 * depth, rows)],
        [pltpu.VMEM(x.shape, jnp.float32) for x in own_in] + [pltpu.SemaphoreType.DMA((3,))],
        HBM,
    )
    row_parts, col_parts = [start], [start]
    for n in range(1, max(ns, nz)):
        col_parts += [swap(start, "srow", n)] if n < ns else []
        row_parts += [swap(start, "scol", n)] if n < nz else []
    field_in = [rho, cluster, flags[0], model[0], vis[0]]
    mt, vt, rho_rows, rho_packed = call(
        prepare_kernel,
        "prepare",
        [],
        field_in,
        [
            jax.ShapeDtypeStruct((dirs, 2, cols, rows), jnp.bfloat16),
            f32(2, cols, rows),
            f32(dirs, rows),
            f32(depth, rows),
        ],
        [(pltpu.SMEM if n < 3 else pltpu.VMEM)(x.shape, x.dtype) for n, x in enumerate(field_in)]
        + [pltpu.SemaphoreType.DMA((12,))],
        HBM,
    )

    scratch = [pltpu.VMEM((cols, 2 * dirs), jnp.float32)]
    scale = 1.0 / (groups * STATIONS * STATIONS)
    plane = f32(2 * dirs, rows)
    fields = [f32(dirs, 2, cols, rows), f32(2, cols, rows), f32(8, rows)]
    z, r, power, grow, gcol, trow, tcol = call(
        functools.partial(first_kernel, ns=ns, nz=nz, span=span),
        "first",
        [],
        [part for parts in zip(row_parts, col_parts) for part in parts] + [mt, vt],
        fields + [plane, plane, plane, plane],
        scratch,
    )
    for step in range(ITERS):
        last = step == ITERS - 1
        if groups == 2:
            power = power + swap(power, ("chan", "srow"), ns + 1)
        else:
            power = lax.psum(power, "chan")
        if last:
            break
        half = 3 * dirs // 2
        same, other = call(
            functools.partial(terms_kernel, span=span),
            "terms",
            [],
            [z, r],
            [f32(half + 8, rows)] * 2,
            [pltpu.VMEM((3 * dirs, rows), jnp.float32)],
        )
        same = lax.dynamic_update_slice(same, power, (half, 0))
        other = lax.dynamic_update_slice(other, power, (half, 0))
        pair_sums, own = call(
            functools.partial(combine_kernel, nz=nz, span=span),
            "combine",
            [],
            [same] + [swap(same if n % 2 == 0 else other, "scol", n) for n in range(1, nz)],
            [f32(half, rows), f32(3 * depth + 8, rows)],
        )
        other_sums = swap(pair_sums, "scol", 1)
        pieces = [own] + [swap(own, "srow", n) for n in range(1, ns)]
        z, r, power, grow, gcol = call(
            functools.partial(sweep_kernel, ns=ns, span=span, scale=scale),
            "sweep",
            [],
            pieces + [pair_sums, other_sums, grow, gcol, trow, tcol, rho_rows, mt, vt],
            fields + [plane, plane],
            scratch,
        )

    parts = call(
        functools.partial(last_terms_kernel, span=span),
        "terms",
        [],
        [z, r],
        [f32(3 * depth + 8, rows)] * nz,
        [pltpu.VMEM((3 * dirs, rows), jnp.float32)],
    )
    parts = [lax.dynamic_update_slice(part, power, (3 * depth, 0)) for part in parts]
    power, mail = call(
        functools.partial(last_combine_kernel, nz=nz, span=span),
        "combine",
        [],
        [parts[0]] + [swap(parts[n], "scol", n) for n in range(1, nz)] + [grow, trow, dual_packed],
        [f32(8, rows), f32(9 * depth, rows)],
    )
    powers = [power] + [swap(power, "srow", n) for n in range(1, ns)]
    mails = [mail] + ([swap(mail, "chan", 1)] if pair else [])
    outs = call(
        functools.partial(
            final_kernel, ns=ns, scale=scale, pair=int(pair), span=span, scal=pair_scalars(pair)
        ),
        "final",
        [],
        powers + mails + [rho_packed],
        [f32(2, span, dirs)] * (3 if pair else 1),
    )
    outs = [x.transpose(2, 0, 1) for x in outs]
    if pair:
        g, coeffs, dual_new = outs
        return (g[None], coeffs[:, None], dual_new[None])
    g = outs[0]
    dual_own = dual[0]
    local = brow[None, :, None, None] * (g + dual_own)[:, None, :, :]
    coeffs = gram_solve(table, lax.psum(local, "chan"))
    dual_new = (
        dual_own + g - jnp.einsum("b,kbcp->kcp", brow, coeffs, precision=lax.Precision.HIGHEST)
    )
    return (g[None], coeffs, dual_new[None])


def solution(mesh):
    placed = (
        P("chan", None, "srow", "scol"),
        P("chan", None, None, "srow", "scol"),
        P("chan", "srow", "scol"),
        P("chan", None, None, ("srow", "scol")),
        P(None, None, None, ("srow", "scol")),
        P("chan", None, None, ("srow", "scol")),
        P(),
        P(),
    )
    return jax.shard_map(
        shards,
        mesh=mesh,
        in_specs=placed,
        out_specs=(
            P("chan", None, None, ("srow", "scol")),
            P(None, None, None, ("srow", "scol")),
            P("chan", None, None, ("srow", "scol")),
        ),
        check_vma=False,
    )
```

```python
import functools
import math

import jax
import jax.numpy as jnp
import numpy as np
from jax import lax
from jax.experimental import pallas as pl
from jax.experimental.pallas import tpu as pltpu
from jax.sharding import PartitionSpec as P

STATIONS = 512
TILE = 16
ITERS = 4

EPS = 1e-05
STEP = 0.5

VMEM_LIMIT = 24 << 20


def basis_table(groups, order):
    xval = (jnp.arange(groups, dtype=jnp.float32) + 0.5) / groups
    columns = [
        math.comb(order - 1, b) * xval**b * (1.0 - xval) ** (order - 1 - b) for b in range(order)
    ]
    return jnp.stack(columns, axis=1)


def pair_scalars(pair):
    if not pair:
        return None
    xval = (np.arange(2, dtype=np.float32) + np.float32(0.5)) / np.float32(2)
    column = xval**0 * (np.float32(1.0) - xval) ** 0
    return float(column[0]), float(column[1]), float(np.sqrt(np.sum(column * column)))


def gram_solve(table, rhs):
    gram = jnp.dot(table.T, table, precision=lax.Precision.HIGHEST)
    factor = jnp.linalg.cholesky(gram)
    order = rhs.shape[1]
    flat = jnp.moveaxis(rhs, 1, 0).reshape(order, -1)
    sol = jax.scipy.linalg.cho_solve((factor, True), flat)
    return jnp.moveaxis(sol.reshape((order, rhs.shape[0]) + rhs.shape[2:]), 0, 1)


def lane_block(shape, span):
    return lax.broadcasted_iota(jnp.int32, shape, 1) // span


def pack_plane(plane, block, span):
    dirs, lanes = plane.shape
    parts = lanes // span
    rows = dirs // parts
    where = lane_block((rows, lanes), span)
    packed = None
    for q in range(parts):
        piece = plane[q * rows : (q + 1) * rows]
        shift = lax.rem((q - block) * span + lanes, lanes)
        piece = pltpu.roll(piece, shift, 1)
        packed = piece if packed is None else jnp.where(where == q, piece, packed)
    return packed


def unpack_planes(pieces, blocks, span):
    rows, lanes = pieces[0].shape
    parts = lanes // span
    where = lane_block((rows, lanes), span)
    out = []
    for q in range(parts):
        plane = None
        for piece, block in zip(pieces, blocks):
            shift = lax.rem((block - q) * span + lanes, lanes)
            moved = pltpu.roll(piece, shift, 1)
            plane = moved if plane is None else jnp.where(where == block, moved, plane)
        out.append(plane)
    return jnp.concatenate(out, axis=0)


def solve(a, cr, ci, gr, gi, tr, ti, rho_eff):
    denom = a + rho_eff
    fresh_r = (cr + a * gr + rho_eff * tr) / denom
    fresh_i = (ci + a * gi + rho_eff * ti) / denom
    return gr + STEP * (fresh_r - gr), gi + STEP * (fresh_i - gi)


def fetch(sources, targets, sems):
    copies = [
        pltpu.make_async_copy(src, dst, sems.at[n])
        for n, (src, dst) in enumerate(zip(sources, targets))
    ]
    for copy in copies:
        copy.start()
    return copies


def pack_kernel(*refs, alone):
    brow_ref, refs = ([1.0], refs) if alone else (refs[0], refs[1:])
    start_ref, dual_out_ref = refs[3:5]
    gains_ref, consensus_ref, dual_ref = refs[5:8]
    for copy in fetch(refs[:3], refs[5:8], refs[8]):
        copy.wait()
    span, dirs = gains_ref.shape[1:]
    lanes = start_ref.shape[1]
    depth = dirs * span // lanes
    rows = []
    for p in range(2):
        target = brow_ref[0] * consensus_ref[0, p]
        for b in range(1, consensus_ref.shape[0]):
            target = target + brow_ref[b] * consensus_ref[b, p]
        rows.append(target - dual_ref[p])
    for fields, out_ref in (
        ([gains_ref[0], gains_ref[1]] + rows, start_ref),
        ([dual_ref[0], dual_ref[1]], dual_out_ref),
    ):
        plane = to_plane(fields, lanes)[:dirs]
        for n in range(len(fields)):
            out_ref[n * depth : (n + 1) * depth, :] = pack_plane(plane, n, span)


def to_plane(fields, lanes):
    x = jnp.concatenate(fields, axis=0)
    if x.shape[0] < lanes:
        x = jnp.concatenate([x, jnp.zeros((lanes - x.shape[0], x.shape[1]), x.dtype)], axis=0)
    if x.shape[1] < lanes:
        x = jnp.concatenate([x, jnp.zeros((lanes, lanes - x.shape[1]), x.dtype)], axis=1)
    return x.T


def prepare_kernel(*refs):
    ins = refs[:5]
    mt_ref, vt_ref, rho_rows_ref, rho_packed_ref = refs[5:9]
    rho_ref, cluster_ref, flags_ref, model_ref, vis_ref, sems = refs[9:]
    dirs, _, rows, cols = model_ref.shape
    pieces = 8
    size = dirs // pieces
    small = fetch(ins[:3] + ins[4:], [rho_ref, cluster_ref, flags_ref, vis_ref], sems)
    large = fetch(
        [ins[3].at[pl.ds(n * size, size)] for n in range(pieces)],
        [model_ref.at[pl.ds(n * size, size)] for n in range(pieces)],
        sems.at[pl.ds(4, pieces)],
    )
    for copy in small:
        copy.wait()
    where = lax.broadcasted_iota(jnp.int32, (1, rows), 1) // TILE
    bands = []
    for b in range(cols // TILE):
        band = jnp.zeros((1, rows), jnp.float32)
        for r in range(rows // TILE):
            band = jnp.where(where == r, flags_ref[r, b].astype(jnp.float32), band)
        bands.append(jnp.broadcast_to(band, (TILE, rows)))
    weight = jnp.concatenate(bands, axis=0)
    weight_bf16 = weight.astype(jnp.bfloat16)
    for p in range(2):
        vt_ref[p] = vis_ref[p].astype(jnp.float32).T * weight
    for k in range(dirs):
        rho_rows_ref[k : k + 1, :] = jnp.full((1, rows), rho_ref[cluster_ref[k]], jnp.float32)
    rho_packed_ref[...] = pack_plane(rho_rows_ref[...], 0, rows * rho_packed_ref.shape[0] // dirs)
    for n in range(pieces):
        large[n].wait()

        def turn(m, carry):
            for k in range(4):
                for p in range(2):
                    at = n * size + 4 * m + k
                    mt_ref[at, p] = model_ref[at, p].T * weight_bf16
            return carry

        lax.fori_loop(0, size // 4, turn, 0)


def residual(mt_ref, vt_ref, grow_ref, gcol_ref, z_ref, r_ref, p_ref, ct_ref):
    dirs, _, cols, rows = mt_ref.shape
    ct_ref[...] = gcol_ref[...].T
    chunk = 64

    def predict(n, carry):
        here = pl.ds(pl.multiple_of(n * chunk, chunk), chunk)
        ctile = ct_ref[here, :]
        acc_r = vt_ref[0, here, :]
        acc_i = vt_ref[1, here, :]
        for k in range(dirs):
            mr = mt_ref[k, 0, here, :].astype(jnp.float32)
            mi = mt_ref[k, 1, here, :].astype(jnp.float32)
            cr = jnp.broadcast_to(ctile[:, k : k + 1], (chunk, rows))
            ci = jnp.broadcast_to(ctile[:, dirs + k : dirs + k + 1], (chunk, rows))
            zr = mr * cr + mi * ci
            zi = mi * cr - mr * ci
            z_ref[k, 0, here, :] = zr
            z_ref[k, 1, here, :] = zi
            gr = grow_ref[k : k + 1, :]
            gi = grow_ref[dirs + k : dirs + k + 1, :]
            acc_r = acc_r - (gr * zr - gi * zi)
            acc_i = acc_i - (gr * zi + gi * zr)
        r_ref[0, here, :] = acc_r
        r_ref[1, here, :] = acc_i
        sq = acc_r * acc_r + acc_i * acc_i
        for c in range(0, chunk, 8):
            carry = carry + sq[c : c + 8]
        return carry

    p_ref[...] = lax.fori_loop(0, cols // chunk, predict, jnp.zeros(p_ref.shape, jnp.float32))


def normal_terms(z_ref, r_ref, out_ref):
    dirs, _, cols, rows = z_ref.shape
    group = 8
    part = 4

    def terms(n, carry):
        k0 = pl.multiple_of(n * group, group)
        blocks = [[], [], []]
        for half in range(0, group, part):
            sums = [[None] * 3 for _ in range(part)]
            for c in range(0, cols, 8):
                rr = r_ref[0, c : c + 8, :]
                ri = r_ref[1, c : c + 8, :]
                for kk in range(part):
                    zr = z_ref[k0 + half + kk, 0, c : c + 8, :]
                    zi = z_ref[k0 + half + kk, 1, c : c + 8, :]
                    new = (zr * zr + zi * zi, zr * rr + zi * ri, zr * ri - zi * rr)
                    for s in range(3):
                        old = sums[kk][s]
                        sums[kk][s] = new[s] if old is None else old + new[s]
            for s in range(3):
                blocks[s] += [jnp.sum(sums[kk][s], axis=0, keepdims=True) for kk in range(part)]
        for s in range(3):
            out_ref[pl.ds(s * dirs + k0, group), :] = jnp.concatenate(blocks[s], axis=0)
        return carry

    lax.fori_loop(0, dirs // group, terms, 0)


def own_parity(shape, span, j):
    return lax.rem(lane_block(shape, span), 2) == lax.rem(j, 2)


def terms_kernel(z_ref, r_ref, own_ref, other_ref, same_ref, all_ref, *, span):
    dirs, _, cols, rows = z_ref.shape
    half = dirs // 2
    normal_terms(z_ref, r_ref, all_ref)
    mine = own_parity((half, rows), span, lax.axis_index("scol"))
    for q in range(3):
        low = all_ref[q * dirs : q * dirs + half, :]
        high = pltpu.roll(all_ref[q * dirs + half : (q + 1) * dirs, :], span, 1)
        keep = jnp.where(mine, low, high)
        own_ref[q * half : (q + 1) * half, :] = keep
        same_ref[q * half : (q + 1) * half, :] = keep
        other_ref[q * half : (q + 1) * half, :] = jnp.where(mine, high, low)
    for ref in (own_ref, same_ref, other_ref):
        ref[3 * half :, :] = jnp.zeros((8, rows), jnp.float32)


def unfold(same, other, span, j):
    mine = own_parity(same.shape, span, j)
    low = jnp.where(mine, same, other)
    high = pltpu.roll(jnp.where(mine, other, same), same.shape[1] - span, 1)
    return jnp.concatenate([low, high], axis=0)


def pack_folded(piece, j, span):
    half, lanes = piece.shape
    parts = lanes // span
    depth = 2 * half // parts
    where = lane_block((depth, lanes), span)
    packed = None
    for q in range(parts):
        block = j + q * depth // half
        at = q * depth % half
        shift = lax.rem((q - block) * span + 2 * lanes, lanes)
        moved = pltpu.roll(piece[at : at + depth], shift, 1)
        packed = moved if packed is None else jnp.where(where == q, moved, packed)
    return packed


def last_terms_kernel(z_ref, r_ref, *refs, span):
    outs, all_ref = refs[:-1], refs[-1]
    dirs, _, cols, rows = z_ref.shape
    depth = dirs * span // rows
    normal_terms(z_ref, r_ref, all_ref)
    for n, out_ref in enumerate(outs):
        block = jnp.bitwise_xor(lax.axis_index("scol"), n)
        for q in range(3):
            plane = all_ref[q * dirs : (q + 1) * dirs, :]
            out_ref[q * depth : (q + 1) * depth, :] = pack_plane(plane, block, span)
        out_ref[3 * depth :, :] = jnp.zeros((8, rows), jnp.float32)


def first_kernel(*refs, ns, nz, span):
    cols_in = refs[:ns]
    rows_in = refs[ns : ns + nz]
    mt_ref, vt_ref = refs[nz + ns : nz + ns + 2]
    outs = refs[nz + ns + 2 : nz + ns + 5]
    grow_ref, gcol_ref, trow_ref, tcol_ref, ct_ref = refs[nz + ns + 5 :]
    dirs = mt_ref.shape[0]
    i, j = lax.axis_index("srow"), lax.axis_index("scol")
    depth = dirs * span // mt_ref.shape[3]
    for pieces, g_ref, t_ref, me in ((rows_in, grow_ref, trow_ref, j), (cols_in, gcol_ref, tcol_ref, i)):
        blocks = [jnp.bitwise_xor(me, n) for n in range(len(pieces))]
        for q in range(4):
            plane = unpack_planes([p[q * depth : (q + 1) * depth, :] for p in pieces], blocks, span)
            dst = g_ref if q < 2 else t_ref
            at = (q % 2) * dirs
            dst[at : at + dirs, :] = plane
    residual(mt_ref, vt_ref, grow_ref, gcol_ref, *outs, ct_ref)


def sweep_kernel(*refs, ns, span, scale):
    pieces = refs[:ns]
    same_ref, other_ref, growin_ref, gcolin_ref, trow_ref, tcol_ref = refs[ns : ns + 6]
    rho_ref, mt_ref, vt_ref = refs[ns + 6 : ns + 9]
    outs = refs[ns + 9 : ns + 12]
    grow_ref, gcol_ref, ct_ref = refs[ns + 12 :]
    dirs = mt_ref.shape[0]
    i = lax.axis_index("srow")
    depth = dirs * span // mt_ref.shape[3]
    power = pieces[0][3 * depth :, :]
    for p in pieces[1:]:
        power = power + p[3 * depth :, :]
    rho_eff = rho_ref[...] * (jnp.sum(power) * scale + EPS)
    re, im = slice(0, dirs), slice(dirs, 2 * dirs)
    half = dirs // 2
    a, cr, ci = [
        unfold(
            same_ref[q * half : (q + 1) * half, :],
            other_ref[q * half : (q + 1) * half, :],
            span,
            lax.axis_index("scol"),
        )
        for q in range(3)
    ]
    grow_ref[re, :], grow_ref[im, :] = solve(
        a, cr, ci, growin_ref[re, :], growin_ref[im, :], trow_ref[re, :], trow_ref[im, :], rho_eff
    )
    blocks = [jnp.bitwise_xor(i, n) for n in range(ns)]
    a, cr, ci = [
        unpack_planes([p[q * depth : (q + 1) * depth, :] for p in pieces], blocks, span)
        for q in range(3)
    ]
    gcol_ref[re, :], gcol_ref[im, :] = solve(
        a, cr, ci, gcolin_ref[re, :], gcolin_ref[im, :], tcol_ref[re, :], tcol_ref[im, :], rho_eff
    )
    residual(mt_ref, vt_ref, grow_ref, gcol_ref, *outs, ct_ref)


def combine_kernel(*refs, nz, span):
    parts = refs[:nz]
    pair_ref, own_ref = refs[nz:]
    half = pair_ref.shape[0] // 3
    depth = 2 * half * span // pair_ref.shape[1]
    total = parts[0][...]
    for p in parts[1:]:
        total = total + p[...]
    pair_ref[...] = total[: 3 * half]
    for q in range(3):
        piece = total[q * half : (q + 1) * half]
        own_ref[q * depth : (q + 1) * depth, :] = pack_folded(piece, lax.axis_index("scol"), span)
    own_ref[3 * depth :, :] = total[3 * half :]


def last_combine_kernel(*refs, nz, span):
    parts = refs[:nz]
    g_ref, t_ref, d_ref, power_ref, mail_ref = refs[nz:]
    dirs = g_ref.shape[0] // 2
    depth = dirs * span // g_ref.shape[1]
    j = lax.axis_index("scol")
    total = parts[0][...]
    for p in parts[1:]:
        total = total + p[...]
    mail_ref[: 3 * depth, :] = total[: 3 * depth]
    power_ref[...] = total[3 * depth :]
    for n, ref in enumerate((g_ref, t_ref)):
        for p in range(2):
            at = (3 + 2 * n + p) * depth
            plane = ref[p * dirs : (p + 1) * dirs, :]
            mail_ref[at : at + depth, :] = pack_plane(plane, j, span)
    mail_ref[7 * depth :, :] = d_ref[...]


def final_kernel(*refs, ns, scale, pair, span, scal):
    powers = refs[:ns]
    mails = refs[ns : ns + 1 + pair]
    rho_ref = refs[ns + 1 + pair]
    outs = refs[ns + 2 + pair :]
    depth, lanes = rho_ref.shape
    dirs = depth * lanes // span
    power = powers[0][...]
    for p in powers[1:]:
        power = power + p[...]
    rho_eff = rho_ref[...] * (jnp.sum(power) * scale + EPS)
    news = []
    for mail in mails:
        a, cr, ci, gr, gi, tr, ti = [mail[q * depth : (q + 1) * depth, :] for q in range(7)]
        news.append(solve(a, cr, ci, gr, gi, tr, ti, rho_eff))
    fields = list(news[0])
    if pair:
        duals = [[m[q * depth : (q + 1) * depth, :] for q in (7, 8)] for m in mails]
        first = lax.axis_index("chan") == 0
        coeffs, new_duals = [], []
        for p in range(2):
            own, other = [news[n][p] + duals[n][p] for n in range(2)]
            low, high = jnp.where(first, own, other), jnp.where(first, other, own)
            total = scal[0] * low + scal[1] * high
            coeffs.append(total / scal[2] / scal[2])
            brow = jnp.where(first, scal[0], scal[1])
            new_duals.append(duals[0][p] + news[0][p] - brow * coeffs[p])
        fields += coeffs + new_duals
    parts = lanes // span
    for at in range(0, len(fields), parts):
        group = fields[at : at + parts]
        plane = unpack_planes(group, list(range(len(group))), span)
        plane = jnp.concatenate([plane, jnp.zeros((lanes - dirs, lanes), jnp.float32)], axis=0)
        turned = plane.T
        for n in range(len(group)):
            out_ref = outs[(at + n) // 2]
            out_ref[(at + n) % 2] = turned[n * span : (n + 1) * span, :dirs]


SMEM = pl.BlockSpec(memory_space=pltpu.SMEM)
VMEM = pl.BlockSpec(memory_space=pltpu.VMEM)
HBM = pl.BlockSpec(memory_space=pltpu.HBM)


def f32(*shape):
    return jax.ShapeDtypeStruct(shape, jnp.float32)


def call(kernel, name, lead, args, outs, scratch=(), place=VMEM):
    if place is HBM:
        args = [pltpu.with_memory_space_constraint(x, pltpu.HBM) for x in args]
    return pl.pallas_call(
        kernel,
        in_specs=[SMEM] * len(lead) + [place] * len(args),
        out_specs=[VMEM] * len(outs),
        out_shape=outs,
        scratch_shapes=scratch,
        compiler_params=pltpu.CompilerParams(vmem_limit_bytes=VMEM_LIMIT),
        name=name,
    )(*lead, *args)


def swap(x, axis, n):
    size = lax.axis_size(axis)
    return lax.ppermute(x, axis, [(m, m ^ n) for m in range(size)])


def shards(vis, model, flags, gains, consensus, dual, rho, cluster):
    groups = lax.axis_size("chan")
    ns = lax.axis_size("srow")
    nz = lax.axis_size("scol")
    order = consensus.shape[1]
    dirs = gains.shape[1]
    span = gains.shape[3]
    rows, cols = vis.shape[2:]
    depth = dirs * span // rows
    f = lax.axis_index("chan")
    pair = groups == 2 and order == 1

    table = basis_table(groups, order)
    brow = lax.dynamic_index_in_dim(table, f, 0, keepdims=False)
    own_in = [
        gains[0].transpose(1, 2, 0),
        consensus.transpose(1, 2, 3, 0),
        dual[0].transpose(1, 2, 0),
    ]
    start, dual_packed = call(
        functools.partial(pack_kernel, alone=order == 1),
        "pack",
        [] if order == 1 else [brow],
        own_in,
        [f32(4 * depth, rows), f32(2 * depth, rows)],
        [pltpu.VMEM(x.shape, jnp.float32) for x in own_in] + [pltpu.SemaphoreType.DMA((3,))],
        HBM,
    )
    col_parts = [start] + [swap(start, "srow", n) for n in range(1, ns)]
    row_parts = [start] + [swap(start, "scol", n) for n in range(1, nz)]
    field_in = [rho, cluster, flags[0], model[0], vis[0]]
    mt, vt, rho_rows, rho_packed = call(
        prepare_kernel,
        "prepare",
        [],
        field_in,
        [
            jax.ShapeDtypeStruct((dirs, 2, cols, rows), jnp.bfloat16),
            f32(2, cols, rows),
            f32(dirs, rows),
            f32(depth, rows),
        ],
        [(pltpu.SMEM if n < 3 else pltpu.VMEM)(x.shape, x.dtype) for n, x in enumerate(field_in)]
        + [pltpu.SemaphoreType.DMA((12,))],
        HBM,
    )

    scratch = [pltpu.VMEM((cols, 2 * dirs), jnp.float32)]
    scale = 1.0 / (groups * STATIONS * STATIONS)
    plane = f32(2 * dirs, rows)
    fields = [f32(dirs, 2, cols, rows), f32(2, cols, rows), f32(8, rows)]
    z, r, power, grow, gcol, trow, tcol = call(
        functools.partial(first_kernel, ns=ns, nz=nz, span=span),
        "first",
        [],
        col_parts + row_parts + [mt, vt],
        fields + [plane, plane, plane, plane],
        scratch,
    )
    for step in range(ITERS):
        last = step == ITERS - 1
        if groups == 2:
            power = power + swap(power, ("chan", "srow"), ns + 1)
        else:
            power = lax.psum(power, "chan")
        if last:
            break
        half = 3 * dirs // 2
        own, other, same = call(
            functools.partial(terms_kernel, span=span),
            "terms",
            [],
            [z, r],
            [f32(half + 8, rows)] * 3,
            [pltpu.VMEM((3 * dirs, rows), jnp.float32)],
        )
        own, other, same = [
            lax.dynamic_update_slice(piece, power, (half, 0)) for piece in (own, other, same)
        ]
        pair_sums, own = call(
            functools.partial(combine_kernel, nz=nz, span=span),
            "combine",
            [],
            [own] + [swap(same if n % 2 == 0 else other, "scol", n) for n in (1, 3, 2)],
            [f32(half, rows), f32(3 * depth + 8, rows)],
        )
        other_sums = swap(pair_sums, "scol", 1)
        pieces = [own] + [swap(own, "srow", n) for n in range(1, ns)]
        z, r, power, grow, gcol = call(
            functools.partial(sweep_kernel, ns=ns, span=span, scale=scale),
            "sweep",
            [],
            pieces + [pair_sums, other_sums, grow, gcol, trow, tcol, rho_rows, mt, vt],
            fields + [plane, plane],
            scratch,
        )

    parts = call(
        functools.partial(last_terms_kernel, span=span),
        "terms",
        [],
        [z, r],
        [f32(3 * depth + 8, rows)] * nz,
        [pltpu.VMEM((3 * dirs, rows), jnp.float32)],
    )
    parts = [lax.dynamic_update_slice(part, power, (3 * depth, 0)) for part in parts]
    power, mail = call(
        functools.partial(last_combine_kernel, nz=nz, span=span),
        "combine",
        [],
        [parts[0]] + [swap(parts[n], "scol", n) for n in (3, 2, 1)] + [grow, trow, dual_packed],
        [f32(8, rows), f32(9 * depth, rows)],
    )
    powers = [power] + [swap(power, "srow", n) for n in range(1, ns)]
    mails = [mail] + ([swap(mail, "chan", 1)] if pair else [])
    outs = call(
        functools.partial(
            final_kernel, ns=ns, scale=scale, pair=int(pair), span=span, scal=pair_scalars(pair)
        ),
        "final",
        [],
        powers + mails + [rho_packed],
        [f32(2, span, dirs)] * (3 if pair else 1),
    )
    outs = [x.transpose(2, 0, 1) for x in outs]
    if pair:
        g, coeffs, dual_new = outs
        return (g[None], coeffs[:, None], dual_new[None])
    g = outs[0]
    dual_own = dual[0]
    local = brow[None, :, None, None] * (g + dual_own)[:, None, :, :]
    coeffs = gram_solve(table, lax.psum(local, "chan"))
    dual_new = (
        dual_own + g - jnp.einsum("b,kbcp->kcp", brow, coeffs, precision=lax.Precision.HIGHEST)
    )
    return (g[None], coeffs, dual_new[None])


def solution(mesh):
    placed = (
        P("chan", None, "srow", "scol"),
        P("chan", None, None, "srow", "scol"),
        P("chan", "srow", "scol"),
        P("chan", None, None, ("srow", "scol")),
        P(None, None, None, ("srow", "scol")),
        P("chan", None, None, ("srow", "scol")),
        P(),
        P(),
    )
    return jax.shard_map(
        shards,
        mesh=mesh,
        in_specs=placed,
        out_specs=(
            P("chan", None, None, ("srow", "scol")),
            P(None, None, None, ("srow", "scol")),
            P("chan", None, None, ("srow", "scol")),
        ),
        check_vma=False,
    )
```

```python
import functools
import math

import jax
import jax.numpy as jnp
import numpy as np
from jax import lax
from jax.experimental import pallas as pl
from jax.experimental.pallas import tpu as pltpu
from jax.sharding import PartitionSpec as P

STATIONS = 512
TILE = 16
ITERS = 4

EPS = 1e-05
STEP = 0.5

VMEM_LIMIT = 24 << 20


def basis_table(groups, order):
    xval = (jnp.arange(groups, dtype=jnp.float32) + 0.5) / groups
    columns = [
        math.comb(order - 1, b) * xval**b * (1.0 - xval) ** (order - 1 - b) for b in range(order)
    ]
    return jnp.stack(columns, axis=1)


def pair_scalars(pair):
    if not pair:
        return None
    xval = (np.arange(2, dtype=np.float32) + np.float32(0.5)) / np.float32(2)
    column = xval**0 * (np.float32(1.0) - xval) ** 0
    return float(column[0]), float(column[1]), float(np.sqrt(np.sum(column * column)))


def gram_solve(table, rhs):
    gram = jnp.dot(table.T, table, precision=lax.Precision.HIGHEST)
    factor = jnp.linalg.cholesky(gram)
    order = rhs.shape[1]
    flat = jnp.moveaxis(rhs, 1, 0).reshape(order, -1)
    sol = jax.scipy.linalg.cho_solve((factor, True), flat)
    return jnp.moveaxis(sol.reshape((order, rhs.shape[0]) + rhs.shape[2:]), 0, 1)


def lane_block(shape, span):
    return lax.broadcasted_iota(jnp.int32, shape, 1) // span


def pack_plane(plane, block, span):
    dirs, lanes = plane.shape
    parts = lanes // span
    rows = dirs // parts
    where = lane_block((rows, lanes), span)
    packed = None
    for q in range(parts):
        piece = plane[q * rows : (q + 1) * rows]
        shift = lax.rem((q - block) * span + lanes, lanes)
        piece = pltpu.roll(piece, shift, 1)
        packed = piece if packed is None else jnp.where(where == q, piece, packed)
    return packed


def unpack_planes(pieces, blocks, span):
    rows, lanes = pieces[0].shape
    parts = lanes // span
    where = lane_block((rows, lanes), span)
    out = []
    for q in range(parts):
        plane = None
        for piece, block in zip(pieces, blocks):
            shift = lax.rem((block - q) * span + lanes, lanes)
            moved = pltpu.roll(piece, shift, 1)
            plane = moved if plane is None else jnp.where(where == block, moved, plane)
        out.append(plane)
    return jnp.concatenate(out, axis=0)


def solve(a, cr, ci, gr, gi, tr, ti, rho_eff):
    denom = a + rho_eff
    fresh_r = (cr + a * gr + rho_eff * tr) / denom
    fresh_i = (ci + a * gi + rho_eff * ti) / denom
    return gr + STEP * (fresh_r - gr), gi + STEP * (fresh_i - gi)


def fetch(sources, targets, sems):
    copies = [
        pltpu.make_async_copy(src, dst, sems.at[n])
        for n, (src, dst) in enumerate(zip(sources, targets))
    ]
    for copy in copies:
        copy.start()
    return copies


def pack_kernel(*refs, alone):
    brow_ref, refs = ([1.0], refs) if alone else (refs[0], refs[1:])
    start_ref, dual_out_ref = refs[3:5]
    gains_ref, consensus_ref, dual_ref = refs[5:8]
    for copy in fetch(refs[:3], refs[5:8], refs[8]):
        copy.wait()
    span, dirs = gains_ref.shape[1:]
    lanes = start_ref.shape[1]
    depth = dirs * span // lanes
    rows = []
    for p in range(2):
        target = brow_ref[0] * consensus_ref[0, p]
        for b in range(1, consensus_ref.shape[0]):
            target = target + brow_ref[b] * consensus_ref[b, p]
        rows.append(target - dual_ref[p])
    for fields, out_ref in (
        ([gains_ref[0], gains_ref[1]] + rows, start_ref),
        ([dual_ref[0], dual_ref[1]], dual_out_ref),
    ):
        plane = to_plane(fields, lanes)[:dirs]
        for n in range(len(fields)):
            out_ref[n * depth : (n + 1) * depth, :] = pack_plane(plane, n, span)


def to_plane(fields, lanes):
    x = jnp.concatenate(fields, axis=0)
    if x.shape[0] < lanes:
        x = jnp.concatenate([x, jnp.zeros((lanes - x.shape[0], x.shape[1]), x.dtype)], axis=0)
    if x.shape[1] < lanes:
        x = jnp.concatenate([x, jnp.zeros((lanes, lanes - x.shape[1]), x.dtype)], axis=1)
    return x.T


def prepare_kernel(*refs):
    ins = refs[:5]
    mt_ref, vt_ref, rho_rows_ref, rho_packed_ref = refs[5:9]
    rho_ref, cluster_ref, flags_ref, model_ref, vis_ref, sems = refs[9:]
    dirs, _, rows, cols = model_ref.shape
    pieces = 8
    size = dirs // pieces
    small = fetch(ins[:3] + ins[4:], [rho_ref, cluster_ref, flags_ref, vis_ref], sems)
    large = fetch(
        [ins[3].at[pl.ds(n * size, size)] for n in range(pieces)],
        [model_ref.at[pl.ds(n * size, size)] for n in range(pieces)],
        sems.at[pl.ds(4, pieces)],
    )
    for copy in small:
        copy.wait()
    where = lax.broadcasted_iota(jnp.int32, (1, rows), 1) // TILE
    bands = []
    for b in range(cols // TILE):
        band = jnp.zeros((1, rows), jnp.float32)
        for r in range(rows // TILE):
            band = jnp.where(where == r, flags_ref[r, b].astype(jnp.float32), band)
        bands.append(jnp.broadcast_to(band, (TILE, rows)))
    weight = jnp.concatenate(bands, axis=0)
    weight_bf16 = weight.astype(jnp.bfloat16)
    square = (cols, cols)
    eye = lax.broadcasted_iota(jnp.int32, square, 0) == lax.broadcasted_iota(jnp.int32, square, 1)
    eye = eye.astype(jnp.float32).astype(jnp.bfloat16)
    for p in range(2):
        vt_ref[p] = vis_ref[p].astype(jnp.float32).T * weight
    for k in range(dirs):
        rho_rows_ref[k : k + 1, :] = jnp.full((1, rows), rho_ref[cluster_ref[k]], jnp.float32)
    rho_packed_ref[...] = pack_plane(rho_rows_ref[...], 0, rows * rho_packed_ref.shape[0] // dirs)
    for n in range(pieces):
        large[n].wait()

        def turn(m, carry):
            for k in range(4):
                for p in range(2):
                    at = n * size + 4 * m + k
                    if k == 0:
                        turned = lax.dot_general(
                            eye,
                            model_ref[at, p],
                            (((1,), (1,)), ((), ())),
                            preferred_element_type=jnp.float32,
                        ).astype(jnp.bfloat16)
                    else:
                        turned = model_ref[at, p].T
                    mt_ref[at, p] = turned * weight_bf16
            return carry

        lax.fori_loop(0, size // 4, turn, 0)


def residual(mt_ref, vt_ref, grow_ref, gcol_ref, z_ref, r_ref, p_ref, ct_ref):
    dirs, _, cols, rows = mt_ref.shape
    ct_ref[...] = gcol_ref[...].T
    chunk = 64

    def predict(n, carry):
        here = pl.ds(pl.multiple_of(n * chunk, chunk), chunk)
        ctile = ct_ref[here, :]
        acc_r = vt_ref[0, here, :]
        acc_i = vt_ref[1, here, :]
        for k in range(dirs):
            mr = mt_ref[k, 0, here, :].astype(jnp.float32)
            mi = mt_ref[k, 1, here, :].astype(jnp.float32)
            cr = jnp.broadcast_to(ctile[:, k : k + 1], (chunk, rows))
            ci = jnp.broadcast_to(ctile[:, dirs + k : dirs + k + 1], (chunk, rows))
            zr = mr * cr + mi * ci
            zi = mi * cr - mr * ci
            z_ref[k, 0, here, :] = zr
            z_ref[k, 1, here, :] = zi
            gr = grow_ref[k : k + 1, :]
            gi = grow_ref[dirs + k : dirs + k + 1, :]
            acc_r = acc_r - (gr * zr - gi * zi)
            acc_i = acc_i - (gr * zi + gi * zr)
        r_ref[0, here, :] = acc_r
        r_ref[1, here, :] = acc_i
        sq = acc_r * acc_r + acc_i * acc_i
        for c in range(0, chunk, 8):
            carry = carry + sq[c : c + 8]
        return carry

    p_ref[...] = lax.fori_loop(0, cols // chunk, predict, jnp.zeros(p_ref.shape, jnp.float32))


def normal_terms(z_ref, r_ref, out_ref):
    dirs, _, cols, rows = z_ref.shape
    group = 8
    part = 4

    def terms(n, carry):
        k0 = pl.multiple_of(n * group, group)
        blocks = [[], [], []]
        for half in range(0, group, part):
            sums = [[None] * 3 for _ in range(part)]
            for c in range(0, cols, 8):
                rr = r_ref[0, c : c + 8, :]
                ri = r_ref[1, c : c + 8, :]
                for kk in range(part):
                    zr = z_ref[k0 + half + kk, 0, c : c + 8, :]
                    zi = z_ref[k0 + half + kk, 1, c : c + 8, :]
                    new = (zr * zr + zi * zi, zr * rr + zi * ri, zr * ri - zi * rr)
                    for s in range(3):
                        old = sums[kk][s]
                        sums[kk][s] = new[s] if old is None else old + new[s]
            for s in range(3):
                blocks[s] += [jnp.sum(sums[kk][s], axis=0, keepdims=True) for kk in range(part)]
        for s in range(3):
            out_ref[pl.ds(s * dirs + k0, group), :] = jnp.concatenate(blocks[s], axis=0)
        return carry

    lax.fori_loop(0, dirs // group, terms, 0)


def own_parity(shape, span, j):
    return lax.rem(lane_block(shape, span), 2) == lax.rem(j, 2)


def terms_kernel(z_ref, r_ref, same_ref, other_ref, all_ref, *, span):
    dirs, _, cols, rows = z_ref.shape
    half = dirs // 2
    normal_terms(z_ref, r_ref, all_ref)
    mine = own_parity((half, rows), span, lax.axis_index("scol"))
    for q in range(3):
        low = all_ref[q * dirs : q * dirs + half, :]
        high = pltpu.roll(all_ref[q * dirs + half : (q + 1) * dirs, :], span, 1)
        same_ref[q * half : (q + 1) * half, :] = jnp.where(mine, low, high)
        other_ref[q * half : (q + 1) * half, :] = jnp.where(mine, high, low)
    for ref in (same_ref, other_ref):
        ref[3 * half :, :] = jnp.zeros((8, rows), jnp.float32)


def unfold(same, other, span, j):
    mine = own_parity(same.shape, span, j)
    low = jnp.where(mine, same, other)
    high = pltpu.roll(jnp.where(mine, other, same), same.shape[1] - span, 1)
    return jnp.concatenate([low, high], axis=0)


def pack_folded(piece, j, span):
    half, lanes = piece.shape
    parts = lanes // span
    depth = 2 * half // parts
    where = lane_block((depth, lanes), span)
    packed = None
    for q in range(parts):
        block = j + q * depth // half
        at = q * depth % half
        shift = lax.rem((q - block) * span + 2 * lanes, lanes)
        moved = pltpu.roll(piece[at : at + depth], shift, 1)
        packed = moved if packed is None else jnp.where(where == q, moved, packed)
    return packed


def last_terms_kernel(z_ref, r_ref, *refs, span):
    outs, all_ref = refs[:-1], refs[-1]
    dirs, _, cols, rows = z_ref.shape
    depth = dirs * span // rows
    normal_terms(z_ref, r_ref, all_ref)
    for n, out_ref in enumerate(outs):
        block = jnp.bitwise_xor(lax.axis_index("scol"), n)
        for q in range(3):
            plane = all_ref[q * dirs : (q + 1) * dirs, :]
            out_ref[q * depth : (q + 1) * depth, :] = pack_plane(plane, block, span)
        out_ref[3 * depth :, :] = jnp.zeros((8, rows), jnp.float32)


def first_kernel(*refs, ns, nz, span):
    cols_in = refs[:ns]
    rows_in = refs[ns : ns + nz]
    mt_ref, vt_ref = refs[nz + ns : nz + ns + 2]
    outs = refs[nz + ns + 2 : nz + ns + 5]
    grow_ref, gcol_ref, trow_ref, tcol_ref, ct_ref = refs[nz + ns + 5 :]
    dirs = mt_ref.shape[0]
    i, j = lax.axis_index("srow"), lax.axis_index("scol")
    depth = dirs * span // mt_ref.shape[3]
    for pieces, g_ref, t_ref, me in ((rows_in, grow_ref, trow_ref, j), (cols_in, gcol_ref, tcol_ref, i)):
        blocks = [jnp.bitwise_xor(me, n) for n in range(len(pieces))]
        for q in range(4):
            plane = unpack_planes([p[q * depth : (q + 1) * depth, :] for p in pieces], blocks, span)
            dst = g_ref if q < 2 else t_ref
            at = (q % 2) * dirs
            dst[at : at + dirs, :] = plane
    residual(mt_ref, vt_ref, grow_ref, gcol_ref, *outs, ct_ref)


def sweep_kernel(*refs, ns, span, scale):
    pieces = refs[:ns]
    same_ref, other_ref, growin_ref, gcolin_ref, trow_ref, tcol_ref = refs[ns : ns + 6]
    rho_ref, mt_ref, vt_ref = refs[ns + 6 : ns + 9]
    outs = refs[ns + 9 : ns + 12]
    grow_ref, gcol_ref, ct_ref = refs[ns + 12 :]
    dirs = mt_ref.shape[0]
    i = lax.axis_index("srow")
    depth = dirs * span // mt_ref.shape[3]
    power = pieces[0][3 * depth :, :]
    for p in pieces[1:]:
        power = power + p[3 * depth :, :]
    rho_eff = rho_ref[...] * (jnp.sum(power) * scale + EPS)
    re, im = slice(0, dirs), slice(dirs, 2 * dirs)
    half = dirs // 2
    a, cr, ci = [
        unfold(
            same_ref[q * half : (q + 1) * half, :],
            other_ref[q * half : (q + 1) * half, :],
            span,
            lax.axis_index("scol"),
        )
        for q in range(3)
    ]
    grow_ref[re, :], grow_ref[im, :] = solve(
        a, cr, ci, growin_ref[re, :], growin_ref[im, :], trow_ref[re, :], trow_ref[im, :], rho_eff
    )
    blocks = [jnp.bitwise_xor(i, n) for n in range(ns)]
    a, cr, ci = [
        unpack_planes([p[q * depth : (q + 1) * depth, :] for p in pieces], blocks, span)
        for q in range(3)
    ]
    gcol_ref[re, :], gcol_ref[im, :] = solve(
        a, cr, ci, gcolin_ref[re, :], gcolin_ref[im, :], tcol_ref[re, :], tcol_ref[im, :], rho_eff
    )
    residual(mt_ref, vt_ref, grow_ref, gcol_ref, *outs, ct_ref)


def combine_kernel(*refs, nz, span):
    parts = refs[:nz]
    pair_ref, own_ref = refs[nz:]
    half = pair_ref.shape[0] // 3
    depth = 2 * half * span // pair_ref.shape[1]
    total = parts[0][...]
    for p in parts[1:]:
        total = total + p[...]
    pair_ref[...] = total[: 3 * half]
    for q in range(3):
        piece = total[q * half : (q + 1) * half]
        own_ref[q * depth : (q + 1) * depth, :] = pack_folded(piece, lax.axis_index("scol"), span)
    own_ref[3 * depth :, :] = total[3 * half :]


def last_combine_kernel(*refs, nz, span):
    parts = refs[:nz]
    g_ref, t_ref, d_ref, power_ref, mail_ref = refs[nz:]
    dirs = g_ref.shape[0] // 2
    depth = dirs * span // g_ref.shape[1]
    j = lax.axis_index("scol")
    total = parts[0][...]
    for p in parts[1:]:
        total = total + p[...]
    mail_ref[: 3 * depth, :] = total[: 3 * depth]
    power_ref[...] = total[3 * depth :]
    for n, ref in enumerate((g_ref, t_ref)):
        for p in range(2):
            at = (3 + 2 * n + p) * depth
            plane = ref[p * dirs : (p + 1) * dirs, :]
            mail_ref[at : at + depth, :] = pack_plane(plane, j, span)
    mail_ref[7 * depth :, :] = d_ref[...]


def final_kernel(*refs, ns, scale, pair, span, scal):
    powers = refs[:ns]
    mails = refs[ns : ns + 1 + pair]
    rho_ref = refs[ns + 1 + pair]
    outs = refs[ns + 2 + pair :]
    depth, lanes = rho_ref.shape
    dirs = depth * lanes // span
    power = powers[0][...]
    for p in powers[1:]:
        power = power + p[...]
    rho_eff = rho_ref[...] * (jnp.sum(power) * scale + EPS)
    news = []
    for mail in mails:
        a, cr, ci, gr, gi, tr, ti = [mail[q * depth : (q + 1) * depth, :] for q in range(7)]
        news.append(solve(a, cr, ci, gr, gi, tr, ti, rho_eff))
    fields = list(news[0])
    if pair:
        duals = [[m[q * depth : (q + 1) * depth, :] for q in (7, 8)] for m in mails]
        first = lax.axis_index("chan") == 0
        coeffs, new_duals = [], []
        for p in range(2):
            own, other = [news[n][p] + duals[n][p] for n in range(2)]
            low, high = jnp.where(first, own, other), jnp.where(first, other, own)
            total = scal[0] * low + scal[1] * high
            coeffs.append(total / scal[2] / scal[2])
            brow = jnp.where(first, scal[0], scal[1])
            new_duals.append(duals[0][p] + news[0][p] - brow * coeffs[p])
        fields += coeffs + new_duals
    parts = lanes // span
    for at in range(0, len(fields), parts):
        group = fields[at : at + parts]
        plane = unpack_planes(group, list(range(len(group))), span)
        plane = jnp.concatenate([plane, jnp.zeros((lanes - dirs, lanes), jnp.float32)], axis=0)
        turned = plane.T
        for n in range(len(group)):
            out_ref = outs[(at + n) // 2]
            out_ref[(at + n) % 2] = turned[n * span : (n + 1) * span, :dirs]


SMEM = pl.BlockSpec(memory_space=pltpu.SMEM)
VMEM = pl.BlockSpec(memory_space=pltpu.VMEM)
HBM = pl.BlockSpec(memory_space=pltpu.HBM)


def f32(*shape):
    return jax.ShapeDtypeStruct(shape, jnp.float32)


def call(kernel, name, lead, args, outs, scratch=(), place=VMEM):
    if place is HBM:
        args = [pltpu.with_memory_space_constraint(x, pltpu.HBM) for x in args]
    return pl.pallas_call(
        kernel,
        in_specs=[SMEM] * len(lead) + [place] * len(args),
        out_specs=[VMEM] * len(outs),
        out_shape=outs,
        scratch_shapes=scratch,
        compiler_params=pltpu.CompilerParams(vmem_limit_bytes=VMEM_LIMIT),
        name=name,
    )(*lead, *args)


def swap(x, axis, n):
    size = lax.axis_size(axis)
    return lax.ppermute(x, axis, [(m, m ^ n) for m in range(size)])


def shards(vis, model, flags, gains, consensus, dual, rho, cluster):
    groups = lax.axis_size("chan")
    ns = lax.axis_size("srow")
    nz = lax.axis_size("scol")
    order = consensus.shape[1]
    dirs = gains.shape[1]
    span = gains.shape[3]
    rows, cols = vis.shape[2:]
    depth = dirs * span // rows
    f = lax.axis_index("chan")
    pair = groups == 2 and order == 1

    table = basis_table(groups, order)
    brow = lax.dynamic_index_in_dim(table, f, 0, keepdims=False)
    own_in = [
        gains[0].transpose(1, 2, 0),
        consensus.transpose(1, 2, 3, 0),
        dual[0].transpose(1, 2, 0),
    ]
    start, dual_packed = call(
        functools.partial(pack_kernel, alone=order == 1),
        "pack",
        [] if order == 1 else [brow],
        own_in,
        [f32(4 * depth, rows), f32(2 * depth, rows)],
        [pltpu.VMEM(x.shape, jnp.float32) for x in own_in] + [pltpu.SemaphoreType.DMA((3,))],
        HBM,
    )
    col_parts = [start] + [swap(start, "srow", n) for n in range(1, ns)]
    row_parts = [start] + [swap(start, "scol", n) for n in range(1, nz)]
    field_in = [rho, cluster, flags[0], model[0], vis[0]]
    mt, vt, rho_rows, rho_packed = call(
        prepare_kernel,
        "prepare",
        [],
        field_in,
        [
            jax.ShapeDtypeStruct((dirs, 2, cols, rows), jnp.bfloat16),
            f32(2, cols, rows),
            f32(dirs, rows),
            f32(depth, rows),
        ],
        [(pltpu.SMEM if n < 3 else pltpu.VMEM)(x.shape, x.dtype) for n, x in enumerate(field_in)]
        + [pltpu.SemaphoreType.DMA((12,))],
        HBM,
    )

    scratch = [pltpu.VMEM((cols, 2 * dirs), jnp.float32)]
    scale = 1.0 / (groups * STATIONS * STATIONS)
    plane = f32(2 * dirs, rows)
    fields = [f32(dirs, 2, cols, rows), f32(2, cols, rows), f32(8, rows)]
    z, r, power, grow, gcol, trow, tcol = call(
        functools.partial(first_kernel, ns=ns, nz=nz, span=span),
        "first",
        [],
        col_parts + row_parts + [mt, vt],
        fields + [plane, plane, plane, plane],
        scratch,
    )
    for step in range(ITERS):
        last = step == ITERS - 1
        if groups == 2:
            power = power + swap(power, ("chan", "srow"), ns + 1)
        else:
            power = lax.psum(power, "chan")
        if last:
            break
        half = 3 * dirs // 2
        same, other = call(
            functools.partial(terms_kernel, span=span),
            "terms",
            [],
            [z, r],
            [f32(half + 8, rows)] * 2,
            [pltpu.VMEM((3 * dirs, rows), jnp.float32)],
        )
        same = lax.dynamic_update_slice(same, power, (half, 0))
        other = lax.dynamic_update_slice(other, power, (half, 0))
        pair_sums, own = call(
            functools.partial(combine_kernel, nz=nz, span=span),
            "combine",
            [],
            [same] + [swap(same if n % 2 == 0 else other, "scol", n) for n in range(1, nz)],
            [f32(half, rows), f32(3 * depth + 8, rows)],
        )
        other_sums = swap(pair_sums, "scol", 1)
        pieces = [own] + [swap(own, "srow", n) for n in range(1, ns)]
        z, r, power, grow, gcol = call(
            functools.partial(sweep_kernel, ns=ns, span=span, scale=scale),
            "sweep",
            [],
            pieces + [pair_sums, other_sums, grow, gcol, trow, tcol, rho_rows, mt, vt],
            fields + [plane, plane],
            scratch,
        )

    parts = call(
        functools.partial(last_terms_kernel, span=span),
        "terms",
        [],
        [z, r],
        [f32(3 * depth + 8, rows)] * nz,
        [pltpu.VMEM((3 * dirs, rows), jnp.float32)],
    )
    parts = [lax.dynamic_update_slice(part, power, (3 * depth, 0)) for part in parts]
    power, mail = call(
        functools.partial(last_combine_kernel, nz=nz, span=span),
        "combine",
        [],
        [parts[0]] + [swap(parts[n], "scol", n) for n in range(1, nz)] + [grow, trow, dual_packed],
        [f32(8, rows), f32(9 * depth, rows)],
    )
    powers = [power] + [swap(power, "srow", n) for n in range(1, ns)]
    mails = [mail] + ([swap(mail, "chan", 1)] if pair else [])
    outs = call(
        functools.partial(
            final_kernel, ns=ns, scale=scale, pair=int(pair), span=span, scal=pair_scalars(pair)
        ),
        "final",
        [],
        powers + mails + [rho_packed],
        [f32(2, span, dirs)] * (3 if pair else 1),
    )
    outs = [x.transpose(2, 0, 1) for x in outs]
    if pair:
        g, coeffs, dual_new = outs
        return (g[None], coeffs[:, None], dual_new[None])
    g = outs[0]
    dual_own = dual[0]
    local = brow[None, :, None, None] * (g + dual_own)[:, None, :, :]
    coeffs = gram_solve(table, lax.psum(local, "chan"))
    dual_new = (
        dual_own + g - jnp.einsum("b,kbcp->kcp", brow, coeffs, precision=lax.Precision.HIGHEST)
    )
    return (g[None], coeffs, dual_new[None])


def solution(mesh):
    placed = (
        P("chan", None, "srow", "scol"),
        P("chan", None, None, "srow", "scol"),
        P("chan", "srow", "scol"),
        P("chan", None, None, ("srow", "scol")),
        P(None, None, None, ("srow", "scol")),
        P("chan", None, None, ("srow", "scol")),
        P(),
        P(),
    )
    return jax.shard_map(
        shards,
        mesh=mesh,
        in_specs=placed,
        out_specs=(
            P("chan", None, None, ("srow", "scol")),
            P(None, None, None, ("srow", "scol")),
            P("chan", None, None, ("srow", "scol")),
        ),
        check_vma=False,
    )
```

```python
import functools
import math

import jax
import jax.numpy as jnp
import numpy as np
from jax import lax
from jax.experimental import pallas as pl
from jax.experimental.pallas import tpu as pltpu
from jax.sharding import PartitionSpec as P

STATIONS = 512
TILE = 16
ITERS = 4

EPS = 1e-05
STEP = 0.5

VMEM_LIMIT = 24 << 20


def basis_table(groups, order):
    xval = (jnp.arange(groups, dtype=jnp.float32) + 0.5) / groups
    columns = [
        math.comb(order - 1, b) * xval**b * (1.0 - xval) ** (order - 1 - b) for b in range(order)
    ]
    return jnp.stack(columns, axis=1)


def pair_scalars(pair):
    if not pair:
        return None
    xval = (np.arange(2, dtype=np.float32) + np.float32(0.5)) / np.float32(2)
    column = xval**0 * (np.float32(1.0) - xval) ** 0
    return float(column[0]), float(column[1]), float(np.sqrt(np.sum(column * column)))


def gram_solve(table, rhs):
    gram = jnp.dot(table.T, table, precision=lax.Precision.HIGHEST)
    factor = jnp.linalg.cholesky(gram)
    order = rhs.shape[1]
    flat = jnp.moveaxis(rhs, 1, 0).reshape(order, -1)
    sol = jax.scipy.linalg.cho_solve((factor, True), flat)
    return jnp.moveaxis(sol.reshape((order, rhs.shape[0]) + rhs.shape[2:]), 0, 1)


def lane_block(shape, span):
    return lax.broadcasted_iota(jnp.int32, shape, 1) // span


def pack_plane(plane, block, span):
    dirs, lanes = plane.shape
    parts = lanes // span
    rows = dirs // parts
    where = lane_block((rows, lanes), span)
    packed = None
    for q in range(parts):
        piece = plane[q * rows : (q + 1) * rows]
        shift = lax.rem((q - block) * span + lanes, lanes)
        piece = pltpu.roll(piece, shift, 1)
        packed = piece if packed is None else jnp.where(where == q, piece, packed)
    return packed


def unpack_planes(pieces, blocks, span):
    rows, lanes = pieces[0].shape
    parts = lanes // span
    where = lane_block((rows, lanes), span)
    out = []
    for q in range(parts):
        plane = None
        for piece, block in zip(pieces, blocks):
            shift = lax.rem((block - q) * span + lanes, lanes)
            moved = pltpu.roll(piece, shift, 1)
            plane = moved if plane is None else jnp.where(where == block, moved, plane)
        out.append(plane)
    return jnp.concatenate(out, axis=0)


def solve(a, cr, ci, gr, gi, tr, ti, rho_eff):
    denom = a + rho_eff
    fresh_r = (cr + a * gr + rho_eff * tr) / denom
    fresh_i = (ci + a * gi + rho_eff * ti) / denom
    return gr + STEP * (fresh_r - gr), gi + STEP * (fresh_i - gi)


def fetch(sources, targets, sems):
    copies = [
        pltpu.make_async_copy(src, dst, sems.at[n])
        for n, (src, dst) in enumerate(zip(sources, targets))
    ]
    for copy in copies:
        copy.start()
    return copies


def pack_kernel(*refs, alone):
    brow_ref, refs = ([1.0], refs) if alone else (refs[0], refs[1:])
    start_ref, dual_out_ref = refs[3:5]
    gains_ref, consensus_ref, dual_ref = refs[5:8]
    for copy in fetch(refs[:3], refs[5:8], refs[8]):
        copy.wait()
    span, dirs = gains_ref.shape[1:]
    lanes = start_ref.shape[1]
    depth = dirs * span // lanes
    rows = []
    for p in range(2):
        target = brow_ref[0] * consensus_ref[0, p]
        for b in range(1, consensus_ref.shape[0]):
            target = target + brow_ref[b] * consensus_ref[b, p]
        rows.append(target - dual_ref[p])
    for fields, out_ref in (
        ([gains_ref[0], gains_ref[1]] + rows, start_ref),
        ([dual_ref[0], dual_ref[1]], dual_out_ref),
    ):
        plane = to_plane(fields, lanes)[:dirs]
        for n in range(len(fields)):
            out_ref[n * depth : (n + 1) * depth, :] = pack_plane(plane, n, span)


def to_plane(fields, lanes):
    x = jnp.concatenate(fields, axis=0)
    if x.shape[0] < lanes:
        x = jnp.concatenate([x, jnp.zeros((lanes - x.shape[0], x.shape[1]), x.dtype)], axis=0)
    if x.shape[1] < lanes:
        x = jnp.concatenate([x, jnp.zeros((lanes, lanes - x.shape[1]), x.dtype)], axis=1)
    return x.T


def prepare_kernel(*refs):
    ins = refs[:5]
    mt_ref, vt_ref, rho_rows_ref, rho_packed_ref = refs[5:9]
    rho_ref, cluster_ref, flags_ref, model_ref, vis_ref, sems = refs[9:]
    dirs, _, rows, cols = model_ref.shape
    pieces = 8
    size = dirs // pieces
    small = fetch(ins[:3] + ins[4:], [rho_ref, cluster_ref, flags_ref, vis_ref], sems)
    large = fetch(
        [ins[3].at[pl.ds(n * size, size)] for n in range(pieces)],
        [model_ref.at[pl.ds(n * size, size)] for n in range(pieces)],
        sems.at[pl.ds(4, pieces)],
    )
    for copy in small:
        copy.wait()
    where = lax.broadcasted_iota(jnp.int32, (1, rows), 1) // TILE
    bands = []
    for b in range(cols // TILE):
        band = jnp.zeros((1, rows), jnp.float32)
        for r in range(rows // TILE):
            band = jnp.where(where == r, flags_ref[r, b].astype(jnp.float32), band)
        bands.append(jnp.broadcast_to(band, (TILE, rows)))
    weight = jnp.concatenate(bands, axis=0)
    weight_bf16 = weight.astype(jnp.bfloat16)
    for p in range(2):
        vt_ref[p] = vis_ref[p].astype(jnp.float32).T * weight
    for k in range(dirs):
        rho_rows_ref[k : k + 1, :] = jnp.full((1, rows), rho_ref[cluster_ref[k]], jnp.float32)
    rho_packed_ref[...] = pack_plane(rho_rows_ref[...], 0, rows * rho_packed_ref.shape[0] // dirs)
    for n in range(pieces):
        large[n].wait()

        def turn(m, carry):
            for k in range(4):
                for p in range(2):
                    at = n * size + 4 * m + k
                    mt_ref[at, p] = model_ref[at, p].T * weight_bf16
            return carry

        lax.fori_loop(0, size // 4, turn, 0)


def residual(mt_ref, vt_ref, grow_ref, gcol_ref, z_ref, r_ref, p_ref, ct_ref):
    dirs, _, cols, rows = mt_ref.shape
    ct_ref[...] = gcol_ref[...].T
    chunk = 64

    def predict(n, carry):
        here = pl.ds(pl.multiple_of(n * chunk, chunk), chunk)
        ctile = ct_ref[here, :]
        acc_r = vt_ref[0, here, :]
        acc_i = vt_ref[1, here, :]
        for k in range(dirs):
            mr = mt_ref[k, 0, here, :].astype(jnp.float32)
            mi = mt_ref[k, 1, here, :].astype(jnp.float32)
            cr = jnp.broadcast_to(ctile[:, k : k + 1], (chunk, rows))
            ci = jnp.broadcast_to(ctile[:, dirs + k : dirs + k + 1], (chunk, rows))
            zr = mr * cr + mi * ci
            zi = mi * cr - mr * ci
            z_ref[k, 0, here, :] = zr
            z_ref[k, 1, here, :] = zi
            gr = grow_ref[k : k + 1, :]
            gi = grow_ref[dirs + k : dirs + k + 1, :]
            acc_r = acc_r - (gr * zr - gi * zi)
            acc_i = acc_i - (gr * zi + gi * zr)
        r_ref[0, here, :] = acc_r
        r_ref[1, here, :] = acc_i
        sq = acc_r * acc_r + acc_i * acc_i
        for c in range(0, chunk, 8):
            carry = carry + sq[c : c + 8]
        return carry

    p_ref[...] = lax.fori_loop(0, cols // chunk, predict, jnp.zeros(p_ref.shape, jnp.float32))


def normal_terms(z_ref, r_ref, out_ref):
    dirs, _, cols, rows = z_ref.shape
    group = 8
    part = 4

    def terms(n, carry):
        k0 = pl.multiple_of(n * group, group)
        blocks = [[], [], []]
        for half in range(0, group, part):
            sums = [[None] * 3 for _ in range(part)]
            for c in range(0, cols, 8):
                rr = r_ref[0, c : c + 8, :]
                ri = r_ref[1, c : c + 8, :]
                for kk in range(part):
                    zr = z_ref[k0 + half + kk, 0, c : c + 8, :]
                    zi = z_ref[k0 + half + kk, 1, c : c + 8, :]
                    new = (zr * zr + zi * zi, zr * rr + zi * ri, zr * ri - zi * rr)
                    for s in range(3):
                        old = sums[kk][s]
                        sums[kk][s] = new[s] if old is None else old + new[s]
            for s in range(3):
                blocks[s] += [jnp.sum(sums[kk][s], axis=0, keepdims=True) for kk in range(part)]
        for s in range(3):
            out_ref[pl.ds(s * dirs + k0, group), :] = jnp.concatenate(blocks[s], axis=0)
        return carry

    lax.fori_loop(0, dirs // group, terms, 0)


def own_parity(shape, span, j):
    return lax.rem(lane_block(shape, span), 2) == lax.rem(j, 2)


def terms_kernel(z_ref, r_ref, same_ref, other_ref, all_ref, *, span):
    dirs, _, cols, rows = z_ref.shape
    half = dirs // 2
    normal_terms(z_ref, r_ref, all_ref)
    mine = own_parity((half, rows), span, lax.axis_index("scol"))
    for q in range(3):
        low = all_ref[q * dirs : q * dirs + half, :]
        high = pltpu.roll(all_ref[q * dirs + half : (q + 1) * dirs, :], span, 1)
        same_ref[q * half : (q + 1) * half, :] = jnp.where(mine, low, high)
        other_ref[q * half : (q + 1) * half, :] = jnp.where(mine, high, low)
    for ref in (same_ref, other_ref):
        ref[3 * half :, :] = jnp.zeros((8, rows), jnp.float32)


def unfold(same, other, span, j):
    mine = own_parity(same.shape, span, j)
    low = jnp.where(mine, same, other)
    high = pltpu.roll(jnp.where(mine, other, same), same.shape[1] - span, 1)
    return jnp.concatenate([low, high], axis=0)


def pack_folded(piece, j, span):
    half, lanes = piece.shape
    parts = lanes // span
    depth = 2 * half // parts
    where = lane_block((depth, lanes), span)
    packed = None
    for q in range(parts):
        block = j + q * depth // half
        at = q * depth % half
        shift = lax.rem((q - block) * span + 2 * lanes, lanes)
        moved = pltpu.roll(piece[at : at + depth], shift, 1)
        packed = moved if packed is None else jnp.where(where == q, moved, packed)
    return packed


def last_terms_kernel(z_ref, r_ref, *refs, span):
    outs, all_ref = refs[:-1], refs[-1]
    dirs, _, cols, rows = z_ref.shape
    depth = dirs * span // rows
    normal_terms(z_ref, r_ref, all_ref)
    for n, out_ref in enumerate(outs):
        block = jnp.bitwise_xor(lax.axis_index("scol"), n)
        for q in range(3):
            plane = all_ref[q * dirs : (q + 1) * dirs, :]
            out_ref[q * depth : (q + 1) * depth, :] = pack_plane(plane, block, span)
        out_ref[3 * depth :, :] = jnp.zeros((8, rows), jnp.float32)


def first_kernel(*refs, ns, nz, span):
    cols_in = refs[:ns]
    rows_in = refs[ns : ns + nz]
    mt_ref, vt_ref = refs[nz + ns : nz + ns + 2]
    outs = refs[nz + ns + 2 : nz + ns + 5]
    grow_ref, gcol_ref, trow_ref, tcol_ref, ct_ref = refs[nz + ns + 5 :]
    dirs = mt_ref.shape[0]
    i, j = lax.axis_index("srow"), lax.axis_index("scol")
    depth = dirs * span // mt_ref.shape[3]
    for pieces, g_ref, t_ref, me in ((rows_in, grow_ref, trow_ref, j), (cols_in, gcol_ref, tcol_ref, i)):
        blocks = [jnp.bitwise_xor(me, n) for n in range(len(pieces))]
        for q in range(4):
            plane = unpack_planes([p[q * depth : (q + 1) * depth, :] for p in pieces], blocks, span)
            dst = g_ref if q < 2 else t_ref
            at = (q % 2) * dirs
            dst[at : at + dirs, :] = plane
    residual(mt_ref, vt_ref, grow_ref, gcol_ref, *outs, ct_ref)


def sweep_kernel(*refs, ns, span, scale):
    pieces = refs[:ns]
    same_ref, other_ref, growin_ref, gcolin_ref, trow_ref, tcol_ref = refs[ns : ns + 6]
    rho_ref, mt_ref, vt_ref = refs[ns + 6 : ns + 9]
    outs = refs[ns + 9 : ns + 12]
    grow_ref, gcol_ref, ct_ref = refs[ns + 12 :]
    dirs = mt_ref.shape[0]
    i = lax.axis_index("srow")
    depth = dirs * span // mt_ref.shape[3]
    power = pieces[0][3 * depth :, :]
    for p in pieces[1:]:
        power = power + p[3 * depth :, :]
    rho_eff = rho_ref[...] * (jnp.sum(power) * scale + EPS)
    re, im = slice(0, dirs), slice(dirs, 2 * dirs)
    half = dirs // 2
    a, cr, ci = [
        unfold(
            same_ref[q * half : (q + 1) * half, :],
            other_ref[q * half : (q + 1) * half, :],
            span,
            lax.axis_index("scol"),
        )
        for q in range(3)
    ]
    grow_ref[re, :], grow_ref[im, :] = solve(
        a, cr, ci, growin_ref[re, :], growin_ref[im, :], trow_ref[re, :], trow_ref[im, :], rho_eff
    )
    blocks = [jnp.bitwise_xor(i, n) for n in range(ns)]
    a, cr, ci = [
        unpack_planes([p[q * depth : (q + 1) * depth, :] for p in pieces], blocks, span)
        for q in range(3)
    ]
    gcol_ref[re, :], gcol_ref[im, :] = solve(
        a, cr, ci, gcolin_ref[re, :], gcolin_ref[im, :], tcol_ref[re, :], tcol_ref[im, :], rho_eff
    )
    residual(mt_ref, vt_ref, grow_ref, gcol_ref, *outs, ct_ref)


def add_kernel(a_ref, b_ref, out_ref):
    out_ref[...] = a_ref[...] + b_ref[...]


def combine_kernel(*refs, nz, span):
    parts = refs[:nz]
    pair_ref, own_ref = refs[nz:]
    half = pair_ref.shape[0] // 3
    depth = 2 * half * span // pair_ref.shape[1]
    total = parts[0][...]
    for p in parts[1:]:
        total = total + p[...]
    pair_ref[...] = total[: 3 * half]
    for q in range(3):
        piece = total[q * half : (q + 1) * half]
        own_ref[q * depth : (q + 1) * depth, :] = pack_folded(piece, lax.axis_index("scol"), span)
    own_ref[3 * depth :, :] = total[3 * half :]


def last_combine_kernel(*refs, nz, span):
    parts = refs[:nz]
    g_ref, t_ref, d_ref, power_ref, mail_ref = refs[nz:]
    dirs = g_ref.shape[0] // 2
    depth = dirs * span // g_ref.shape[1]
    j = lax.axis_index("scol")
    total = parts[0][...]
    for p in parts[1:]:
        total = total + p[...]
    mail_ref[: 3 * depth, :] = total[: 3 * depth]
    power_ref[...] = total[3 * depth :]
    for n, ref in enumerate((g_ref, t_ref)):
        for p in range(2):
            at = (3 + 2 * n + p) * depth
            plane = ref[p * dirs : (p + 1) * dirs, :]
            mail_ref[at : at + depth, :] = pack_plane(plane, j, span)
    mail_ref[7 * depth :, :] = d_ref[...]


def final_kernel(*refs, ns, scale, pair, span, scal):
    powers = refs[:ns]
    mails = refs[ns : ns + 1 + pair]
    rho_ref = refs[ns + 1 + pair]
    outs = refs[ns + 2 + pair :]
    depth, lanes = rho_ref.shape
    dirs = depth * lanes // span
    power = powers[0][...]
    for p in powers[1:]:
        power = power + p[...]
    rho_eff = rho_ref[...] * (jnp.sum(power) * scale + EPS)
    news = []
    for mail in mails:
        a, cr, ci, gr, gi, tr, ti = [mail[q * depth : (q + 1) * depth, :] for q in range(7)]
        news.append(solve(a, cr, ci, gr, gi, tr, ti, rho_eff))
    fields = list(news[0])
    if pair:
        duals = [[m[q * depth : (q + 1) * depth, :] for q in (7, 8)] for m in mails]
        first = lax.axis_index("chan") == 0
        coeffs, new_duals = [], []
        for p in range(2):
            own, other = [news[n][p] + duals[n][p] for n in range(2)]
            low, high = jnp.where(first, own, other), jnp.where(first, other, own)
            total = scal[0] * low + scal[1] * high
            coeffs.append(total / scal[2] / scal[2])
            brow = jnp.where(first, scal[0], scal[1])
            new_duals.append(duals[0][p] + news[0][p] - brow * coeffs[p])
        fields += coeffs + new_duals
    parts = lanes // span
    for at in range(0, len(fields), parts):
        group = fields[at : at + parts]
        plane = unpack_planes(group, list(range(len(group))), span)
        plane = jnp.concatenate([plane, jnp.zeros((lanes - dirs, lanes), jnp.float32)], axis=0)
        turned = plane.T
        for n in range(len(group)):
            out_ref = outs[(at + n) // 2]
            out_ref[(at + n) % 2] = turned[n * span : (n + 1) * span, :dirs]


SMEM = pl.BlockSpec(memory_space=pltpu.SMEM)
VMEM = pl.BlockSpec(memory_space=pltpu.VMEM)
HBM = pl.BlockSpec(memory_space=pltpu.HBM)


def f32(*shape):
    return jax.ShapeDtypeStruct(shape, jnp.float32)


def call(kernel, name, lead, args, outs, scratch=(), place=VMEM):
    if place is HBM:
        args = [pltpu.with_memory_space_constraint(x, pltpu.HBM) for x in args]
    return pl.pallas_call(
        kernel,
        in_specs=[SMEM] * len(lead) + [place] * len(args),
        out_specs=[VMEM] * len(outs),
        out_shape=outs,
        scratch_shapes=scratch,
        compiler_params=pltpu.CompilerParams(vmem_limit_bytes=VMEM_LIMIT),
        name=name,
    )(*lead, *args)


def swap(x, axis, n):
    size = lax.axis_size(axis)
    return lax.ppermute(x, axis, [(m, m ^ n) for m in range(size)])


def shards(vis, model, flags, gains, consensus, dual, rho, cluster):
    groups = lax.axis_size("chan")
    ns = lax.axis_size("srow")
    nz = lax.axis_size("scol")
    order = consensus.shape[1]
    dirs = gains.shape[1]
    span = gains.shape[3]
    rows, cols = vis.shape[2:]
    depth = dirs * span // rows
    f = lax.axis_index("chan")
    pair = groups == 2 and order == 1

    table = basis_table(groups, order)
    brow = lax.dynamic_index_in_dim(table, f, 0, keepdims=False)
    own_in = [
        gains[0].transpose(1, 2, 0),
        consensus.transpose(1, 2, 3, 0),
        dual[0].transpose(1, 2, 0),
    ]
    start, dual_packed = call(
        functools.partial(pack_kernel, alone=order == 1),
        "pack",
        [] if order == 1 else [brow],
        own_in,
        [f32(4 * depth, rows), f32(2 * depth, rows)],
        [pltpu.VMEM(x.shape, jnp.float32) for x in own_in] + [pltpu.SemaphoreType.DMA((3,))],
        HBM,
    )
    col_parts = [start] + [swap(start, "srow", n) for n in range(1, ns)]
    row_parts = [start] + [swap(start, "scol", n) for n in range(1, nz)]
    field_in = [rho, cluster, flags[0], model[0], vis[0]]
    mt, vt, rho_rows, rho_packed = call(
        prepare_kernel,
        "prepare",
        [],
        field_in,
        [
            jax.ShapeDtypeStruct((dirs, 2, cols, rows), jnp.bfloat16),
            f32(2, cols, rows),
            f32(dirs, rows),
            f32(depth, rows),
        ],
        [(pltpu.SMEM if n < 3 else pltpu.VMEM)(x.shape, x.dtype) for n, x in enumerate(field_in)]
        + [pltpu.SemaphoreType.DMA((12,))],
        HBM,
    )

    scratch = [pltpu.VMEM((cols, 2 * dirs), jnp.float32)]
    scale = 1.0 / (groups * STATIONS * STATIONS)
    plane = f32(2 * dirs, rows)
    fields = [f32(dirs, 2, cols, rows), f32(2, cols, rows), f32(8, rows)]
    z, r, power, grow, gcol, trow, tcol = call(
        functools.partial(first_kernel, ns=ns, nz=nz, span=span),
        "first",
        [],
        col_parts + row_parts + [mt, vt],
        fields + [plane, plane, plane, plane],
        scratch,
    )
    for step in range(ITERS):
        last = step == ITERS - 1
        if groups == 2:
            power = power + swap(power, ("chan", "srow"), ns + 1)
        else:
            power = lax.psum(power, "chan")
        if last:
            break
        half = 3 * dirs // 2
        same, other = call(
            functools.partial(terms_kernel, span=span),
            "terms",
            [],
            [z, r],
            [f32(half + 8, rows)] * 2,
            [pltpu.VMEM((3 * dirs, rows), jnp.float32)],
        )
        same = lax.dynamic_update_slice(same, power, (half, 0))
        other = lax.dynamic_update_slice(other, power, (half, 0))
        sums = call(add_kernel, "add", [], [same, swap(other, "scol", 1)], [f32(half + 8, rows)])[0]
        pair_sums, own = call(
            functools.partial(combine_kernel, nz=2, span=span),
            "combine",
            [],
            [sums, swap(sums, "scol", 2)],
            [f32(half, rows), f32(3 * depth + 8, rows)],
        )
        other_sums = swap(pair_sums, "scol", 1)
        pieces = [own] + [swap(own, "srow", n) for n in range(1, ns)]
        z, r, power, grow, gcol = call(
            functools.partial(sweep_kernel, ns=ns, span=span, scale=scale),
            "sweep",
            [],
            pieces + [pair_sums, other_sums, grow, gcol, trow, tcol, rho_rows, mt, vt],
            fields + [plane, plane],
            scratch,
        )

    parts = call(
        functools.partial(last_terms_kernel, span=span),
        "terms",
        [],
        [z, r],
        [f32(3 * depth + 8, rows)] * nz,
        [pltpu.VMEM((3 * dirs, rows), jnp.float32)],
    )
    parts = [lax.dynamic_update_slice(part, power, (3 * depth, 0)) for part in parts]
    power, mail = call(
        functools.partial(last_combine_kernel, nz=nz, span=span),
        "combine",
        [],
        [parts[0]] + [swap(parts[n], "scol", n) for n in range(1, nz)] + [grow, trow, dual_packed],
        [f32(8, rows), f32(9 * depth, rows)],
    )
    powers = [power] + [swap(power, "srow", n) for n in range(1, ns)]
    mails = [mail] + ([swap(mail, "chan", 1)] if pair else [])
    outs = call(
        functools.partial(
            final_kernel, ns=ns, scale=scale, pair=int(pair), span=span, scal=pair_scalars(pair)
        ),
        "final",
        [],
        powers + mails + [rho_packed],
        [f32(2, span, dirs)] * (3 if pair else 1),
    )
    outs = [x.transpose(2, 0, 1) for x in outs]
    if pair:
        g, coeffs, dual_new = outs
        return (g[None], coeffs[:, None], dual_new[None])
    g = outs[0]
    dual_own = dual[0]
    local = brow[None, :, None, None] * (g + dual_own)[:, None, :, :]
    coeffs = gram_solve(table, lax.psum(local, "chan"))
    dual_new = (
        dual_own + g - jnp.einsum("b,kbcp->kcp", brow, coeffs, precision=lax.Precision.HIGHEST)
    )
    return (g[None], coeffs, dual_new[None])


def solution(mesh):
    placed = (
        P("chan", None, "srow", "scol"),
        P("chan", None, None, "srow", "scol"),
        P("chan", "srow", "scol"),
        P("chan", None, None, ("srow", "scol")),
        P(None, None, None, ("srow", "scol")),
        P("chan", None, None, ("srow", "scol")),
        P(),
        P(),
    )
    return jax.shard_map(
        shards,
        mesh=mesh,
        in_specs=placed,
        out_specs=(
            P("chan", None, None, ("srow", "scol")),
            P(None, None, None, ("srow", "scol")),
            P("chan", None, None, ("srow", "scol")),
        ),
        check_vma=False,
    )
```

```python
import functools
import math

import jax
import jax.numpy as jnp
import numpy as np
from jax import lax
from jax.experimental import pallas as pl
from jax.experimental.pallas import tpu as pltpu
from jax.sharding import PartitionSpec as P

STATIONS = 512
TILE = 16
ITERS = 4

EPS = 1e-05
STEP = 0.5

VMEM_LIMIT = 24 << 20


def basis_table(groups, order):
    xval = (jnp.arange(groups, dtype=jnp.float32) + 0.5) / groups
    columns = [
        math.comb(order - 1, b) * xval**b * (1.0 - xval) ** (order - 1 - b) for b in range(order)
    ]
    return jnp.stack(columns, axis=1)


def pair_scalars(pair):
    if not pair:
        return None
    xval = (np.arange(2, dtype=np.float32) + np.float32(0.5)) / np.float32(2)
    column = xval**0 * (np.float32(1.0) - xval) ** 0
    return float(column[0]), float(column[1]), float(np.sqrt(np.sum(column * column)))


def gram_solve(table, rhs):
    gram = jnp.dot(table.T, table, precision=lax.Precision.HIGHEST)
    factor = jnp.linalg.cholesky(gram)
    order = rhs.shape[1]
    flat = jnp.moveaxis(rhs, 1, 0).reshape(order, -1)
    sol = jax.scipy.linalg.cho_solve((factor, True), flat)
    return jnp.moveaxis(sol.reshape((order, rhs.shape[0]) + rhs.shape[2:]), 0, 1)


def lane_block(shape, span):
    return lax.broadcasted_iota(jnp.int32, shape, 1) // span


def pack_plane(plane, block, span):
    dirs, lanes = plane.shape
    parts = lanes // span
    rows = dirs // parts
    where = lane_block((rows, lanes), span)
    packed = None
    for q in range(parts):
        piece = plane[q * rows : (q + 1) * rows]
        shift = lax.rem((q - block) * span + lanes, lanes)
        piece = pltpu.roll(piece, shift, 1)
        packed = piece if packed is None else jnp.where(where == q, piece, packed)
    return packed


def unpack_planes(pieces, blocks, span):
    rows, lanes = pieces[0].shape
    parts = lanes // span
    where = lane_block((rows, lanes), span)
    out = []
    for q in range(parts):
        plane = None
        for piece, block in zip(pieces, blocks):
            shift = lax.rem((block - q) * span + lanes, lanes)
            moved = pltpu.roll(piece, shift, 1)
            plane = moved if plane is None else jnp.where(where == block, moved, plane)
        out.append(plane)
    return jnp.concatenate(out, axis=0)


def solve(a, cr, ci, gr, gi, tr, ti, rho_eff):
    denom = a + rho_eff
    fresh_r = (cr + a * gr + rho_eff * tr) / denom
    fresh_i = (ci + a * gi + rho_eff * ti) / denom
    return gr + STEP * (fresh_r - gr), gi + STEP * (fresh_i - gi)


def fetch(sources, targets, sems):
    copies = [
        pltpu.make_async_copy(src, dst, sems.at[n])
        for n, (src, dst) in enumerate(zip(sources, targets))
    ]
    for copy in copies:
        copy.start()
    return copies


def pack_kernel(*refs, alone):
    brow_ref, refs = ([1.0], refs) if alone else (refs[0], refs[1:])
    start_ref, dual_out_ref = refs[3:5]
    gains_ref, consensus_ref, dual_ref = refs[5:8]
    for copy in fetch(refs[:3], refs[5:8], refs[8]):
        copy.wait()
    span, dirs = gains_ref.shape[1:]
    lanes = start_ref.shape[1]
    depth = dirs * span // lanes
    rows = []
    for p in range(2):
        target = brow_ref[0] * consensus_ref[0, p]
        for b in range(1, consensus_ref.shape[0]):
            target = target + brow_ref[b] * consensus_ref[b, p]
        rows.append(target - dual_ref[p])
    for fields, out_ref in (
        ([gains_ref[0], gains_ref[1]] + rows, start_ref),
        ([dual_ref[0], dual_ref[1]], dual_out_ref),
    ):
        plane = to_plane(fields, lanes)[:dirs]
        for n in range(len(fields)):
            out_ref[n * depth : (n + 1) * depth, :] = pack_plane(plane, n, span)


def to_plane(fields, lanes):
    x = jnp.concatenate(fields, axis=0)
    if x.shape[0] < lanes:
        x = jnp.concatenate([x, jnp.zeros((lanes - x.shape[0], x.shape[1]), x.dtype)], axis=0)
    if x.shape[1] < lanes:
        x = jnp.concatenate([x, jnp.zeros((lanes, lanes - x.shape[1]), x.dtype)], axis=1)
    return x.T


def prepare_kernel(*refs):
    ins = refs[:5]
    mt_ref, vt_ref, rho_rows_ref, rho_packed_ref = refs[5:9]
    rho_ref, cluster_ref, flags_ref, model_ref, vis_ref, sems = refs[9:]
    dirs, _, rows, cols = model_ref.shape
    pieces = 8
    size = dirs // pieces
    small = fetch(ins[:3] + ins[4:], [rho_ref, cluster_ref, flags_ref, vis_ref], sems)
    large = fetch(
        [ins[3].at[pl.ds(n * size, size)] for n in range(pieces)],
        [model_ref.at[pl.ds(n * size, size)] for n in range(pieces)],
        sems.at[pl.ds(4, pieces)],
    )
    for copy in small:
        copy.wait()
    where = lax.broadcasted_iota(jnp.int32, (1, rows), 1) // TILE
    bands = []
    for b in range(cols // TILE):
        band = jnp.zeros((1, rows), jnp.float32)
        for r in range(rows // TILE):
            band = jnp.where(where == r, flags_ref[r, b].astype(jnp.float32), band)
        bands.append(jnp.broadcast_to(band, (TILE, rows)))
    weight = jnp.concatenate(bands, axis=0)
    weight_bf16 = weight.astype(jnp.bfloat16)
    for p in range(2):
        vt_ref[p] = vis_ref[p].astype(jnp.float32).T * weight
    for k in range(dirs):
        rho_rows_ref[k : k + 1, :] = jnp.full((1, rows), rho_ref[cluster_ref[k]], jnp.float32)
    rho_packed_ref[...] = pack_plane(rho_rows_ref[...], 0, rows * rho_packed_ref.shape[0] // dirs)
    for n in range(pieces):
        large[n].wait()

        def turn(m, carry):
            for k in range(4):
                for p in range(2):
                    at = n * size + 4 * m + k
                    mt_ref[at, p] = model_ref[at, p].T * weight_bf16
            return carry

        lax.fori_loop(0, size // 4, turn, 0)


def residual(mt_ref, vt_ref, grow_ref, gcol_ref, z_ref, r_ref, p_ref, ct_ref):
    dirs, _, cols, rows = mt_ref.shape
    ct_ref[...] = gcol_ref[...].T
    chunk = 64

    def predict(n, carry):
        here = pl.ds(pl.multiple_of(n * chunk, chunk), chunk)
        ctile = ct_ref[here, :]
        acc_r = vt_ref[0, here, :]
        acc_i = vt_ref[1, here, :]
        for k in range(dirs):
            mr = mt_ref[k, 0, here, :].astype(jnp.float32)
            mi = mt_ref[k, 1, here, :].astype(jnp.float32)
            cr = jnp.broadcast_to(ctile[:, k : k + 1], (chunk, rows))
            ci = jnp.broadcast_to(ctile[:, dirs + k : dirs + k + 1], (chunk, rows))
            zr = mr * cr + mi * ci
            zi = mi * cr - mr * ci
            z_ref[k, 0, here, :] = zr
            z_ref[k, 1, here, :] = zi
            gr = grow_ref[k : k + 1, :]
            gi = grow_ref[dirs + k : dirs + k + 1, :]
            acc_r = acc_r - (gr * zr - gi * zi)
            acc_i = acc_i - (gr * zi + gi * zr)
        r_ref[0, here, :] = acc_r
        r_ref[1, here, :] = acc_i
        sq = acc_r * acc_r + acc_i * acc_i
        for c in range(0, chunk, 8):
            carry = carry + sq[c : c + 8]
        return carry

    p_ref[...] = lax.fori_loop(0, cols // chunk, predict, jnp.zeros(p_ref.shape, jnp.float32))


def normal_terms(z_ref, r_ref, out_ref):
    dirs, _, cols, rows = z_ref.shape
    group = 8
    part = 4

    def terms(n, carry):
        k0 = pl.multiple_of(n * group, group)
        blocks = [[], [], []]
        for half in range(0, group, part):
            sums = [[None] * 3 for _ in range(part)]
            for c in range(0, cols, 8):
                rr = r_ref[0, c : c + 8, :]
                ri = r_ref[1, c : c + 8, :]
                for kk in range(part):
                    zr = z_ref[k0 + half + kk, 0, c : c + 8, :]
                    zi = z_ref[k0 + half + kk, 1, c : c + 8, :]
                    new = (zr * zr + zi * zi, zr * rr + zi * ri, zr * ri - zi * rr)
                    for s in range(3):
                        old = sums[kk][s]
                        sums[kk][s] = new[s] if old is None else old + new[s]
            for s in range(3):
                blocks[s] += [jnp.sum(sums[kk][s], axis=0, keepdims=True) for kk in range(part)]
        for s in range(3):
            out_ref[pl.ds(s * dirs + k0, group), :] = jnp.concatenate(blocks[s], axis=0)
        return carry

    lax.fori_loop(0, dirs // group, terms, 0)


def own_parity(shape, span, j):
    return lax.rem(lane_block(shape, span), 2) == lax.rem(j, 2)


def terms_kernel(z_ref, r_ref, same_ref, other_ref, all_ref, *, span):
    dirs, _, cols, rows = z_ref.shape
    half = dirs // 2
    normal_terms(z_ref, r_ref, all_ref)
    mine = own_parity((half, rows), span, lax.axis_index("scol"))
    for q in range(3):
        low = all_ref[q * dirs : q * dirs + half, :]
        high = pltpu.roll(all_ref[q * dirs + half : (q + 1) * dirs, :], span, 1)
        same_ref[q * half : (q + 1) * half, :] = jnp.where(mine, low, high)
        other_ref[q * half : (q + 1) * half, :] = jnp.where(mine, high, low)
    for ref in (same_ref, other_ref):
        ref[3 * half :, :] = jnp.zeros((8, rows), jnp.float32)


def unfold(same, other, span, j):
    mine = own_parity(same.shape, span, j)
    low = jnp.where(mine, same, other)
    high = pltpu.roll(jnp.where(mine, other, same), same.shape[1] - span, 1)
    return jnp.concatenate([low, high], axis=0)


def pack_folded(piece, j, span):
    half, lanes = piece.shape
    parts = lanes // span
    depth = 2 * half // parts
    where = lane_block((depth, lanes), span)
    packed = None
    for q in range(parts):
        block = j + q * depth // half
        at = q * depth % half
        shift = lax.rem((q - block) * span + 2 * lanes, lanes)
        moved = pltpu.roll(piece[at : at + depth], shift, 1)
        packed = moved if packed is None else jnp.where(where == q, moved, packed)
    return packed


def last_terms_kernel(z_ref, r_ref, *refs, span):
    outs, all_ref = refs[:-1], refs[-1]
    dirs, _, cols, rows = z_ref.shape
    depth = dirs * span // rows
    normal_terms(z_ref, r_ref, all_ref)
    for n, out_ref in enumerate(outs):
        block = jnp.bitwise_xor(lax.axis_index("scol"), n)
        for q in range(3):
            plane = all_ref[q * dirs : (q + 1) * dirs, :]
            out_ref[q * depth : (q + 1) * depth, :] = pack_plane(plane, block, span)
        out_ref[3 * depth :, :] = jnp.zeros((8, rows), jnp.float32)


def first_kernel(*refs, ns, nz, span):
    cols_in = refs[:ns]
    rows_in = refs[ns : ns + nz]
    mt_ref, vt_ref = refs[nz + ns : nz + ns + 2]
    outs = refs[nz + ns + 2 : nz + ns + 5]
    grow_ref, gcol_ref, trow_ref, tcol_ref, ct_ref = refs[nz + ns + 5 :]
    dirs = mt_ref.shape[0]
    i, j = lax.axis_index("srow"), lax.axis_index("scol")
    depth = dirs * span // mt_ref.shape[3]
    for pieces, g_ref, t_ref, me in ((rows_in, grow_ref, trow_ref, j), (cols_in, gcol_ref, tcol_ref, i)):
        blocks = [jnp.bitwise_xor(me, n) for n in range(len(pieces))]
        for q in range(4):
            plane = unpack_planes([p[q * depth : (q + 1) * depth, :] for p in pieces], blocks, span)
            dst = g_ref if q < 2 else t_ref
            at = (q % 2) * dirs
            dst[at : at + dirs, :] = plane
    residual(mt_ref, vt_ref, grow_ref, gcol_ref, *outs, ct_ref)


def sweep_kernel(*refs, ns, span, scale):
    pieces = refs[:ns]
    same_ref, other_ref, growin_ref, gcolin_ref, trow_ref, tcol_ref = refs[ns : ns + 6]
    rho_ref, mt_ref, vt_ref = refs[ns + 6 : ns + 9]
    outs = refs[ns + 9 : ns + 12]
    grow_ref, gcol_ref, ct_ref = refs[ns + 12 :]
    dirs = mt_ref.shape[0]
    i = lax.axis_index("srow")
    depth = dirs * span // mt_ref.shape[3]
    power = pieces[0][3 * depth :, :]
    for p in pieces[1:]:
        power = power + p[3 * depth :, :]
    rho_eff = rho_ref[...] * (jnp.sum(power) * scale + EPS)
    re, im = slice(0, dirs), slice(dirs, 2 * dirs)
    half = dirs // 2
    a, cr, ci = [
        unfold(
            same_ref[q * half : (q + 1) * half, :],
            other_ref[q * half : (q + 1) * half, :],
            span,
            lax.axis_index("scol"),
        )
        for q in range(3)
    ]
    grow_ref[re, :], grow_ref[im, :] = solve(
        a, cr, ci, growin_ref[re, :], growin_ref[im, :], trow_ref[re, :], trow_ref[im, :], rho_eff
    )
    blocks = [jnp.bitwise_xor(i, n) for n in range(ns)]
    a, cr, ci = [
        unpack_planes([p[q * depth : (q + 1) * depth, :] for p in pieces], blocks, span)
        for q in range(3)
    ]
    gcol_ref[re, :], gcol_ref[im, :] = solve(
        a, cr, ci, gcolin_ref[re, :], gcolin_ref[im, :], tcol_ref[re, :], tcol_ref[im, :], rho_eff
    )
    residual(mt_ref, vt_ref, grow_ref, gcol_ref, *outs, ct_ref)


def combine_kernel(*refs, nz, span):
    parts = refs[:nz]
    pair_ref, own_ref = refs[nz:]
    half = pair_ref.shape[0] // 3
    depth = 2 * half * span // pair_ref.shape[1]
    total = parts[0][...]
    for p in parts[1:]:
        total = total + p[...]
    pair_ref[...] = total[: 3 * half]
    for q in range(3):
        piece = total[q * half : (q + 1) * half]
        own_ref[q * depth : (q + 1) * depth, :] = pack_folded(piece, lax.axis_index("scol"), span)
    own_ref[3 * depth :, :] = total[3 * half :]


def last_combine_kernel(*refs, nz, span):
    parts = refs[:nz]
    g_ref, t_ref, d_ref, power_ref, mail_ref = refs[nz:]
    dirs = g_ref.shape[0] // 2
    depth = dirs * span // g_ref.shape[1]
    j = lax.axis_index("scol")
    total = parts[0][...]
    for p in parts[1:]:
        total = total + p[...]
    mail_ref[: 3 * depth, :] = total[: 3 * depth]
    power_ref[...] = total[3 * depth :]
    for n, ref in enumerate((g_ref, t_ref)):
        for p in range(2):
            at = (3 + 2 * n + p) * depth
            plane = ref[p * dirs : (p + 1) * dirs, :]
            mail_ref[at : at + depth, :] = pack_plane(plane, j, span)
    mail_ref[7 * depth :, :] = d_ref[...]


def final_kernel(*refs, ns, scale, pair, span, scal):
    powers = refs[:ns]
    mails = refs[ns : ns + 1 + pair]
    rho_ref = refs[ns + 1 + pair]
    outs = refs[ns + 2 + pair :]
    depth, lanes = rho_ref.shape
    dirs = depth * lanes // span
    power = powers[0][...]
    for p in powers[1:]:
        power = power + p[...]
    rho_eff = rho_ref[...] * (jnp.sum(power) * scale + EPS)
    news = []
    for mail in mails:
        a, cr, ci, gr, gi, tr, ti = [mail[q * depth : (q + 1) * depth, :] for q in range(7)]
        news.append(solve(a, cr, ci, gr, gi, tr, ti, rho_eff))
    fields = list(news[0])
    if pair:
        duals = [[m[q * depth : (q + 1) * depth, :] for q in (7, 8)] for m in mails]
        first = lax.axis_index("chan") == 0
        coeffs, new_duals = [], []
        for p in range(2):
            own, other = [news[n][p] + duals[n][p] for n in range(2)]
            low, high = jnp.where(first, own, other), jnp.where(first, other, own)
            total = scal[0] * low + scal[1] * high
            coeffs.append(total / scal[2] / scal[2])
            brow = jnp.where(first, scal[0], scal[1])
            new_duals.append(duals[0][p] + news[0][p] - brow * coeffs[p])
        fields += coeffs + new_duals
    parts = lanes // span
    for at in range(0, len(fields), parts):
        group = fields[at : at + parts]
        plane = unpack_planes(group, list(range(len(group))), span)
        plane = jnp.concatenate([plane, jnp.zeros((lanes - dirs, lanes), jnp.float32)], axis=0)
        turned = plane.T
        for n in range(len(group)):
            out_ref = outs[(at + n) // 2]
            out_ref[(at + n) % 2] = turned[n * span : (n + 1) * span, :dirs]


SMEM = pl.BlockSpec(memory_space=pltpu.SMEM)
VMEM = pl.BlockSpec(memory_space=pltpu.VMEM)
HBM = pl.BlockSpec(memory_space=pltpu.HBM)


def f32(*shape):
    return jax.ShapeDtypeStruct(shape, jnp.float32)


def call(kernel, name, lead, args, outs, scratch=(), place=VMEM):
    if place is HBM:
        args = [pltpu.with_memory_space_constraint(x, pltpu.HBM) for x in args]
    return pl.pallas_call(
        kernel,
        in_specs=[SMEM] * len(lead) + [place] * len(args),
        out_specs=[VMEM] * len(outs),
        out_shape=outs,
        scratch_shapes=scratch,
        compiler_params=pltpu.CompilerParams(vmem_limit_bytes=VMEM_LIMIT),
        name=name,
    )(*lead, *args)


def swap(x, axis, n):
    size = lax.axis_size(axis)
    return lax.ppermute(x, axis, [(m, m ^ n) for m in range(size)])


def shards(vis, model, flags, gains, consensus, dual, rho, cluster):
    groups = lax.axis_size("chan")
    ns = lax.axis_size("srow")
    nz = lax.axis_size("scol")
    order = consensus.shape[1]
    dirs = gains.shape[1]
    span = gains.shape[3]
    rows, cols = vis.shape[2:]
    depth = dirs * span // rows
    f = lax.axis_index("chan")
    pair = groups == 2 and order == 1

    table = basis_table(groups, order)
    brow = lax.dynamic_index_in_dim(table, f, 0, keepdims=False)
    own_in = [
        gains[0].transpose(1, 2, 0),
        consensus.transpose(1, 2, 3, 0),
        dual[0].transpose(1, 2, 0),
    ]
    start, dual_packed = call(
        functools.partial(pack_kernel, alone=order == 1),
        "pack",
        [] if order == 1 else [brow],
        own_in,
        [f32(4 * depth, rows), f32(2 * depth, rows)],
        [pltpu.VMEM(x.shape, jnp.float32) for x in own_in] + [pltpu.SemaphoreType.DMA((3,))],
        HBM,
    )
    col_parts = [start] + [swap(start, "srow", n) for n in range(1, ns)]
    row_parts = [start] + [swap(start, "scol", n) for n in range(1, nz)]
    field_in = [rho, cluster, flags[0], model[0], vis[0]]
    mt, vt, rho_rows, rho_packed = call(
        prepare_kernel,
        "prepare",
        [],
        field_in,
        [
            jax.ShapeDtypeStruct((dirs, 2, cols, rows), jnp.bfloat16),
            f32(2, cols, rows),
            f32(dirs, rows),
            f32(depth, rows),
        ],
        [(pltpu.SMEM if n < 3 else pltpu.VMEM)(x.shape, x.dtype) for n, x in enumerate(field_in)]
        + [pltpu.SemaphoreType.DMA((12,))],
        HBM,
    )

    scratch = [pltpu.VMEM((cols, 2 * dirs), jnp.float32)]
    scale = 1.0 / (groups * STATIONS * STATIONS)
    plane = f32(2 * dirs, rows)
    fields = [f32(dirs, 2, cols, rows), f32(2, cols, rows), f32(8, rows)]
    z, r, power, grow, gcol, trow, tcol = call(
        functools.partial(first_kernel, ns=ns, nz=nz, span=span),
        "first",
        [],
        col_parts + row_parts + [mt, vt],
        fields + [plane, plane, plane, plane],
        scratch,
    )
    for step in range(ITERS):
        last = step == ITERS - 1
        if groups == 2:
            power = power + swap(power, ("chan", "srow"), ns + 1)
        else:
            power = lax.psum(power, "chan")
        if last:
            break
        half = 3 * dirs // 2
        same, other = call(
            functools.partial(terms_kernel, span=span),
            "terms",
            [],
            [z, r],
            [f32(half + 8, rows)] * 2,
            [pltpu.VMEM((3 * dirs, rows), jnp.float32)],
        )
        same = lax.dynamic_update_slice(same, power, (half, 0))
        other = lax.dynamic_update_slice(other, power, (half, 0))
        pair_sums, own = call(
            functools.partial(combine_kernel, nz=nz, span=span),
            "combine",
            [],
            [same] + [swap(same if n % 2 == 0 else other, "scol", n) for n in range(1, nz)],
            [f32(half, rows), f32(3 * depth + 8, rows)],
        )
        other_sums = swap(pair_sums, "scol", 1)
        pieces = [own] + [swap(own, "srow", n) for n in range(1, ns)]
        z, r, power, grow, gcol = call(
            functools.partial(sweep_kernel, ns=ns, span=span, scale=scale),
            "sweep",
            [],
            pieces + [pair_sums, other_sums, grow, gcol, trow, tcol, rho_rows, mt, vt],
            fields + [plane, plane],
            scratch,
        )

    parts = call(
        functools.partial(last_terms_kernel, span=span),
        "terms",
        [],
        [z, r],
        [f32(3 * depth + 8, rows)] * nz,
        [pltpu.VMEM((3 * dirs, rows), jnp.float32)],
    )
    parts = [lax.dynamic_update_slice(part, power, (3 * depth, 0)) for part in parts]
    power, mail = call(
        functools.partial(last_combine_kernel, nz=nz, span=span),
        "combine",
        [],
        [parts[0]] + [swap(parts[n], "scol", n) for n in range(1, nz)] + [grow, trow, dual_packed],
        [f32(8, rows), f32(9 * depth, rows)],
    )
    powers = [power] + [swap(power, "srow", n) for n in range(1, ns)]
    mails = [mail] + ([swap(mail, "chan", 1)] if pair else [])
    outs = call(
        functools.partial(
            final_kernel, ns=ns, scale=scale, pair=int(pair), span=span, scal=pair_scalars(pair)
        ),
        "final",
        [],
        powers + mails + [rho_packed],
        [f32(2, span, dirs)] * (3 if pair else 1),
    )
    outs = [x.transpose(2, 0, 1) for x in outs]
    if pair:
        g, coeffs, dual_new = outs
        return (g[None], coeffs[:, None], dual_new[None])
    g = outs[0]
    dual_own = dual[0]
    local = brow[None, :, None, None] * (g + dual_own)[:, None, :, :]
    coeffs = gram_solve(table, lax.psum(local, "chan"))
    dual_new = (
        dual_own + g - jnp.einsum("b,kbcp->kcp", brow, coeffs, precision=lax.Precision.HIGHEST)
    )
    return (g[None], coeffs, dual_new[None])


def solution(mesh):
    placed = (
        P("chan", None, "srow", "scol"),
        P("chan", None, None, "srow", "scol"),
        P("chan", "srow", "scol"),
        P("chan", None, None, ("srow", "scol")),
        P(None, None, None, ("srow", "scol")),
        P("chan", None, None, ("srow", "scol")),
        P(),
        P(),
    )
    return jax.shard_map(
        shards,
        mesh=mesh,
        in_specs=placed,
        out_specs=(
            P("chan", None, None, ("srow", "scol")),
            P(None, None, None, ("srow", "scol")),
            P("chan", None, None, ("srow", "scol")),
        ),
        check_vma=False,
    )
```

```python
import functools
import math

import jax
import jax.numpy as jnp
import numpy as np
from jax import lax
from jax.experimental import pallas as pl
from jax.experimental.pallas import tpu as pltpu
from jax.sharding import PartitionSpec as P

STATIONS = 512
TILE = 16
ITERS = 4

EPS = 1e-05
STEP = 0.5

VMEM_LIMIT = 24 << 20


def basis_table(groups, order):
    xval = (jnp.arange(groups, dtype=jnp.float32) + 0.5) / groups
    columns = [
        math.comb(order - 1, b) * xval**b * (1.0 - xval) ** (order - 1 - b) for b in range(order)
    ]
    return jnp.stack(columns, axis=1)


def pair_scalars(pair):
    if not pair:
        return None
    xval = (np.arange(2, dtype=np.float32) + np.float32(0.5)) / np.float32(2)
    column = xval**0 * (np.float32(1.0) - xval) ** 0
    return float(column[0]), float(column[1]), float(np.sqrt(np.sum(column * column)))


def gram_solve(table, rhs):
    gram = jnp.dot(table.T, table, precision=lax.Precision.HIGHEST)
    factor = jnp.linalg.cholesky(gram)
    order = rhs.shape[1]
    flat = jnp.moveaxis(rhs, 1, 0).reshape(order, -1)
    sol = jax.scipy.linalg.cho_solve((factor, True), flat)
    return jnp.moveaxis(sol.reshape((order, rhs.shape[0]) + rhs.shape[2:]), 0, 1)


def lane_block(shape, span):
    return lax.broadcasted_iota(jnp.int32, shape, 1) // span


def pack_plane(plane, block, span):
    dirs, lanes = plane.shape
    parts = lanes // span
    rows = dirs // parts
    where = lane_block((rows, lanes), span)
    packed = None
    for q in range(parts):
        piece = plane[q * rows : (q + 1) * rows]
        shift = lax.rem((q - block) * span + lanes, lanes)
        piece = pltpu.roll(piece, shift, 1)
        packed = piece if packed is None else jnp.where(where == q, piece, packed)
    return packed


def unpack_planes(pieces, blocks, span):
    rows, lanes = pieces[0].shape
    parts = lanes // span
    where = lane_block((rows, lanes), span)
    out = []
    for q in range(parts):
        plane = None
        for piece, block in zip(pieces, blocks):
            shift = lax.rem((block - q) * span + lanes, lanes)
            moved = pltpu.roll(piece, shift, 1)
            plane = moved if plane is None else jnp.where(where == block, moved, plane)
        out.append(plane)
    return jnp.concatenate(out, axis=0)


def solve(a, cr, ci, gr, gi, tr, ti, rho_eff):
    denom = a + rho_eff
    fresh_r = (cr + a * gr + rho_eff * tr) / denom
    fresh_i = (ci + a * gi + rho_eff * ti) / denom
    return gr + STEP * (fresh_r - gr), gi + STEP * (fresh_i - gi)


def fetch(sources, targets, sems):
    copies = [
        pltpu.make_async_copy(src, dst, sems.at[n])
        for n, (src, dst) in enumerate(zip(sources, targets))
    ]
    for copy in copies:
        copy.start()
    return copies


def pack_kernel(*refs, alone):
    brow_ref, refs = ([1.0], refs) if alone else (refs[0], refs[1:])
    start_ref, dual_out_ref = refs[3:5]
    gains_ref, consensus_ref, dual_ref = refs[5:8]
    for copy in fetch(refs[:3], refs[5:8], refs[8]):
        copy.wait()
    span, dirs = gains_ref.shape[1:]
    lanes = start_ref.shape[1]
    depth = dirs * span // lanes
    rows = []
    for p in range(2):
        target = brow_ref[0] * consensus_ref[0, p]
        for b in range(1, consensus_ref.shape[0]):
            target = target + brow_ref[b] * consensus_ref[b, p]
        rows.append(target - dual_ref[p])
    for fields, out_ref in (
        ([gains_ref[0], gains_ref[1]] + rows, start_ref),
        ([dual_ref[0], dual_ref[1]], dual_out_ref),
    ):
        plane = to_plane(fields, lanes)[:dirs]
        for n in range(len(fields)):
            out_ref[n * depth : (n + 1) * depth, :] = pack_plane(plane, n, span)


def to_plane(fields, lanes):
    x = jnp.concatenate(fields, axis=0)
    if x.shape[0] < lanes:
        x = jnp.concatenate([x, jnp.zeros((lanes - x.shape[0], x.shape[1]), x.dtype)], axis=0)
    if x.shape[1] < lanes:
        x = jnp.concatenate([x, jnp.zeros((lanes, lanes - x.shape[1]), x.dtype)], axis=1)
    return x.T


def prepare_kernel(*refs):
    ins = refs[:5]
    mt_ref, vt_ref, rho_rows_ref, rho_packed_ref = refs[5:9]
    rho_ref, cluster_ref, flags_ref, model_ref, vis_ref, sems = refs[9:]
    dirs, _, rows, cols = model_ref.shape
    pieces = 8
    size = dirs // pieces
    small = fetch(ins[:3] + ins[4:], [rho_ref, cluster_ref, flags_ref, vis_ref], sems)
    large = fetch(
        [ins[3].at[pl.ds(n * size, size)] for n in range(pieces)],
        [model_ref.at[pl.ds(n * size, size)] for n in range(pieces)],
        sems.at[pl.ds(4, pieces)],
    )
    for copy in small:
        copy.wait()
    where = lax.broadcasted_iota(jnp.int32, (1, rows), 1) // TILE
    bands = []
    for b in range(cols // TILE):
        band = jnp.zeros((1, rows), jnp.float32)
        for r in range(rows // TILE):
            band = jnp.where(where == r, flags_ref[r, b].astype(jnp.float32), band)
        bands.append(jnp.broadcast_to(band, (TILE, rows)))
    weight = jnp.concatenate(bands, axis=0)
    weight_bf16 = weight.astype(jnp.bfloat16)
    for p in range(2):
        vt_ref[p] = vis_ref[p].astype(jnp.float32).T * weight
    for k in range(dirs):
        rho_rows_ref[k : k + 1, :] = jnp.full((1, rows), rho_ref[cluster_ref[k]], jnp.float32)
    rho_packed_ref[...] = pack_plane(rho_rows_ref[...], 0, rows * rho_packed_ref.shape[0] // dirs)
    for n in range(pieces):
        large[n].wait()

        def turn(m, carry):
            for k in range(4):
                for p in range(2):
                    at = n * size + 4 * m + k
                    mt_ref[at, p] = model_ref[at, p].T * weight_bf16
            return carry

        lax.fori_loop(0, size // 4, turn, 0)


def residual(mt_ref, vt_ref, grow_ref, gcol_ref, z_ref, r_ref, p_ref, ct_ref):
    dirs, _, cols, rows = mt_ref.shape
    ct_ref[...] = gcol_ref[...].T
    chunk = 64

    def predict(n, carry):
        here = pl.ds(pl.multiple_of(n * chunk, chunk), chunk)
        ctile = ct_ref[here, :]
        acc_r = vt_ref[0, here, :]
        acc_i = vt_ref[1, here, :]
        for k in range(dirs):
            mr = mt_ref[k, 0, here, :].astype(jnp.float32)
            mi = mt_ref[k, 1, here, :].astype(jnp.float32)
            cr = jnp.broadcast_to(ctile[:, k : k + 1], (chunk, rows))
            ci = jnp.broadcast_to(ctile[:, dirs + k : dirs + k + 1], (chunk, rows))
            zr = mr * cr + mi * ci
            zi = mi * cr - mr * ci
            z_ref[k, 0, here, :] = zr
            z_ref[k, 1, here, :] = zi
            gr = grow_ref[k : k + 1, :]
            gi = grow_ref[dirs + k : dirs + k + 1, :]
            acc_r = acc_r - (gr * zr - gi * zi)
            acc_i = acc_i - (gr * zi + gi * zr)
        r_ref[0, here, :] = acc_r
        r_ref[1, here, :] = acc_i
        sq = acc_r * acc_r + acc_i * acc_i
        for c in range(0, chunk, 8):
            carry = carry + sq[c : c + 8]
        return carry

    p_ref[...] = lax.fori_loop(0, cols // chunk, predict, jnp.zeros(p_ref.shape, jnp.float32))


def normal_terms(z_ref, r_ref, out_ref):
    dirs, _, cols, rows = z_ref.shape
    group = 8
    part = 4

    def terms(n, carry):
        k0 = pl.multiple_of(n * group, group)
        blocks = [[], [], []]
        for half in range(0, group, part):
            sums = [[None] * 3 for _ in range(part)]
            for c in range(0, cols, 8):
                rr = r_ref[0, c : c + 8, :]
                ri = r_ref[1, c : c + 8, :]
                for kk in range(part):
                    zr = z_ref[k0 + half + kk, 0, c : c + 8, :]
                    zi = z_ref[k0 + half + kk, 1, c : c + 8, :]
                    new = (zr * zr + zi * zi, zr * rr + zi * ri, zr * ri - zi * rr)
                    for s in range(3):
                        old = sums[kk][s]
                        sums[kk][s] = new[s] if old is None else old + new[s]
            for s in range(3):
                blocks[s] += [jnp.sum(sums[kk][s], axis=0, keepdims=True) for kk in range(part)]
        for s in range(3):
            out_ref[pl.ds(s * dirs + k0, group), :] = jnp.concatenate(blocks[s], axis=0)
        return carry

    lax.fori_loop(0, dirs // group, terms, 0)


def own_parity(shape, span, j):
    return lax.rem(lane_block(shape, span), 2) == lax.rem(j, 2)


def terms_kernel(z_ref, r_ref, same_ref, other_ref, all_ref, *, span):
    dirs, _, cols, rows = z_ref.shape
    half = dirs // 2
    normal_terms(z_ref, r_ref, all_ref)
    mine = own_parity((half, rows), span, lax.axis_index("scol"))
    for q in range(3):
        low = all_ref[q * dirs : q * dirs + half, :]
        high = pltpu.roll(all_ref[q * dirs + half : (q + 1) * dirs, :], span, 1)
        same_ref[q * half : (q + 1) * half, :] = jnp.where(mine, low, high)
        other_ref[q * half : (q + 1) * half, :] = jnp.where(mine, high, low)
    for ref in (same_ref, other_ref):
        ref[3 * half :, :] = jnp.zeros((8, rows), jnp.float32)


def unfold(same, other, span, j):
    mine = own_parity(same.shape, span, j)
    low = jnp.where(mine, same, other)
    high = pltpu.roll(jnp.where(mine, other, same), same.shape[1] - span, 1)
    return jnp.concatenate([low, high], axis=0)


def pack_folded(piece, j, span):
    half, lanes = piece.shape
    parts = lanes // span
    depth = 2 * half // parts
    where = lane_block((depth, lanes), span)
    packed = None
    for q in range(parts):
        block = j + q * depth // half
        at = q * depth % half
        shift = lax.rem((q - block) * span + 2 * lanes, lanes)
        moved = pltpu.roll(piece[at : at + depth], shift, 1)
        packed = moved if packed is None else jnp.where(where == q, moved, packed)
    return packed


def last_terms_kernel(z_ref, r_ref, *refs, span):
    outs, all_ref = refs[:-1], refs[-1]
    dirs, _, cols, rows = z_ref.shape
    depth = dirs * span // rows
    normal_terms(z_ref, r_ref, all_ref)
    for n, out_ref in enumerate(outs):
        block = jnp.bitwise_xor(lax.axis_index("scol"), n)
        for q in range(3):
            plane = all_ref[q * dirs : (q + 1) * dirs, :]
            out_ref[q * depth : (q + 1) * depth, :] = pack_plane(plane, block, span)
        out_ref[3 * depth :, :] = jnp.zeros((8, rows), jnp.float32)


def first_kernel(*refs, ns, nz, span):
    rows_in = refs[: 2 * nz : 2]
    cols_in = refs[1 : 2 * nz : 2]
    mt_ref, vt_ref = refs[nz + ns : nz + ns + 2]
    outs = refs[nz + ns + 2 : nz + ns + 5]
    grow_ref, gcol_ref, trow_ref, tcol_ref, ct_ref = refs[nz + ns + 5 :]
    dirs = mt_ref.shape[0]
    i, j = lax.axis_index("srow"), lax.axis_index("scol")
    depth = dirs * span // mt_ref.shape[3]
    for pieces, g_ref, t_ref, me in ((rows_in, grow_ref, trow_ref, j), (cols_in, gcol_ref, tcol_ref, i)):
        blocks = [jnp.bitwise_xor(me, n) for n in range(len(pieces))]
        for q in range(4):
            plane = unpack_planes([p[q * depth : (q + 1) * depth, :] for p in pieces], blocks, span)
            dst = g_ref if q < 2 else t_ref
            at = (q % 2) * dirs
            dst[at : at + dirs, :] = plane
    residual(mt_ref, vt_ref, grow_ref, gcol_ref, *outs, ct_ref)


def sweep_kernel(*refs, ns, span, scale):
    pieces = refs[:2] + refs[3 : ns + 1]
    other_ref = refs[2]
    same_ref, growin_ref, gcolin_ref, trow_ref, tcol_ref = refs[ns + 1 : ns + 6]
    rho_ref, mt_ref, vt_ref = refs[ns + 6 : ns + 9]
    outs = refs[ns + 9 : ns + 12]
    grow_ref, gcol_ref, ct_ref = refs[ns + 12 :]
    dirs = mt_ref.shape[0]
    i = lax.axis_index("srow")
    depth = dirs * span // mt_ref.shape[3]
    power = pieces[0][3 * depth :, :]
    for p in pieces[1:]:
        power = power + p[3 * depth :, :]
    rho_eff = rho_ref[...] * (jnp.sum(power) * scale + EPS)
    re, im = slice(0, dirs), slice(dirs, 2 * dirs)
    half = dirs // 2
    a, cr, ci = [
        unfold(
            same_ref[q * half : (q + 1) * half, :],
            other_ref[q * half : (q + 1) * half, :],
            span,
            lax.axis_index("scol"),
        )
        for q in range(3)
    ]
    grow_ref[re, :], grow_ref[im, :] = solve(
        a, cr, ci, growin_ref[re, :], growin_ref[im, :], trow_ref[re, :], trow_ref[im, :], rho_eff
    )
    blocks = [jnp.bitwise_xor(i, n) for n in range(ns)]
    a, cr, ci = [
        unpack_planes([p[q * depth : (q + 1) * depth, :] for p in pieces], blocks, span)
        for q in range(3)
    ]
    gcol_ref[re, :], gcol_ref[im, :] = solve(
        a, cr, ci, gcolin_ref[re, :], gcolin_ref[im, :], tcol_ref[re, :], tcol_ref[im, :], rho_eff
    )
    residual(mt_ref, vt_ref, grow_ref, gcol_ref, *outs, ct_ref)


def combine_kernel(*refs, nz, span):
    parts = refs[:nz]
    pair_ref, own_ref, *copies = refs[nz:]
    half = pair_ref.shape[0] // 3
    depth = 2 * half * span // pair_ref.shape[1]
    total = parts[0][...]
    for p in parts[1:]:
        total = total + p[...]
    pair_ref[...] = total[: 3 * half]
    for q in range(3):
        piece = total[q * half : (q + 1) * half]
        own_ref[q * depth : (q + 1) * depth, :] = pack_folded(piece, lax.axis_index("scol"), span)
    own_ref[3 * depth :, :] = total[3 * half :]
    for ref in copies:
        ref[...] = own_ref[...]


def last_combine_kernel(*refs, nz, span):
    parts = refs[:nz]
    g_ref, t_ref, d_ref, power_ref, mail_ref = refs[nz:]
    dirs = g_ref.shape[0] // 2
    depth = dirs * span // g_ref.shape[1]
    j = lax.axis_index("scol")
    total = parts[0][...]
    for p in parts[1:]:
        total = total + p[...]
    mail_ref[: 3 * depth, :] = total[: 3 * depth]
    power_ref[...] = total[3 * depth :]
    for n, ref in enumerate((g_ref, t_ref)):
        for p in range(2):
            at = (3 + 2 * n + p) * depth
            plane = ref[p * dirs : (p + 1) * dirs, :]
            mail_ref[at : at + depth, :] = pack_plane(plane, j, span)
    mail_ref[7 * depth :, :] = d_ref[...]


def final_kernel(*refs, ns, scale, pair, span, scal):
    powers = refs[:ns]
    mails = refs[ns : ns + 1 + pair]
    rho_ref = refs[ns + 1 + pair]
    outs = refs[ns + 2 + pair :]
    depth, lanes = rho_ref.shape
    dirs = depth * lanes // span
    power = powers[0][...]
    for p in powers[1:]:
        power = power + p[...]
    rho_eff = rho_ref[...] * (jnp.sum(power) * scale + EPS)
    news = []
    for mail in mails:
        a, cr, ci, gr, gi, tr, ti = [mail[q * depth : (q + 1) * depth, :] for q in range(7)]
        news.append(solve(a, cr, ci, gr, gi, tr, ti, rho_eff))
    fields = list(news[0])
    if pair:
        duals = [[m[q * depth : (q + 1) * depth, :] for q in (7, 8)] for m in mails]
        first = lax.axis_index("chan") == 0
        coeffs, new_duals = [], []
        for p in range(2):
            own, other = [news[n][p] + duals[n][p] for n in range(2)]
            low, high = jnp.where(first, own, other), jnp.where(first, other, own)
            total = scal[0] * low + scal[1] * high
            coeffs.append(total / scal[2] / scal[2])
            brow = jnp.where(first, scal[0], scal[1])
            new_duals.append(duals[0][p] + news[0][p] - brow * coeffs[p])
        fields += coeffs + new_duals
    parts = lanes // span
    for at in range(0, len(fields), parts):
        group = fields[at : at + parts]
        plane = unpack_planes(group, list(range(len(group))), span)
        plane = jnp.concatenate([plane, jnp.zeros((lanes - dirs, lanes), jnp.float32)], axis=0)
        turned = plane.T
        for n in range(len(group)):
            out_ref = outs[(at + n) // 2]
            out_ref[(at + n) % 2] = turned[n * span : (n + 1) * span, :dirs]


SMEM = pl.BlockSpec(memory_space=pltpu.SMEM)
VMEM = pl.BlockSpec(memory_space=pltpu.VMEM)
HBM = pl.BlockSpec(memory_space=pltpu.HBM)


def f32(*shape):
    return jax.ShapeDtypeStruct(shape, jnp.float32)


def call(kernel, name, lead, args, outs, scratch=(), place=VMEM):
    if place is HBM:
        args = [pltpu.with_memory_space_constraint(x, pltpu.HBM) for x in args]
    return pl.pallas_call(
        kernel,
        in_specs=[SMEM] * len(lead) + [place] * len(args),
        out_specs=[VMEM] * len(outs),
        out_shape=outs,
        scratch_shapes=scratch,
        compiler_params=pltpu.CompilerParams(vmem_limit_bytes=VMEM_LIMIT),
        name=name,
    )(*lead, *args)


def swap(x, axis, n):
    size = lax.axis_size(axis)
    return lax.ppermute(x, axis, [(m, m ^ n) for m in range(size)])


def shards(vis, model, flags, gains, consensus, dual, rho, cluster):
    groups = lax.axis_size("chan")
    ns = lax.axis_size("srow")
    nz = lax.axis_size("scol")
    order = consensus.shape[1]
    dirs = gains.shape[1]
    span = gains.shape[3]
    rows, cols = vis.shape[2:]
    depth = dirs * span // rows
    f = lax.axis_index("chan")
    pair = groups == 2 and order == 1

    table = basis_table(groups, order)
    brow = lax.dynamic_index_in_dim(table, f, 0, keepdims=False)
    own_in = [
        gains[0].transpose(1, 2, 0),
        consensus.transpose(1, 2, 3, 0),
        dual[0].transpose(1, 2, 0),
    ]
    start, dual_packed = call(
        functools.partial(pack_kernel, alone=order == 1),
        "pack",
        [] if order == 1 else [brow],
        own_in,
        [f32(4 * depth, rows), f32(2 * depth, rows)],
        [pltpu.VMEM(x.shape, jnp.float32) for x in own_in] + [pltpu.SemaphoreType.DMA((3,))],
        HBM,
    )
    row_parts, col_parts = [start], [start]
    for n in range(1, max(ns, nz)):
        col_parts += [swap(start, "srow", n)] if n < ns else []
        row_parts += [swap(start, "scol", n)] if n < nz else []
    field_in = [rho, cluster, flags[0], model[0], vis[0]]
    mt, vt, rho_rows, rho_packed = call(
        prepare_kernel,
        "prepare",
        [],
        field_in,
        [
            jax.ShapeDtypeStruct((dirs, 2, cols, rows), jnp.bfloat16),
            f32(2, cols, rows),
            f32(dirs, rows),
            f32(depth, rows),
        ],
        [(pltpu.SMEM if n < 3 else pltpu.VMEM)(x.shape, x.dtype) for n, x in enumerate(field_in)]
        + [pltpu.SemaphoreType.DMA((12,))],
        HBM,
    )

    scratch = [pltpu.VMEM((cols, 2 * dirs), jnp.float32)]
    scale = 1.0 / (groups * STATIONS * STATIONS)
    plane = f32(2 * dirs, rows)
    fields = [f32(dirs, 2, cols, rows), f32(2, cols, rows), f32(8, rows)]
    z, r, power, grow, gcol, trow, tcol = call(
        functools.partial(first_kernel, ns=ns, nz=nz, span=span),
        "first",
        [],
        [part for parts in zip(row_parts, col_parts) for part in parts] + [mt, vt],
        fields + [plane, plane, plane, plane],
        scratch,
    )
    for step in range(ITERS):
        last = step == ITERS - 1
        if groups == 2:
            power = power + swap(power, ("chan", "srow"), ns + 1)
        else:
            power = lax.psum(power, "chan")
        if last:
            break
        half = 3 * dirs // 2
        same, other = call(
            functools.partial(terms_kernel, span=span),
            "terms",
            [],
            [z, r],
            [f32(half + 8, rows)] * 2,
            [pltpu.VMEM((3 * dirs, rows), jnp.float32)],
        )
        same = lax.dynamic_update_slice(same, power, (half, 0))
        other = lax.dynamic_update_slice(other, power, (half, 0))
        pair_sums, own, *copies = call(
            functools.partial(combine_kernel, nz=nz, span=span),
            "combine",
            [],
            [same] + [swap(same if n % 2 == 0 else other, "scol", n) for n in range(1, nz)],
            [f32(half, rows)] + [f32(3 * depth + 8, rows)] * (ns - 1),
        )
        other_sums = swap(pair_sums, "scol", 1)
        pieces = [own, swap(own, "srow", 1)]
        pieces += [swap(copy, "srow", n + 2) for n, copy in enumerate(copies)]
        z, r, power, grow, gcol = call(
            functools.partial(sweep_kernel, ns=ns, span=span, scale=scale),
            "sweep",
            [],
            pieces[:2] + [other_sums] + pieces[2:] + [pair_sums, grow, gcol, trow, tcol, rho_rows, mt, vt],
            fields + [plane, plane],
            scratch,
        )

    parts = call(
        functools.partial(last_terms_kernel, span=span),
        "terms",
        [],
        [z, r],
        [f32(3 * depth + 8, rows)] * nz,
        [pltpu.VMEM((3 * dirs, rows), jnp.float32)],
    )
    parts = [lax.dynamic_update_slice(part, power, (3 * depth, 0)) for part in parts]
    power, mail = call(
        functools.partial(last_combine_kernel, nz=nz, span=span),
        "combine",
        [],
        [parts[0]] + [swap(parts[n], "scol", n) for n in range(1, nz)] + [grow, trow, dual_packed],
        [f32(8, rows), f32(9 * depth, rows)],
    )
    powers = [power] + [swap(power, "srow", n) for n in range(1, ns)]
    mails = [mail] + ([swap(mail, "chan", 1)] if pair else [])
    outs = call(
        functools.partial(
            final_kernel, ns=ns, scale=scale, pair=int(pair), span=span, scal=pair_scalars(pair)
        ),
        "final",
        [],
        powers + mails + [rho_packed],
        [f32(2, span, dirs)] * (3 if pair else 1),
    )
    outs = [x.transpose(2, 0, 1) for x in outs]
    if pair:
        g, coeffs, dual_new = outs
        return (g[None], coeffs[:, None], dual_new[None])
    g = outs[0]
    dual_own = dual[0]
    local = brow[None, :, None, None] * (g + dual_own)[:, None, :, :]
    coeffs = gram_solve(table, lax.psum(local, "chan"))
    dual_new = (
        dual_own + g - jnp.einsum("b,kbcp->kcp", brow, coeffs, precision=lax.Precision.HIGHEST)
    )
    return (g[None], coeffs, dual_new[None])


def solution(mesh):
    placed = (
        P("chan", None, "srow", "scol"),
        P("chan", None, None, "srow", "scol"),
        P("chan", "srow", "scol"),
        P("chan", None, None, ("srow", "scol")),
        P(None, None, None, ("srow", "scol")),
        P("chan", None, None, ("srow", "scol")),
        P(),
        P(),
    )
    return jax.shard_map(
        shards,
        mesh=mesh,
        in_specs=placed,
        out_specs=(
            P("chan", None, None, ("srow", "scol")),
            P(None, None, None, ("srow", "scol")),
            P("chan", None, None, ("srow", "scol")),
        ),
        check_vma=False,
    )
```
